32 devices in a mesh: fsdp: 2 (over x), ctx: 4 (over y, core), tp: 4 (over z).
Axes of the slice: x: 2, y: 2, z: 4, core: 2. Of those that a mesh axis runs over, the one named last changes fastest.
Arguments:
- inputs: bfloat16 [4, 1024, 2048], P('fsdp', 'ctx'), may hold values from -6 to 6
- prefix: int32 [4], P('fsdp'), may hold values from 102 to 512, as said below
- expert_ids: int32 [4, 1024, 8], P('fsdp', 'ctx'), may hold values from 0 to 15, all different within a row
- norm_gains: bfloat16 [4, 2048], P(None, ('fsdp', 'ctx')), may hold values from 0.5 to 1.5
- qkv_weight: bfloat16 [3, 2048, 2048], P(None, ('fsdp', 'ctx'), 'tp'), may hold values from -0.125 to 0.125
- out_weight: bfloat16 [2048, 2048], P(('fsdp', 'ctx'), 'tp'), may hold values from -1 to 1
- router_weight: bfloat16 [2048, 16], P(('fsdp', 'ctx')), may hold values from -0.0625 to 0.0625
- gate_up_weight: bfloat16 [16, 2, 2048, 1024], P(None, None, ('fsdp', 'ctx'), 'tp'), may hold values from -0.125 to 0.125
- down_weight: bfloat16 [16, 2048, 1024], P(None, ('fsdp', 'ctx'), 'tp'), may hold values from -1.5 to 1.5
- cotangent: bfloat16 [4, 1024, 2048], P('fsdp', 'ctx'), may hold values from -6 to 6
Outputs:
- outputs: bfloat16 [4, 1024, 2048], P('fsdp', 'ctx')
- grad_inputs: bfloat16 [4, 1024, 2048], P('fsdp', 'ctx')
- grad_norm_gains: float32 [4, 2048], P(None, ('fsdp', 'ctx'))
- grad_qkv_weight: float32 [3, 2048, 2048], P(None, ('fsdp', 'ctx'), 'tp')
- grad_out_weight: float32 [2048, 2048], P(('fsdp', 'ctx'), 'tp')
- grad_router_weight: float32 [2048, 16], P(('fsdp', 'ctx'))
- grad_gate_up_weight: float32 [16, 2, 2048, 1024], P(None, None, ('fsdp', 'ctx'), 'tp')
- grad_down_weight: float32 [16, 2048, 1024], P(None, ('fsdp', 'ctx'), 'tp')
The draws below stay inside these ranges and needn't reach their ends.
Inputs may be any that keep to these rules, and one draw needn't show every extreme that they name: `expert_ids`: each token names 8 different experts. Some sequence has the shortest and some the longest allowed prefix.
All inputs are finite; a program needn't handle non-finite values.
Results may differ from the reference program's by a relative error of at most 0.017.
Values may be sent and summed in bfloat16 or wider, within the bound.
No kernel may reach another device: no remote copies, remote signals or barrier semaphores. Data moves between devices by JAX's collectives and lax.ppermute only.
A program may use at most 384 MiB of HBM per device.

```python
import jax
import jax.numpy as jnp
from jax import lax

D = 2048
HEADS = 16
HEAD_DIM = 128
FF = 1024
EXPERTS = 16
TOPK = 8
LEN = 1024
SEQS = 4


def draw_prefix(key, part):
    shortest = LEN // 10
    prefix_range = LEN // 2 - shortest
    others = jax.random.randint(jax.random.fold_in(key, 1), (SEQS - 2,), 0, prefix_range + 1).astype(jnp.int32)
    values = jnp.concatenate([jnp.array([0, prefix_range], jnp.int32), others])
    return (shortest + jax.random.permutation(jax.random.fold_in(key, 2), values)).astype(jnp.int32)


def levels(stream_key, extent, pieces, least, largest):
    def one(position, shards_of):
        draws = jax.random.uniform(jax.random.fold_in(jax.random.fold_in(stream_key, 6), position), (shards_of,), jnp.float32, least / len(pieces), largest / len(pieces))
        return jnp.repeat(jnp.exp(draws), extent[position] // shards_of).reshape((-1,) + (1,) * (len(extent) - position - 1))

    factor_of = one(*pieces[0])
    for cut in pieces[1:]:
        factor_of = factor_of * one(*cut)
    return factor_of


def picks_of(key, rows, amount, top, lift):
    sequence = jax.random.permutation(jax.random.fold_in(key, 1), amount)
    pull = sequence
    for power in range(3):
        pull = pull * pull // amount
    pull = pull * lift // amount
    tickets = jax.random.randint(jax.random.fold_in(key, 2), (rows, amount), 0, 4096) + pull
    fixed_rows = jax.random.permutation(jax.random.fold_in(key, 3), rows)[jnp.arange(amount) % rows]
    tickets = jnp.where(jnp.arange(rows)[:, None] == fixed_rows[None, :], 1 << 14, tickets)
    merit = tickets * amount + jnp.arange(amount)
    return lax.top_k(merit.astype(jnp.int32), top)[1].astype(jnp.int32)


def normal_values(stream_key, shape, spread, bound, split=(), kind=jnp.bfloat16):
    values = jax.random.normal(stream_key, shape, jnp.float32) * spread
    if len(split) > 0:
        values = levels(stream_key, shape, split, -0.22, 0.18) * values
    return jnp.clip(values, min=-bound, max=bound).astype(kind)


def setup_inputs(seed: int = 0) -> dict:
    splits = jax.random.split(jax.random.key(seed), 11)
    inputs = normal_values(splits[0], (SEQS, LEN, D), 1.0, 6.0, ((0, 2), (1, 4)))
    prefix = draw_prefix(jax.random.fold_in(splits[10], 71), 0)
    expert_ids = picks_of(splits[2], SEQS * LEN, EXPERTS, TOPK, 4096).reshape((SEQS, LEN, TOPK))
    norm_gains = jnp.clip(1.0 + 0.1 * jax.random.normal(splits[3], (4, D), jnp.float32), 0.5, 1.5).astype(jnp.bfloat16)
    qkv_weight = normal_values(splits[4], (3, D, D), D ** -0.5, 0.125, ((1, 8), (2, 4)))
    out_weight = normal_values(splits[5], (D, D), (D // 64) ** -0.5, 1.0, ((0, 8), (1, 4)))
    router_weight = normal_values(splits[6], (D, EXPERTS), (4 * D) ** -0.5, 0.0625, ((0, 8),))
    gate_up_weight = normal_values(splits[7], (EXPERTS, 2, D, FF), D ** -0.5, 0.125, ((2, 8), (3, 4)))
    down_weight = normal_values(splits[8], (EXPERTS, D, FF), (max(FF // 64, 1)) ** -0.5, 1.5, ((1, 8), (2, 4)))
    cotangent = normal_values(splits[9], (SEQS, LEN, D), 1.0, 6.0, ((0, 2), (1, 4)))
    return {"inputs": inputs, "prefix": prefix, "expert_ids": expert_ids, "norm_gains": norm_gains, "qkv_weight": qkv_weight, "out_weight": out_weight, "router_weight": router_weight, "gate_up_weight": gate_up_weight, "down_weight": down_weight, "cotangent": cotangent}


EPSILON = 1e-05
THETA = 10000.0

@jax.custom_vjp
def low(v):
    return lax.optimization_barrier(v.astype(jnp.bfloat16)).astype(jnp.float32)

@jax.custom_vjp
def low_back(v):
    return v

def low_keep(v):
    return (low(v), None)

def low_pass(kept, grad):
    return (grad,)

def back_keep(v):
    return (v, None)

def back_low(kept, grad):
    return (low(grad),)
low.defvjp(low_keep, low_pass)
low_back.defvjp(back_keep, back_low)

def precise(form, left, right):
    return jnp.einsum(form, left, right, precision=lax.Precision.HIGHEST)

def norm(values, gain):
    return values * lax.rsqrt(lax.optimization_barrier(jnp.mean(values * values, -1, keepdims=True)) + EPSILON) * gain

def rotary_tables(positions, head_width):
    halves = jnp.arange(0, head_width, 2).astype(jnp.float32) / head_width
    inverse = 1.0 / THETA ** halves
    angles = positions.astype(jnp.float32)[:, None] * inverse[None, :]
    return (jnp.cos(angles), jnp.sin(angles))

def rotate(values, cosine, sine):
    half = values.shape[-1] // 2
    first = values[..., :half]
    second = values[..., half:]
    cosine = cosine[:, None, :]
    sine = sine[:, None, :]
    return jnp.concatenate([first * cosine - second * sine, second * cosine + first * sine], -1)

def attend(queries, keys, values, limit):
    places = jnp.arange(LEN, dtype=jnp.int32)
    visible = (places[None, :] <= places[:, None]) | (places[None, :] < limit)
    scores = low_back(precise('qhd,khd->hqk', queries, keys) * HEAD_DIM ** (-0.5))
    masked = jnp.where(visible[None], scores, -1e+30)
    probs = jax.nn.softmax(masked, -1)
    return precise('hqk,khd->qhd', low(probs), values)

def forward(residual_in, limits, choices, gains, qkv, out_proj, router, gate_up, down):
    group = residual_in.shape[0]
    normed_one = low(norm(residual_in, gains[0]))
    query_raw = low_back(precise('gld,de->gle', normed_one, qkv[0]))
    key_raw = low_back(precise('gld,de->gle', normed_one, qkv[1]))
    values = low_back(low(precise('gld,de->gle', normed_one, qkv[2])))
    cosine, sine = rotary_tables(jnp.arange(LEN, dtype=jnp.int32), HEAD_DIM)
    head_shape = (group, LEN, HEADS, HEAD_DIM)
    queries = low(rotate(norm(query_raw, gains[2]).reshape(head_shape), cosine, sine))
    keys = low(rotate(norm(key_raw, gains[3]).reshape(head_shape), cosine, sine))

    def attend_one(entries):
        return attend(entries[0], entries[1], entries[2], entries[3])
    mixed = lax.map(jax.checkpoint(attend_one), (queries, keys, values.reshape(head_shape), limits))
    heads_out = low_back(low(mixed.reshape(group, LEN, D)))
    mid = residual_in + low_back(precise('gle,de->gld', heads_out, out_proj))
    normed_two = low(norm(mid, gains[1]))
    router_probs = jax.nn.softmax(low_back(precise('gld,de->gle', normed_two, router)), -1)
    chosen = lax.optimization_barrier(jnp.sum((choices[..., None] == jnp.arange(EXPERTS, dtype=jnp.int32)).astype(jnp.float32), -2))
    gates = router_probs * chosen

    def expert(total, entries):
        pair_weights, down_one, gate_one = entries
        gate_act = low_back(precise('gld,df->glf', normed_two, pair_weights[0]))
        up_act = low_back(precise('gld,df->glf', normed_two, pair_weights[1]))
        hidden = low(gate_one[..., None] * jax.nn.silu(gate_act) * up_act)
        return (total + precise('glf,df->gld', hidden, down_one), None)
    total, unused = lax.scan(jax.checkpoint(expert), jnp.zeros_like(mid), (gate_up, down, jnp.moveaxis(gates, -1, 0)))
    return mid + low_back(total)

def reference(inputs, prefix, expert_ids, norm_gains, qkv_weight, out_weight, router_weight, gate_up_weight, down_weight, cotangent):
    weights = (norm_gains.astype(jnp.float32), qkv_weight.astype(jnp.float32), out_weight.astype(jnp.float32), router_weight.astype(jnp.float32), gate_up_weight.astype(jnp.float32), down_weight.astype(jnp.float32))
    per_group = max([count_try for count_try in range(1, SEQS + 1) if SEQS % count_try == 0 and count_try * LEN <= max(4096, LEN)])
    groups = SEQS // per_group
    sliced = (inputs.astype(jnp.float32).reshape(groups, per_group, LEN, D), prefix.reshape(groups, per_group), expert_ids.reshape(groups, per_group, LEN, TOPK), cotangent.astype(jnp.float32).reshape(groups, per_group, LEN, D))

    def step(totals, entries):
        residual_in, limits, choices, grad_in = entries

        def local_forward(values_in, gains, qkv, out_proj, router, gate_up, down):
            return forward(values_in, limits, choices, gains, qkv, out_proj, router, gate_up, down)
        result, pullback = jax.vjp(local_forward, residual_in, *weights)
        grads = pullback(grad_in)
        totals = tuple((running + extra for running, extra in zip(totals, grads[1:])))
        return (totals, (result, grads[0]))
    zeros = tuple((jnp.zeros_like(weight) for weight in weights))
    totals, (results, grad_rows) = lax.scan(step, zeros, sliced)
    return (results.reshape(SEQS, LEN, D).astype(jnp.bfloat16), grad_rows.reshape(SEQS, LEN, D).astype(jnp.bfloat16), totals[0], totals[1], totals[2], totals[3], totals[4], totals[5])
```

```python
import functools

import jax
import jax.numpy as jnp
from jax import lax
from jax.experimental import pallas as pl
from jax.experimental.pallas import tpu as pltpu
from jax.sharding import Mesh, PartitionSpec as P

HEAD_DIM = 128
EPSILON = 1e-05
THETA = 10000.0
TILE = 256
F32 = jnp.float32
BF16 = jnp.bfloat16
FR = ("fsdp", "row")
PLANE = ("fsdp", "row", "core")
EVERY = ("fsdp", "row", "core", "tp")


def nn(a, b):
    return lax.dot_general(a, b, (((1,), (0,)), ((), ())), preferred_element_type=F32)


def nt(a, b):
    return lax.dot_general(a, b, (((1,), (1,)), ((), ())), preferred_element_type=F32)


def tn(a, b):
    return lax.dot_general(a, b, (((0,), (0,)), ((), ())), preferred_element_type=F32)


def call(kernel, name, grid, in_specs, out_specs, out_shape, flops, moved, scratch=(), prefetch=0, limit=56, aliases=None):
    return pl.pallas_call(
        kernel,
        name=name,
        out_shape=out_shape,
        grid_spec=pltpu.PrefetchScalarGridSpec(
            num_scalar_prefetch=prefetch,
            grid=grid,
            in_specs=in_specs,
            out_specs=out_specs,
            scratch_shapes=list(scratch),
        ),
        input_output_aliases=aliases or {},
        compiler_params=pltpu.CompilerParams(
            dimension_semantics=("arbitrary",) * len(grid), vmem_limit_bytes=limit << 20
        ),
        cost_estimate=pl.CostEstimate(flops=int(flops), bytes_accessed=int(moved), transcendentals=0),
    )


def fixed(shape):
    return pl.BlockSpec(shape, lambda *a: (0,) * len(shape), pipeline_mode=pl.Buffered(1))


def sds(shape, dtype):
    return jax.ShapeDtypeStruct(shape, dtype)


def qkv_kernel(x_ref, g_ref, w_ref, n_ref, raw_ref, v_ref, sq_ref):
    c = pl.program_id(0)

    @pl.when(c == 0)
    def _():
        x = x_ref[...].astype(F32)
        r = lax.rsqrt(jnp.mean(x * x, -1, keepdims=True) + EPSILON)
        n_ref[...] = (x * r * g_ref[...]).astype(BF16)

    w = w_ref[...]
    y = nn(n_ref[...], w.reshape(w.shape[0] * w.shape[2], w.shape[3]))

    @pl.when(c < 2)
    def _():
        raw_ref[0] = y
        sq_ref[0] = jnp.broadcast_to(jnp.sum(y * y, -1, keepdims=True), sq_ref.shape[1:])

    @pl.when(c == 2)
    def _():
        v_ref[...] = y.astype(BF16)


def qkv_project(x, gain, w):
    t, d = x.shape
    p, _, ds, n = w.shape
    return call(
        qkv_kernel,
        "qkv",
        (3,),
        [
            fixed((t, d)),
            fixed((1, d)),
            pl.BlockSpec((p, 1, ds, n), lambda c: (0, c, 0, 0)),
        ],
        [
            pl.BlockSpec((t, d), lambda c: (0, 0)),
            pl.BlockSpec((1, t, n), lambda c: (jnp.minimum(c, 1), 0, 0)),
            pl.BlockSpec((t, n), lambda c: (0, 0)),
            pl.BlockSpec((1, t, 128), lambda c: (jnp.minimum(c, 1), 0, 0)),
        ],
        [sds((t, d), BF16), sds((2, t, n), F32), sds((t, n), BF16), sds((2, t, 128), F32)],
        6 * t * d * n,
        2 * (3 * d * n + 2 * t * d) + 10 * t * n,
    )(x, gain, w)


def turn(v, cosine, sine):
    half = v.shape[-1] // 2
    return v * cosine + pltpu.roll(v, half, 1) * sine


def prep_kernel(raw_ref, s_ref, g_ref, cos_ref, sin_ref, q_ref, k_ref):
    reps = raw_ref.shape[1] // cos_ref.shape[0]
    cosine = jnp.concatenate([cos_ref[...]] * reps, 0)
    sine = jnp.concatenate([sin_ref[...]] * reps, 0)
    q = raw_ref[0] * s_ref[0] * g_ref[0]
    k = raw_ref[1] * s_ref[1] * g_ref[1]
    q_ref[...] = turn(q, cosine, sine).astype(BF16)
    k_ref[...] = turn(k, cosine, sine).astype(BF16)


def prepare(raw, scales, gains, cosine, sine):
    _, t, n = raw.shape
    h = HEAD_DIM
    length = cosine.shape[0]
    return call(
        prep_kernel,
        "prep",
        (n // h,),
        [
            pl.BlockSpec((2, t, h), lambda i: (0, 0, i)),
            fixed((2, t, 1)),
            pl.BlockSpec((2, 1, h), lambda i: (0, 0, i)),
            fixed((length, h)),
            fixed((length, h)),
        ],
        [pl.BlockSpec((t, h), lambda i: (0, i))] * 2,
        [sds((t, n), BF16)] * 2,
        20 * t * n,
        12 * t * n,
    )(raw, scales, gains, cosine, sine)


def masked_probs(s, scal_ref, q, ks):
    length = q.shape[0]
    prefix = scal_ref[5 + s]
    rows = lax.broadcasted_iota(jnp.int32, (length, length), 0) + scal_ref[4]
    columns = lax.broadcasted_iota(jnp.int32, (length, length), 1)
    pieces = []
    for b, k in enumerate(ks):
        place = columns + scal_ref[b]
        visible = (place <= rows) | (place < prefix)
        pieces.append(jnp.where(visible, nt(q, k) * HEAD_DIM ** (-0.5), -1e30))
    scores = jnp.concatenate(pieces, 1)
    expo = jnp.exp(scores - jnp.max(scores, -1, keepdims=True))
    return expo / jnp.sum(expo, -1, keepdims=True)


def attend_kernel(scal_ref, q_ref, *refs):
    o_ref = refs[8]
    probs = masked_probs(pl.program_id(0), scal_ref, q_ref[...], [r[...] for r in refs[:4]])
    v = jnp.concatenate([r[...] for r in refs[4:8]], 0)
    o_ref[...] = nn(probs.astype(BF16), v).astype(BF16)


def attend(scal, q, blocks, length):
    t, n = q.shape
    h = HEAD_DIM
    one = pl.BlockSpec((length, h), lambda s, i, *_: (s, i))
    return call(
        attend_kernel,
        "attend",
        (t // length, n // h),
        [one] * 9,
        one,
        sds((t, n), BF16),
        16 * t * n * length,
        24 * t * n,
        prefetch=1,
    )(scal, q, *blocks)


def attend_back_kernel(scal_ref, q_ref, *refs):
    g_ref, dq_ref, outs = refs[8], refs[9], refs[10:]
    length = q_ref.shape[0]
    q = q_ref[...]
    grad = g_ref[...]
    probs = masked_probs(pl.program_id(0), scal_ref, q, [r[...] for r in refs[:4]])
    k = jnp.concatenate([r[...] for r in refs[:4]], 0)
    v = jnp.concatenate([r[...] for r in refs[4:8]], 0)
    d_probs = nt(grad, v)
    inner = jnp.sum(probs * d_probs, -1, keepdims=True)
    d_scores = (probs * (d_probs - inner)).astype(BF16)
    scale = HEAD_DIM ** (-0.5)
    dq_ref[...] = nn(d_scores, k) * scale
    dk = (tn(d_scores, q) * scale).astype(BF16)
    dv = tn(probs.astype(BF16), grad).astype(BF16)
    for b, o in enumerate(outs):
        o[0] = dk[b * length : (b + 1) * length]
        o[1] = dv[b * length : (b + 1) * length]


def attend_back(scal, q, blocks, grad, length):
    t, n = q.shape
    h = HEAD_DIM
    one = pl.BlockSpec((length, h), lambda s, i, *_: (s, i))
    two = pl.BlockSpec((2, length, h), lambda s, i, *_: (0, s, i))
    return call(
        attend_back_kernel,
        "attend_back",
        (t // length, n // h),
        [one] * 10,
        [one] + [two] * 4,
        [sds((t, n), F32)] + [sds((2, t, n), BF16)] * 4,
        40 * t * n * length,
        48 * t * n,
        prefetch=1,
    )(scal, q, *blocks, grad)


def out_kernel(place_ref, h_ref, w_ref, *outs):
    w = w_ref[...]
    w = w.reshape(-1, w.shape[-1])
    rows = outs[0].shape[0]
    for r, o in enumerate(outs):
        start = pl.multiple_of(place_ref[r], rows)
        o[...] = nt(h_ref[pl.ds(start, rows), :], w).astype(BF16)


def project_out(places, heads, w, pieces):
    t, n = heads.shape
    p, _, ds, _ = w.shape
    pb = max(1, TILE // ds)
    return call(
        out_kernel,
        "outproj",
        (p // pb,),
        [fixed((t, n)), pl.BlockSpec((pb, 1, ds, n), lambda g, *_: (g, 3, 0, 0))],
        [pl.BlockSpec((t // pieces, pb * ds), lambda g, *_: (0, g))] * pieces,
        [sds((t // pieces, p * ds), BF16)] * pieces,
        2 * t * n * p * ds,
        2 * (t * n + n * p * ds + t * p * ds),
        prefetch=1,
    )(places, heads, w)


def d_heads_kernel(place_ref, g_ref, w_ref, o_ref, *, pieces):
    w = w_ref[...]
    y = nn(g_ref[...], w.reshape(w.shape[0] * w.shape[2], w.shape[3])).astype(BF16)
    rows = y.shape[0] // pieces
    for r in range(pieces):
        o_ref[pl.ds(pl.multiple_of(place_ref[r], rows), rows), :] = y[r * rows : (r + 1) * rows]


def heads_grad(places, grad, w, pieces):
    t, d = grad.shape
    p, _, ds, n = w.shape
    return call(
        functools.partial(d_heads_kernel, pieces=pieces),
        "dheads",
        (1,),
        [fixed((t, d)), pl.BlockSpec((p, 1, ds, n), lambda g, *_: (0, 3, 0, 0))],
        fixed((t, n)),
        sds((t, n), BF16),
        2 * t * n * d,
        2 * (t * n + n * d + t * d),
        prefetch=1,
    )(places, grad, w)


def grad_out_kernel(place_ref, g_ref, h_ref, o_ref, *, pieces):
    rows = g_ref.shape[0] // pieces
    heads = jnp.concatenate(
        [h_ref[pl.ds(pl.multiple_of(place_ref[r], rows), rows), :] for r in range(pieces)], 0
    )
    o_ref[...] = tn(g_ref[...], heads).astype(BF16).reshape(o_ref.shape)


def out_weight_grad(places, grad, heads, p, pieces):
    t, d = grad.shape
    n = heads.shape[1]
    ds = d // p
    pb = max(1, TILE // ds)
    return call(
        functools.partial(grad_out_kernel, pieces=pieces),
        "gradout",
        (p // pb,),
        [pl.BlockSpec((t, pb * ds), lambda g, *_: (0, g)), fixed((t, n))],
        pl.BlockSpec((pb, 1, ds, n), lambda g, *_: (g, 3, 0, 0)),
        sds((p, 4, ds, n), BF16),
        2 * t * n * d,
        2 * (t * n + n * d + t * d),
        prefetch=1,
    )(places, grad, heads)


def router_kernel(x_ref, w_ref, ids_ref, o_ref, *, experts):
    logits = nt(x_ref[...], w_ref[...])
    lane = lax.broadcasted_iota(jnp.int32, logits.shape, 1)
    logits = jnp.where(lane < experts, logits, -1e30)
    expo = jnp.exp(logits - jnp.max(logits, -1, keepdims=True))
    probs = expo / jnp.sum(expo, -1, keepdims=True)
    chosen = jnp.zeros_like(probs)
    for j in range(ids_ref.shape[1]):
        chosen += (ids_ref[:, j : j + 1] == lane).astype(F32)
    o_ref[...] = probs * chosen


def route(x, router, ids, experts):
    t, d = x.shape
    return call(
        functools.partial(router_kernel, experts=experts),
        "router",
        (1,),
        [fixed((t, d)), fixed(router.shape), fixed(ids.shape)],
        fixed((t, 128)),
        sds((t, 128), F32),
        2 * t * d * 128,
        2 * t * d,
    )(x, router, ids)


def expert_kernel(scal_ref, x0_ref, x1_ref, c0_ref, c1_ref, g0_ref, g1_ref, w_ref, hid_ref, dgu_ref, dg_ref):
    e = pl.program_id(0)
    t = x0_ref.shape[0]

    @pl.when(e == 0)
    def _():
        dg_ref[...] = jnp.zeros_like(dg_ref)

    width = w_ref.shape[0] * w_ref.shape[3]
    f = w_ref.shape[4]
    me = scal_ref[0] + e
    out_lane = scal_ref[1] + e
    lane = lax.broadcasted_iota(jnp.int32, (TILE, 128), 1)
    for half, (x_ref, c_ref, g_ref) in enumerate(((x0_ref, c0_ref, g0_ref), (x1_ref, c1_ref, g1_ref))):
        for tile in range(t // TILE):
            rows = pl.ds(tile * TILE, TILE)
            to = pl.ds(half * t + tile * TILE, TILE)
            x = x_ref[rows, :]
            a = nn(x, w_ref[:, 0, 0].reshape(width, f))
            b = nn(x, w_ref[:, 0, 1].reshape(width, f))
            dh = nn(c_ref[rows, :], w_ref[:, 0, 2].reshape(width, f))
            gate = jnp.sum(jnp.where(lane == me, g_ref[rows, :], 0.0), -1, keepdims=True)
            sigma = jax.nn.sigmoid(a)
            swish = a * sigma
            act = swish * b
            hid_ref[to, :] = (gate * act).astype(BF16)
            d_gate = jnp.sum(dh * act, -1, keepdims=True)
            dg_ref[to, :] += jnp.where(lane == out_lane, d_gate, 0.0)
            inner = dh * gate
            dgu_ref[to, :f] = (inner * b * sigma * (1.0 + a * (1.0 - sigma))).astype(BF16)
            dgu_ref[to, f:] = (inner * swish).astype(BF16)


def expert_up(scal, x0, x1, c0, c1, g0, g1, w):
    t, d = x0.shape
    p, e, _, ds, f = w.shape
    return call(
        expert_kernel,
        "expert_up",
        (e,),
        [fixed((t, d))] * 4
        + [fixed((t, 128))] * 2
        + [pl.BlockSpec((p, 1, 3, ds, f), lambda i, *_: (0, i, 0, 0, 0))],
        [
            pl.BlockSpec((2 * t, f), lambda i, *_: (0, i)),
            pl.BlockSpec((2 * t, 2 * f), lambda i, *_: (0, i)),
            pl.BlockSpec((2 * t, 128), lambda i, *_: (0, 0)),
        ],
        [sds((2 * t, e * f), BF16), sds((2 * t, e * 2 * f), BF16), sds((2 * t, 128), F32)],
        12 * t * d * f * e,
        2 * (3 * d * f * e + 4 * t * d + 6 * t * f * e),
        prefetch=1,
    )(scal, x0, x1, c0, c1, g0, g1, w)


def expert_grad_kernel(x0_ref, x1_ref, c0_ref, c1_ref, hid_ref, dgu_ref, o_ref):
    pb, e, _, ds, f = o_ref.shape
    t = x0_ref.shape[0]
    for i in range(e):
        both = tn(x0_ref[...], dgu_ref[:t, i * 2 * f : (i + 1) * 2 * f]) + tn(
            x1_ref[...], dgu_ref[t:, i * 2 * f : (i + 1) * 2 * f]
        )
        o_ref[:, i, 0] = both[:, :f].astype(BF16).reshape(pb, ds, f)
        o_ref[:, i, 1] = both[:, f:].astype(BF16).reshape(pb, ds, f)
        down = tn(c0_ref[...], hid_ref[:t, i * f : (i + 1) * f]) + tn(
            c1_ref[...], hid_ref[t:, i * f : (i + 1) * f]
        )
        o_ref[:, i, 2] = down.astype(BF16).reshape(pb, ds, f)


def expert_grads(x0, x1, c0, c1, hid, dgu, p, e):
    t, d = x0.shape
    ds = d // p
    f = hid.shape[1] // e
    pb = max(1, TILE // ds)
    column = pl.BlockSpec((t, pb * ds), lambda g: (0, g))
    return call(
        expert_grad_kernel,
        "expert_grad",
        (p // pb,),
        [column] * 4 + [fixed(hid.shape), fixed(dgu.shape)],
        pl.BlockSpec((pb, e, 3, ds, f), lambda g: (g, 0, 0, 0, 0)),
        sds((p, e, 3, ds, f), BF16),
        12 * t * d * f * e,
        2 * (3 * d * f * e + 4 * t * d + 6 * t * f * e),
    )(x0, x1, c0, c1, hid, dgu)


def joined(w_ref, planes):
    pb, e, _, ds, f = w_ref.shape
    return jnp.concatenate([w_ref[:, i, c].reshape(pb * ds, f) for i in range(e) for c in range(planes)], 1)


def down_kernel(*refs, planes, parts):
    acts, ws, outs = refs[:parts], refs[parts : 2 * parts], refs[2 * parts :]
    t = outs[0].shape[0]
    for half, o in enumerate(outs):
        total = None
        for a, w in zip(acts, ws):
            piece = nt(a[half * t : (half + 1) * t, :], joined(w, planes))
            total = piece if total is None else total + piece
        o[...] = total.astype(BF16)


def expert_down(acts, ws, plane, planes, name):
    t2, k = acts[0].shape
    p, e, _, ds, f = ws[0].shape
    t = t2 // 2
    pb = max(1, TILE // ds)
    parts = len(acts)
    out = pl.BlockSpec((t, pb * ds), lambda g: (0, g))
    return call(
        functools.partial(down_kernel, planes=planes, parts=parts),
        name,
        (p // pb,),
        [fixed(a.shape) for a in acts]
        + [pl.BlockSpec((pb, e, planes, ds, f), lambda g: (g, 0, plane, 0, 0))] * parts,
        [out, out],
        [sds((t, p * ds), BF16)] * 2,
        2 * t2 * k * parts * p * ds,
        2 * parts * (t2 * k + k * p * ds) + 2 * t2 * p * ds,
    )(*acts, *ws)


def unturn_kernel(dq_ref, dk_ref, raw_ref, s_ref, g_ref, cos_ref, sin_ref, u_ref, in_ref, gg_ref):
    h = pl.program_id(0)
    reps = raw_ref.shape[1] // cos_ref.shape[0]
    cosine = jnp.concatenate([cos_ref[...]] * reps, 0)
    sine = jnp.concatenate([sin_ref[...]] * reps, 0)
    for i, grad in enumerate((dq_ref[...], dk_ref[...])):
        u = turn(grad, cosine, -sine)
        hat = raw_ref[i] * s_ref[i]
        product = u * hat
        u_ref[i] = u
        gg_ref[i] = jnp.sum(product, 0, keepdims=True)
        row = jnp.broadcast_to(jnp.sum(product * g_ref[i], -1, keepdims=True), in_ref.shape[1:])

        @pl.when(h == 0)
        def _():
            in_ref[i] = row

        @pl.when(h != 0)
        def _():
            in_ref[i] += row


def unturn(dq, dk, raw, scales, gains, cosine, sine):
    _, t, n = raw.shape
    h = HEAD_DIM
    length = cosine.shape[0]
    column = pl.BlockSpec((t, h), lambda i: (0, i))
    pair = pl.BlockSpec((2, t, h), lambda i: (0, 0, i))
    return call(
        unturn_kernel,
        "unturn",
        (n // h,),
        [
            column,
            column,
            pair,
            fixed((2, t, 1)),
            pl.BlockSpec((2, 1, h), lambda i: (0, 0, i)),
            fixed((length, h)),
            fixed((length, h)),
        ],
        [
            pair,
            pl.BlockSpec((2, t, 128), lambda i: (0, 0, 0)),
            pl.BlockSpec((2, 1, h), lambda i: (0, 0, i)),
        ],
        [sds((2, t, n), F32), sds((2, t, 128), F32), sds((2, 1, n), F32)],
        30 * t * n,
        24 * t * n,
    )(dq, dk, raw, scales, gains, cosine, sine)


def raw_grads_kernel(place_ref, u_ref, raw_ref, s_ref, in_ref, g_ref, dv_ref, n_ref, w_ref, kept_ref, *refs):
    gw_ref, outs, d_ref = refs[0], refs[1:-1], refs[-1]
    t, n = dv_ref.shape

    @pl.when(pl.program_id(0) == 0)
    def _():
        for i in range(2):
            hat = raw_ref[i] * s_ref[i]
            d_ref[:, i * n : (i + 1) * n] = (
                s_ref[i] * (u_ref[i] * g_ref[i] - hat * in_ref[i])
            ).astype(BF16)
        d_ref[:, 2 * n :] = dv_ref[...]

    pb, _, ds, _ = w_ref.shape
    w = jnp.concatenate([w_ref[:, c].reshape(pb * ds, n) for c in range(3)], 1)
    rows = outs[0].shape[0]
    for r, o in enumerate(outs):
        o[...] = nt(d_ref[pl.ds(pl.multiple_of(place_ref[r], rows), rows), :], w).astype(BF16)
    grads = tn(n_ref[...], d_ref[...]).astype(BF16)
    for c in range(3):
        gw_ref[:, c] = grads[:, c * n : (c + 1) * n].reshape(pb, ds, n)


def raw_grads(places, u, raw, scales, inner, gains, dv, normed, w, kept, pieces):
    t, d = normed.shape
    p, _, ds, n = w.shape
    pb = max(1, TILE // ds)
    block = pl.BlockSpec((pb, 3, ds, n), lambda g, *_: (g, 0, 0, 0))
    return call(
        raw_grads_kernel,
        "rawgrads",
        (p // pb,),
        [
            fixed((2, t, n)),
            fixed((2, t, n)),
            fixed((2, t, 1)),
            fixed((2, t, 1)),
            fixed((2, 1, n)),
            fixed((t, n)),
            pl.BlockSpec((t, pb * ds), lambda g, *_: (0, g)),
            block,
            pl.BlockSpec(memory_space=pl.ANY),
        ],
        [block] + [pl.BlockSpec((t // pieces, pb * ds), lambda g, *_: (0, g))] * pieces,
        [sds(kept.shape, BF16)] + [sds((t // pieces, d), BF16)] * pieces,
        12 * t * d * n,
        2 * (6 * d * n + 2 * t * d) + 20 * t * n,
        scratch=[pltpu.VMEM((t, 3 * n), BF16)],
        prefetch=1,
        aliases={9: 0},
    )(places, u, raw, scales, inner, gains, dv, normed, w, kept)


def swap(value, axis):
    return lax.ppermute(value, axis, [(0, 1), (1, 0)])


def spread(value):
    rows = swap(value, "row")
    return (value, swap(value, "core"), rows, swap(rows, "core"))


def across(value, k):
    size = lax.axis_size("tp")
    return lax.ppermute(value, "tp", [(i, i ^ k) for i in range(size)])


def gather(own):
    far = across(own, 2)
    return [own, across(own, 1), far, across(far, 1)]


def scatter(chunks):
    kind = chunks[0].dtype
    near = chunks[2].astype(F32) + across(chunks[3], 1).astype(F32)
    near, beside = lax.optimization_barrier((near.astype(kind), chunks[1]))
    return [chunks[0], across(beside, 1), across(near, 2)]


def total(pieces):
    return sum(v.astype(F32) for v in pieces)


def both_cores(own, other, pieces):
    rows = own.shape[0] // pieces
    got = swap(other, "core")
    return [
        (own[r * rows : (r + 1) * rows].astype(F32) + got[r * rows : (r + 1) * rows].astype(F32)).astype(BF16)
        for r in range(pieces)
    ]


def in_place_kernel(place_ref, *refs):
    for r, piece in enumerate(refs[:-1]):

        @pl.when(pl.program_id(0) == r)
        def _():
            refs[-1][...] = piece[...]


def in_place(pieces, places):
    rows, d = pieces[0].shape
    count = len(pieces)
    return call(
        in_place_kernel,
        "inplace",
        (count,),
        [fixed((rows, d))] * count,
        pl.BlockSpec((rows, d), lambda r, place: (place[r] // rows, 0)),
        sds((rows * count, d), pieces[0].dtype),
        0,
        4 * rows * count * d,
        prefetch=1,
    )(places, *pieces)


def meet(value):
    value = value + across(value, 1)
    return value + across(value, 2)


def relative(value, places, pieces):
    rows = value.shape[0] // pieces
    return [lax.dynamic_slice_in_dim(value, places[r], rows, 0) for r in range(pieces)]


def body(
    inputs,
    prefix,
    expert_ids,
    norm_gains,
    qkv_weight,
    out_weight,
    router_weight,
    gate_up_weight,
    down_weight,
    cotangent,
    *,
    chunks,
):
    sequences, length, width = inputs.shape
    t = sequences * length
    tp = lax.axis_size("tp")
    quarter = t // tp
    column = lax.axis_index("tp")
    core = lax.axis_index("core")
    ctx = lax.axis_index("row") * 2 + core
    experts = router_weight.shape[1]
    half = experts // 2
    e = half // chunks
    x = inputs.reshape(t, width)
    places = jnp.stack([column ^ r for r in range(tp)]).astype(jnp.int32) * quarter
    cots = relative(cotangent.reshape(t, width), places, tp)
    c0 = jnp.concatenate(cots, 0)
    ids = relative(expert_ids.reshape(t, -1), places, tp)
    ids0 = jnp.concatenate(ids, 0)
    x_q = lax.dynamic_slice_in_dim(x, column * quarter, quarter, 0).astype(F32)

    attn_local = jnp.concatenate([qkv_weight, out_weight[None]], 0)
    attn_w = lax.all_gather(attn_local, PLANE, axis=0, tiled=False)
    gains_low = lax.all_gather(norm_gains, PLANE, axis=1, tiled=True)
    router = lax.all_gather(router_weight, PLANE, axis=0, tiled=True)
    triple = jnp.concatenate([gate_up_weight, down_weight[:, None]], 1)
    ds, f = triple.shape[2:]
    grouped = triple.reshape(2, chunks, e, 3, ds, f)
    ws = []
    for k in range(chunks):
        mine = lax.all_to_all(grouped[:, k], "core", 0, 0, tiled=True)
        full = lax.all_gather(mine, FR, axis=0, tiled=False)
        ws.append(full.reshape(-1, e, 3, ds, f))
    attn_w, gains_low, router = lax.optimization_barrier((attn_w, gains_low, router))
    p = attn_w.shape[0]
    c1 = swap(c0, "core")
    ids1 = swap(ids0, "core")

    gains = gains_low.astype(F32)
    n = attn_w.shape[3]
    router_rows = jnp.concatenate([router.T, jnp.zeros((128 - experts, width), BF16)], 0)

    normed_one, raw, values, squares = qkv_project(x, gains[0:1], attn_w)
    v_blocks = spread(values)
    squares = meet(squares[:, :, 0])
    scales = lax.rsqrt(squares / width + EPSILON)[:, :, None]
    own_gains = lax.dynamic_slice_in_dim(gains[2:4], column * n, n, 1)[:, None, :]
    halves = jnp.arange(0, HEAD_DIM, 2).astype(F32) / HEAD_DIM
    inverse = 1.0 / THETA**halves
    positions = ctx * length + jnp.arange(length, dtype=jnp.int32)
    angles = positions.astype(F32)[:, None] * inverse[None, :]
    cosine = jnp.concatenate([jnp.cos(angles)] * 2, 1)
    sine = jnp.concatenate([-jnp.sin(angles), jnp.sin(angles)], 1)
    queries, keys = prepare(raw, scales, own_gains, cosine, sine)
    blocks = spread(keys) + v_blocks
    offsets = jnp.stack([ctx, ctx ^ 1, ctx ^ 2, ctx ^ 3, ctx]).astype(jnp.int32) * length
    scal = jnp.concatenate([offsets, prefix.astype(jnp.int32)])
    heads = attend(scal, queries, blocks, length)
    mid = x_q + total(scatter(project_out(places, heads, attn_w, tp)))
    scale_two = lax.rsqrt(jnp.mean(mid * mid, -1, keepdims=True) + EPSILON)
    normal_two = mid * scale_two
    two_low = (normal_two * gains[1]).astype(BF16)
    x0 = jnp.concatenate(gather(two_low), 0)
    x1 = swap(x0, "core")

    g0 = route(x0, router_rows, ids0, experts)
    g1 = route(x1, router_rows, ids1, experts)
    hids, dgus, d_gates, grads = [], [], None, []
    for k in range(chunks):
        where = jnp.stack([core * half + k * e, k * e]).astype(jnp.int32)
        hid, dgu, dg = expert_up(where, x0, x1, c0, c1, g0, g1, ws[k])
        hids.append(hid)
        dgus.append(dgu)
        d_gates = dg if d_gates is None else d_gates + dg
        if k < chunks - 1:
            grad = expert_grads(x0, x1, c0, c1, hid, dgu, p, e)
            grad, x0, x1 = lax.optimization_barrier((grad, x0, x1))
            grads.append(grad)
    dx0, dx1 = expert_down(dgus, ws, 0, 2, "expert_dx")
    dx0, dx1, hids, dgus = lax.optimization_barrier((dx0, dx1, hids, dgus))
    dx, hids, dgus = lax.optimization_barrier((both_cores(dx0, dx1, tp), hids, dgus))
    d_normed = scatter(dx)
    gates_all = d_gates[:, :half]
    away = swap(gates_all[t:], "core")
    gates_own = jnp.where(
        core == 0,
        jnp.concatenate([gates_all[:t], away], 1),
        jnp.concatenate([away, gates_all[:t]], 1),
    )
    gate_grads = scatter([gates_own[r * quarter : (r + 1) * quarter] for r in range(tp)])
    grads.append(expert_grads(x0, x1, c0, c1, hids[-1], dgus[-1], p, e))
    last, hids = lax.optimization_barrier((grads[-1], hids))
    grads[-1] = last
    m0, m1 = expert_down(hids, ws, 2, 1, "expert_out")
    d_normed, gate_grads, m0, m1 = lax.optimization_barrier((d_normed, gate_grads, m0, m1))
    d_normed = total(d_normed)
    gate_grads = total(gate_grads)
    grads = [
        lax.psum_scatter(g.reshape(p // 2, 2, e, 3, ds, f), FR, scatter_dimension=0, tiled=False)
        for g in grads
    ]

    chosen = jnp.sum((ids[0][:, :, None] == jnp.arange(experts, dtype=jnp.int32)).astype(F32), 1)
    router_probs = jax.nn.softmax(jnp.dot(two_low, router, preferred_element_type=F32), -1)
    masked = gate_grads * chosen
    d_logits = (router_probs * (masked - jnp.sum(router_probs * masked, -1, keepdims=True))).astype(BF16)
    grad_router = tn(d_logits, two_low)
    d_normed = d_normed + nt(d_logits, router)
    weighted = d_normed * gains[1]
    d_mid = cots[0].astype(F32) + scale_two * (
        weighted - normal_two * jnp.mean(weighted * normal_two, -1, keepdims=True)
    )
    gain_two = jnp.sum(d_normed * normal_two, 0)
    d_mid_low = jnp.concatenate(gather(d_mid.astype(BF16)), 0)

    m0, m1, d_mid_low = lax.optimization_barrier((m0, m1, d_mid_low))
    d_heads = heads_grad(places, d_mid_low, attn_w, tp)
    grad_out = out_weight_grad(places, d_mid_low, heads, p, tp)
    moe = scatter(both_cores(m0, m1, tp))
    dq, b0, b1, b2, b3 = attend_back(scal, queries, blocks, d_heads, length)
    r1 = swap(b1, "core")
    r3 = swap(b3, "core")
    r2 = swap((b2.astype(F32) + r3.astype(F32)).astype(BF16), "row")
    d_kv = b0.astype(F32) + r1.astype(F32) + r2.astype(F32)
    dq, d_kv, moe, grads[0] = lax.optimization_barrier((dq, d_kv, moe, grads[0]))
    out_pieces = gather((mid + total(moe)).astype(BF16))
    u, inner, gain_qk = unturn(dq, d_kv[0], raw, scales, own_gains, cosine, sine)
    inner = (meet(inner[:, :, 0]) / width)[:, :, None]
    placed = lax.dynamic_update_slice_in_dim(
        jnp.zeros((2, width), F32), gain_qk[:, 0, :], column * n, 1
    )
    grad_attn, *d_one = raw_grads(
        places, u, raw, scales, inner, own_gains, d_kv[1].astype(BF16), normed_one, attn_w, grad_out, tp
    )
    grad_attn, grads[-1] = lax.optimization_barrier((grad_attn, grads[-1]))
    grad_attn = lax.psum_scatter(grad_attn, PLANE, scatter_dimension=0, tiled=False)
    d_one = total(scatter(d_one))
    scale_one = lax.rsqrt(jnp.mean(x_q * x_q, -1, keepdims=True) + EPSILON)
    normal_one = x_q * scale_one
    weighted_one = d_one * gains[0]
    grad_in = d_mid + scale_one * (
        weighted_one - normal_one * jnp.mean(weighted_one * normal_one, -1, keepdims=True)
    )
    gain_one = jnp.sum(d_one * normal_one, 0)
    grad_inputs = in_place(gather(grad_in.astype(BF16)), places).reshape(inputs.shape)
    outputs = in_place(out_pieces, places).reshape(inputs.shape)

    small = jnp.concatenate([grad_router, gain_one[None], gain_two[None], placed], 0)
    rows = small.shape[0]
    small = small.reshape(rows, p, ds).transpose(1, 0, 2)
    small = jnp.sum(lax.all_to_all(small, PLANE, 0, 0, tiled=True), 0)
    small = meet(small)
    owned_gains = small[experts:]
    owned_router = small[:experts].T

    owned = []
    for g in grads:
        owned.append(lax.all_to_all(g, "core", 0, 0, tiled=True))
    stacked = jnp.stack(owned, 1).astype(F32)
    owned_gate_up = stacked[:, :, :, :2].reshape(experts, 2, ds, f)
    owned_down = stacked[:, :, :, 2].reshape(experts, ds, f)
    grad_attn = grad_attn.astype(F32)
    return (
        outputs,
        grad_inputs,
        owned_gains,
        grad_attn[:3],
        grad_attn[3],
        owned_router,
        owned_gate_up,
        owned_down,
    )


def solution(mesh):
    fsdp, ctx, tp = (mesh.shape[a] for a in ("fsdp", "ctx", "tp"))
    fine = Mesh(mesh.devices.reshape(fsdp, ctx // 2, 2, tp), EVERY)
    tokens = P("fsdp", ("row", "core"), None)
    weights = (
        P(None, PLANE),
        P(None, PLANE, "tp"),
        P(PLANE, "tp"),
        P(PLANE, None),
        P(None, None, PLANE, "tp"),
        P(None, PLANE, "tp"),
    )
    return jax.shard_map(
        functools.partial(body, chunks=2),
        mesh=fine,
        in_specs=(tokens, P("fsdp"), tokens) + weights + (tokens,),
        out_specs=(tokens, tokens) + weights,
        check_vma=False,
    )
```

```python
import functools

import jax
import jax.numpy as jnp
from jax import lax
from jax.experimental import pallas as pl
from jax.experimental.pallas import tpu as pltpu
from jax.sharding import Mesh, PartitionSpec as P

HEAD_DIM = 128
EPSILON = 1e-05
THETA = 10000.0
TILE = 256
F32 = jnp.float32
BF16 = jnp.bfloat16
FR = ("fsdp", "row")
LANES = 128
PLANE = ("fsdp", "row", "core")
EVERY = ("fsdp", "row", "core", "tp")


def nn(a, b):
    return lax.dot_general(a, b, (((1,), (0,)), ((), ())), preferred_element_type=F32)


def nt(a, b):
    return lax.dot_general(a, b, (((1,), (1,)), ((), ())), preferred_element_type=F32)


def tn(a, b):
    return lax.dot_general(a, b, (((0,), (0,)), ((), ())), preferred_element_type=F32)


def call(kernel, name, grid, in_specs, out_specs, out_shape, flops, moved, scratch=(), prefetch=0, limit=56, aliases=None):
    return pl.pallas_call(
        kernel,
        name=name,
        out_shape=out_shape,
        grid_spec=pltpu.PrefetchScalarGridSpec(
            num_scalar_prefetch=prefetch,
            grid=grid,
            in_specs=in_specs,
            out_specs=out_specs,
            scratch_shapes=list(scratch),
        ),
        input_output_aliases=aliases or {},
        compiler_params=pltpu.CompilerParams(
            dimension_semantics=("arbitrary",) * len(grid), vmem_limit_bytes=limit << 20
        ),
        cost_estimate=pl.CostEstimate(flops=int(flops), bytes_accessed=int(moved), transcendentals=0),
    )


def fixed(shape):
    return pl.BlockSpec(shape, lambda *a: (0,) * len(shape), pipeline_mode=pl.Buffered(1))


def sds(shape, dtype):
    return jax.ShapeDtypeStruct(shape, dtype)


def qkv_kernel(x_ref, g_ref, w_ref, n_ref, raw_ref, v_ref, sq_ref):
    c = pl.program_id(0)

    @pl.when(c == 0)
    def _():
        x = x_ref[...].astype(F32)
        r = lax.rsqrt(jnp.mean(x * x, -1, keepdims=True) + EPSILON)
        n_ref[...] = (x * r * g_ref[...]).astype(BF16)

    w = w_ref[...]
    y = nn(n_ref[...], w.reshape(w.shape[0] * w.shape[2], w.shape[3]))

    @pl.when(c < 2)
    def _():
        raw_ref[0] = y
        sq_ref[0] = jnp.broadcast_to(jnp.sum(y * y, -1, keepdims=True), sq_ref.shape[1:])

    @pl.when(c == 2)
    def _():
        v_ref[...] = y.astype(BF16)


def qkv_project(x, gain, w):
    t, d = x.shape
    p, _, ds, n = w.shape
    return call(
        qkv_kernel,
        "qkv",
        (3,),
        [
            fixed((t, d)),
            fixed((1, d)),
            pl.BlockSpec((p, 1, ds, n), lambda c: (0, c, 0, 0)),
        ],
        [
            pl.BlockSpec((t, d), lambda c: (0, 0)),
            pl.BlockSpec((1, t, n), lambda c: (jnp.minimum(c, 1), 0, 0)),
            pl.BlockSpec((t, n), lambda c: (0, 0)),
            pl.BlockSpec((1, t, 128), lambda c: (jnp.minimum(c, 1), 0, 0)),
        ],
        [sds((t, d), BF16), sds((2, t, n), F32), sds((t, n), BF16), sds((2, t, 128), F32)],
        6 * t * d * n,
        2 * (3 * d * n + 2 * t * d) + 10 * t * n,
    )(x, gain, w)


def turn(v, cosine, sine):
    half = v.shape[-1] // 2
    return v * cosine + pltpu.roll(v, half, 1) * sine


def prep_kernel(raw_ref, s_ref, g_ref, cos_ref, sin_ref, q_ref, k_ref):
    reps = raw_ref.shape[1] // cos_ref.shape[0]
    cosine = jnp.concatenate([cos_ref[...]] * reps, 0)
    sine = jnp.concatenate([sin_ref[...]] * reps, 0)
    q = raw_ref[0] * s_ref[0] * g_ref[0]
    k = raw_ref[1] * s_ref[1] * g_ref[1]
    q_ref[...] = turn(q, cosine, sine).astype(BF16)
    k_ref[...] = turn(k, cosine, sine).astype(BF16)


def prepare(raw, scales, gains, cosine, sine):
    _, t, n = raw.shape
    h = HEAD_DIM
    length = cosine.shape[0]
    return call(
        prep_kernel,
        "prep",
        (n // h,),
        [
            pl.BlockSpec((2, t, h), lambda i: (0, 0, i)),
            fixed((2, t, 1)),
            pl.BlockSpec((2, 1, h), lambda i: (0, 0, i)),
            fixed((length, h)),
            fixed((length, h)),
        ],
        [pl.BlockSpec((t, h), lambda i: (0, i))] * 2,
        [sds((t, n), BF16)] * 2,
        20 * t * n,
        12 * t * n,
    )(raw, scales, gains, cosine, sine)


def masked_probs(s, scal_ref, q, ks):
    length = q.shape[0]
    prefix = scal_ref[5 + s]
    rows = lax.broadcasted_iota(jnp.int32, (length, length), 0) + scal_ref[4]
    columns = lax.broadcasted_iota(jnp.int32, (length, length), 1)
    pieces = []
    for b, k in enumerate(ks):
        place = columns + scal_ref[b]
        visible = (place <= rows) | (place < prefix)
        pieces.append(jnp.where(visible, nt(q, k) * HEAD_DIM ** (-0.5), -1e30))
    scores = jnp.concatenate(pieces, 1)
    expo = jnp.exp(scores - jnp.max(scores, -1, keepdims=True))
    return expo / jnp.sum(expo, -1, keepdims=True)


def attend_kernel(scal_ref, q_ref, *refs):
    o_ref = refs[8]
    probs = masked_probs(pl.program_id(0), scal_ref, q_ref[...], [r[...] for r in refs[:4]])
    v = jnp.concatenate([r[...] for r in refs[4:8]], 0)
    o_ref[...] = nn(probs.astype(BF16), v).astype(BF16)


def attend(scal, q, blocks, length):
    t, n = q.shape
    h = HEAD_DIM
    one = pl.BlockSpec((length, h), lambda s, i, *_: (s, i))
    return call(
        attend_kernel,
        "attend",
        (t // length, n // h),
        [one] * 9,
        one,
        sds((t, n), BF16),
        16 * t * n * length,
        24 * t * n,
        prefetch=1,
    )(scal, q, *blocks)


def attend_back_kernel(scal_ref, q_ref, *refs):
    g_ref, dq_ref, outs = refs[8], refs[9], refs[10:]
    length = q_ref.shape[0]
    q = q_ref[...]
    grad = g_ref[...]
    probs = masked_probs(pl.program_id(0), scal_ref, q, [r[...] for r in refs[:4]])
    k = jnp.concatenate([r[...] for r in refs[:4]], 0)
    v = jnp.concatenate([r[...] for r in refs[4:8]], 0)
    d_probs = nt(grad, v)
    inner = jnp.sum(probs * d_probs, -1, keepdims=True)
    d_scores = (probs * (d_probs - inner)).astype(BF16)
    scale = HEAD_DIM ** (-0.5)
    dq_ref[...] = nn(d_scores, k) * scale
    dk = (tn(d_scores, q) * scale).astype(BF16)
    dv = tn(probs.astype(BF16), grad).astype(BF16)
    for b, o in enumerate(outs):
        o[0] = dk[b * length : (b + 1) * length]
        o[1] = dv[b * length : (b + 1) * length]


def attend_back(scal, q, blocks, grad, length):
    t, n = q.shape
    h = HEAD_DIM
    one = pl.BlockSpec((length, h), lambda s, i, *_: (s, i))
    two = pl.BlockSpec((2, length, h), lambda s, i, *_: (0, s, i))
    return call(
        attend_back_kernel,
        "attend_back",
        (t // length, n // h),
        [one] * 10,
        [one] + [two] * 4,
        [sds((t, n), F32)] + [sds((2, t, n), BF16)] * 4,
        40 * t * n * length,
        48 * t * n,
        prefetch=1,
    )(scal, q, *blocks, grad)


def out_kernel(place_ref, h_ref, w_ref, *outs):
    w = w_ref[...]
    w = w.reshape(-1, w.shape[-1])
    rows = outs[0].shape[0]
    heads = jnp.concatenate(
        [h_ref[pl.ds(pl.multiple_of(place_ref[r], rows), rows), :] for r in range(len(outs))], 0
    )
    y = nt(heads, w).astype(BF16)
    for r, o in enumerate(outs):
        o[...] = y[r * rows : (r + 1) * rows]


def project_out(places, heads, w, pieces):
    t, n = heads.shape
    p, _, ds, _ = w.shape
    pb = max(1, 2 * TILE // ds)
    return call(
        out_kernel,
        "outproj",
        (p // pb,),
        [fixed((t, n)), pl.BlockSpec((pb, 1, ds, n), lambda g, *_: (g, 3, 0, 0))],
        [pl.BlockSpec((t // pieces, pb * ds), lambda g, *_: (0, g))] * pieces,
        [sds((t // pieces, p * ds), BF16)] * pieces,
        2 * t * n * p * ds,
        2 * (t * n + n * p * ds + t * p * ds),
        prefetch=1,
    )(places, heads, w)


def d_heads_kernel(place_ref, g_ref, w_ref, o_ref, *, pieces):
    w = w_ref[...]
    y = nn(g_ref[...], w.reshape(w.shape[0] * w.shape[2], w.shape[3])).astype(BF16)
    rows = y.shape[0] // pieces
    for r in range(pieces):
        o_ref[pl.ds(pl.multiple_of(place_ref[r], rows), rows), :] = y[r * rows : (r + 1) * rows]


def heads_grad(places, grad, w, pieces):
    t, d = grad.shape
    p, _, ds, n = w.shape
    return call(
        functools.partial(d_heads_kernel, pieces=pieces),
        "dheads",
        (1,),
        [fixed((t, d)), pl.BlockSpec((p, 1, ds, n), lambda g, *_: (0, 3, 0, 0), pipeline_mode=pl.Buffered(1))],
        fixed((t, n)),
        sds((t, n), BF16),
        2 * t * n * d,
        2 * (t * n + n * d + t * d),
        prefetch=1,
    )(places, grad, w)


def grad_out_kernel(place_ref, g_ref, h_ref, o_ref, *, pieces):
    rows = g_ref.shape[0] // pieces
    heads = jnp.concatenate(
        [h_ref[pl.ds(pl.multiple_of(place_ref[r], rows), rows), :] for r in range(pieces)], 0
    )
    o_ref[...] = tn(g_ref[...], heads).astype(BF16).reshape(o_ref.shape)


def out_weight_grad(places, grad, heads, p, pieces):
    t, d = grad.shape
    n = heads.shape[1]
    ds = d // p
    pb = max(1, TILE // ds)
    return call(
        functools.partial(grad_out_kernel, pieces=pieces),
        "gradout",
        (p // pb,),
        [pl.BlockSpec((t, pb * ds), lambda g, *_: (0, g)), fixed((t, n))],
        pl.BlockSpec((pb, ds, n), lambda g, *_: (g, 0, 0)),
        sds((p, ds, n), BF16),
        2 * t * n * d,
        2 * (t * n + n * d + t * d),
        prefetch=1,
    )(places, grad, heads)


def norm_two_kernel(x_ref, a_ref, b_ref, c_ref, g_ref, w_ref, ids_ref, mid_ref, ext_ref, probs_ref, chosen_ref, *, experts):
    mid = x_ref[...].astype(F32) + a_ref[...].astype(F32) + b_ref[...].astype(F32) + c_ref[...].astype(F32)
    mid_ref[...] = mid
    d = mid.shape[1]
    r = lax.rsqrt(jnp.mean(mid * mid, -1, keepdims=True) + EPSILON)
    low = (mid * r * g_ref[...]).astype(BF16)
    ext_ref[:, :d] = low
    logits = nt(low, w_ref[...])
    lane = lax.broadcasted_iota(jnp.int32, logits.shape, 1)
    logits = jnp.where(lane < experts, logits, -1e30)
    expo = jnp.exp(logits - jnp.max(logits, -1, keepdims=True))
    probs = expo / jnp.sum(expo, -1, keepdims=True)
    chosen = jnp.zeros_like(probs)
    for j in range(ids_ref.shape[1]):
        chosen += (ids_ref[:, j : j + 1] == lane).astype(F32)
    probs_ref[...] = probs
    chosen_ref[...] = chosen
    gates = probs * chosen
    high = gates.astype(BF16)
    rest = (gates - high.astype(F32)).astype(BF16)
    ext_ref[:, d:] = jnp.concatenate([high[:, : LANES // 2], rest[:, : LANES // 2]], 1)


def norm_two(x, sums, gain, router, ids, experts):
    t, d = x.shape
    return call(
        functools.partial(norm_two_kernel, experts=experts),
        "norm_two",
        (1,),
        [fixed((t, d))] * 4 + [fixed((1, d)), fixed(router.shape), fixed(ids.shape)],
        [fixed((t, d)), fixed((t, d + LANES)), fixed((t, LANES)), fixed((t, LANES))],
        [sds((t, d), F32), sds((t, d + LANES), BF16), sds((t, LANES), F32), sds((t, LANES), F32)],
        2 * t * d * LANES,
        14 * t * d,
    )(x, *sums, gain, router, ids)


def norm_two_back_kernel(a_ref, b_ref, c_ref, mid_ref, ext_ref, probs_ref, chosen_ref, cot_ref, g_ref, w_ref, *outs):
    mid_grad_ref, low_ref, gain_ref, router_ref = outs
    d = mid_ref.shape[1]
    du = a_ref[...].astype(F32) + b_ref[...].astype(F32) + c_ref[...].astype(F32)
    probs = probs_ref[...]
    masked = du[:, d:] * chosen_ref[...]
    d_logits = (probs * (masked - jnp.sum(probs * masked, -1, keepdims=True))).astype(BF16)
    router_ref[...] = tn(d_logits, ext_ref[:, :d])
    u = du[:, :d] + nn(d_logits, w_ref[...])
    mid = mid_ref[...]
    r = lax.rsqrt(jnp.mean(mid * mid, -1, keepdims=True) + EPSILON)
    hat = mid * r
    gain_ref[...] = jnp.sum(u * hat, 0, keepdims=True)
    w = u * g_ref[...]
    grad = cot_ref[...].astype(F32) + r * (w - hat * jnp.mean(w * hat, -1, keepdims=True))
    mid_grad_ref[...] = grad
    low_ref[...] = grad.astype(BF16)


def norm_two_back(sums, mid, ext, probs, chosen, cot, gain, router):
    t, d = mid.shape
    wide = fixed((t, d + LANES))
    return call(
        norm_two_back_kernel,
        "norm_two_back",
        (1,),
        [wide] * 3
        + [fixed((t, d)), wide, fixed((t, LANES)), fixed((t, LANES)), fixed((t, d)), fixed((1, d)), fixed(router.shape)],
        [fixed((t, d)), fixed((t, d)), fixed((1, d)), fixed((LANES, d))],
        [sds((t, d), F32), sds((t, d), BF16), sds((1, d), F32), sds((LANES, d), F32)],
        4 * t * d * LANES,
        20 * t * d,
    )(*sums, mid, ext, probs, chosen, cot, gain, router)


def norm_one_back_kernel(a_ref, b_ref, c_ref, x_ref, mid_grad_ref, g_ref, o_ref, gain_ref):
    u = a_ref[...].astype(F32) + b_ref[...].astype(F32) + c_ref[...].astype(F32)
    x = x_ref[...].astype(F32)
    r = lax.rsqrt(jnp.mean(x * x, -1, keepdims=True) + EPSILON)
    hat = x * r
    gain_ref[...] = jnp.sum(u * hat, 0, keepdims=True)
    w = u * g_ref[...]
    o_ref[...] = (mid_grad_ref[...] + r * (w - hat * jnp.mean(w * hat, -1, keepdims=True))).astype(BF16)


def norm_one_back(sums, x, mid_grad, gain):
    t, d = x.shape
    return call(
        norm_one_back_kernel,
        "norm_one_back",
        (1,),
        [fixed((t, d))] * 5 + [fixed((1, d))],
        [fixed((t, d)), fixed((1, d))],
        [sds((t, d), BF16), sds((1, d), F32)],
        20 * t * d,
        14 * t * d,
    )(*sums, x, mid_grad, gain)


def expert_kernel(first_ref, *refs, parts):
    xs, cs, w_ref = refs[:parts], refs[parts : 2 * parts], refs[2 * parts]
    hid_ref, dgu_ref, dg_ref = refs[2 * parts + 1 :]
    e = pl.program_id(0)
    t = cs[0].shape[0]
    d = cs[0].shape[1]

    @pl.when(e == 0)
    def _():
        dg_ref[...] = jnp.zeros_like(dg_ref)

    f = w_ref.shape[4]
    me = first_ref[0] + e
    lane = lax.broadcasted_iota(jnp.int32, (t, LANES), 1)
    for part, (x_ref, c_ref) in enumerate(zip(xs, cs)):

        def block(x_ref=x_ref, c_ref=c_ref, to=slice(part * t, (part + 1) * t)):
            x = x_ref[:, :d]
            a = nn(x, w_ref[:, 0, 0].reshape(d, f))
            b = nn(x, w_ref[:, 0, 1].reshape(d, f))
            dh = nn(c_ref[...], w_ref[:, 0, 2].reshape(d, f))
            mine = (lane == me) | (lane == me + LANES // 2)
            gate = jnp.sum(jnp.where(mine, x_ref[:, d:].astype(F32), 0.0), -1, keepdims=True)
            sigma = jax.nn.sigmoid(a)
            swish = a * sigma
            act = swish * b
            hid_ref[to, :] = (gate * act).astype(BF16)
            d_gate = jnp.sum(dh * act, -1, keepdims=True)
            dg_ref[to, :] += jnp.where(lane == me, d_gate, 0.0)
            inner = dh * gate
            dgu_ref[to, :f] = (inner * b * sigma * (1.0 + a * (1.0 - sigma))).astype(BF16)
            dgu_ref[to, f:] = (inner * swish).astype(BF16)

        block()


def expert_up(first, xs, cs, w):
    t, d = cs[0].shape
    parts = len(cs)
    p, e, _, ds, f = w.shape
    every = parts * t
    return call(
        functools.partial(expert_kernel, parts=parts),
        "expert_up",
        (e,),
        [fixed(x.shape) for x in xs]
        + [fixed((t, d))] * parts
        + [pl.BlockSpec((p, 1, 3, ds, f), lambda i, *_: (0, i, 0, 0, 0))],
        [
            pl.BlockSpec((every, f), lambda i, *_: (0, i)),
            pl.BlockSpec((every, 2 * f), lambda i, *_: (0, i)),
            pl.BlockSpec((every, LANES), lambda i, *_: (0, 0)),
        ],
        [sds((every, e * f), BF16), sds((every, e * 2 * f), BF16), sds((every, LANES), F32)],
        6 * every * d * f * e,
        2 * (3 * d * f * e + 2 * every * d + 3 * every * f * e),
        prefetch=1,
    )(first, *xs, *cs, w)


def expert_grad_kernel(col_ref, *refs, parts, groups, sides):
    xs, cs = refs[:parts], refs[parts : 2 * parts]
    hids, dgus = refs[2 * parts : 2 * parts + groups], refs[2 * parts + groups : 2 * parts + 2 * groups]
    outs = refs[2 * parts + 2 * groups :]
    pb, e, _, ds, f = outs[0].shape
    x = jnp.concatenate([r[...] for r in xs], 0)
    c = jnp.concatenate([r[...] for r in cs], 0)
    share = x.shape[0] // groups
    step = pl.program_id(0)
    each = pl.num_programs(0) // sides

    def product(left, refs):
        return sum(tn(left[g * share : (g + 1) * share], r[...]) for g, r in enumerate(refs)).astype(BF16)

    both = product(x, dgus)
    down = product(c, hids)
    for side, o in enumerate(outs):

        @pl.when(step // each == side)
        def _():
            for i in range(e):
                o[:, i, 0] = both[:, 2 * i * f : (2 * i + 1) * f].reshape(pb, ds, f)
                o[:, i, 1] = both[:, (2 * i + 1) * f : (2 * i + 2) * f].reshape(pb, ds, f)
                o[:, i, 2] = down[:, i * f : (i + 1) * f].reshape(pb, ds, f)


def expert_grads(columns, xs, cs, hids, dgus, p, e, sides):
    t, d = cs[0].shape
    parts = len(cs)
    groups = len(hids)
    ds = d // p
    f = hids[0].shape[1] // e
    pb = max(1, TILE // ds)
    steps = p // pb
    each = steps // sides
    column = pl.BlockSpec((t, pb * ds), lambda g, col: (0, col[g]))

    def out(side):
        return pl.BlockSpec(
            (pb, e, 3, ds, f), lambda g, col: (jnp.clip(g - side * each, 0, each - 1), 0, 0, 0, 0)
        )

    return call(
        functools.partial(expert_grad_kernel, parts=parts, groups=groups, sides=sides),
        "expert_grad",
        (steps,),
        [column] * (2 * parts) + [fixed(h.shape) for h in hids] + [fixed(g.shape) for g in dgus],
        [out(side) for side in range(sides)],
        [sds((p // sides, e, 3, ds, f), BF16)] * sides,
        6 * parts * t * d * f * e,
        2 * (3 * d * f * e + 2 * parts * t * d + 3 * parts * t * f * e),
        prefetch=1,
    )(columns, *xs, *cs, *hids, *dgus)


def settle_kernel(spot_ref, *refs, pieces):
    gate_up_ref, down_ref = refs[-2:]
    each = pl.num_programs(0) // pieces
    for r in range(pieces):

        @pl.when(pl.program_id(0) // each == r)
        def _():
            gate_up_ref[...] = refs[r][:, :2].astype(F32)
            down_ref[...] = refs[r][:, 2].astype(F32)


def settle(spots, pieces, kept, experts):
    e, _, ds, f = pieces[0].shape
    count = len(pieces)
    each = e // 2

    def piece(r):
        return pl.BlockSpec((2, 3, ds, f), lambda g, spot: (jnp.clip(g - r * each, 0, each - 1), 0, 0, 0))

    return call(
        functools.partial(settle_kernel, pieces=count),
        "settle",
        (count * each,),
        [piece(r) for r in range(count)] + [pl.BlockSpec(memory_space=pl.ANY)] * len(kept),
        [
            pl.BlockSpec((2, 2, ds, f), lambda g, spot: (spot[g], 0, 0, 0)),
            pl.BlockSpec((2, ds, f), lambda g, spot: (spot[g], 0, 0)),
        ],
        [sds((experts, 2, ds, f), F32), sds((experts, ds, f), F32)],
        0,
        18 * count * e * ds * f,
        prefetch=1,
        aliases={1 + count + i: i for i in range(len(kept))},
    )(spots, *pieces, *kept)


def down_kernel(*refs, planes, chunks, sides, begun):
    acts, ws = refs[:chunks], refs[chunks : 2 * chunks]
    gates = refs[2 * chunks : 2 * chunks + sides]
    before = refs[2 * chunks + sides : 2 * chunks + sides + begun]
    outs = refs[2 * chunks + sides + begun :]
    g = pl.program_id(0)
    pb, _, _, ds, f = ws[0].shape
    wide = pb * ds
    rows = outs[0].shape[0]
    joined = [
        jnp.concatenate([w[:, i, c].reshape(wide, f) for i in range(w.shape[1]) for c in range(planes)], 1)
        for w in ws
    ]
    to = pl.ds(pl.multiple_of(g * wide, wide), wide)
    for part, o in enumerate(outs):
        own = slice(part * rows, (part + 1) * rows)
        value = sum(nt(a[own, :], w) for a, w in zip(acts, joined))
        if begun:
            value += before[part][...].astype(F32)
        o[:, to] = value.astype(BF16)
    if sides:

        @pl.when(g == 0)
        def _():
            for part, o in enumerate(outs):
                own = slice(part * rows, (part + 1) * rows)
                o[:, o.shape[1] - LANES :] = sum(s[own, :] for s in gates).astype(BF16)


def expert_down(acts, ws, plane, planes, gates, before, parts, name):
    every = acts[0].shape[0]
    p, _, _, ds, f = ws[0].shape
    k = sum(a.shape[1] for a in acts)
    t = every // parts
    chunks = len(acts)
    d = p * ds + (LANES if gates else 0)
    pb = max(1, 2 * TILE // ds)
    return call(
        functools.partial(down_kernel, planes=planes, chunks=chunks, sides=len(gates), begun=len(before)),
        name,
        (p // pb,),
        [fixed(a.shape) for a in acts]
        + [pl.BlockSpec((pb, w.shape[1], planes, ds, f), lambda g: (g, 0, plane, 0, 0)) for w in ws]
        + [fixed((every, LANES))] * len(gates)
        + [pl.BlockSpec((t, pb * ds), lambda g: (0, g))] * len(before),
        [pl.BlockSpec((t, d), lambda g: (0, 0))] * parts,
        [sds((t, d), BF16)] * parts,
        2 * every * k * p * ds,
        2 * (every * k + k * p * ds) + 2 * every * d,
    )(*acts, *ws, *gates, *before)


def unturn_kernel(dq_ref, dk_ref, raw_ref, s_ref, g_ref, cos_ref, sin_ref, u_ref, in_ref, gg_ref):
    h = pl.program_id(0)
    reps = raw_ref.shape[1] // cos_ref.shape[0]
    cosine = jnp.concatenate([cos_ref[...]] * reps, 0)
    sine = jnp.concatenate([sin_ref[...]] * reps, 0)
    for i, grad in enumerate((dq_ref[...], dk_ref[...])):
        u = turn(grad, cosine, -sine)
        hat = raw_ref[i] * s_ref[i]
        product = u * hat
        u_ref[i] = u
        gg_ref[i] = jnp.sum(product, 0, keepdims=True)
        row = jnp.broadcast_to(jnp.sum(product * g_ref[i], -1, keepdims=True), in_ref.shape[1:])

        @pl.when(h == 0)
        def _():
            in_ref[i] = row

        @pl.when(h != 0)
        def _():
            in_ref[i] += row


def unturn(dq, dk, raw, scales, gains, cosine, sine):
    _, t, n = raw.shape
    h = HEAD_DIM
    length = cosine.shape[0]
    column = pl.BlockSpec((t, h), lambda i: (0, i))
    pair = pl.BlockSpec((2, t, h), lambda i: (0, 0, i))
    return call(
        unturn_kernel,
        "unturn",
        (n // h,),
        [
            column,
            column,
            pair,
            fixed((2, t, 1)),
            pl.BlockSpec((2, 1, h), lambda i: (0, 0, i)),
            fixed((length, h)),
            fixed((length, h)),
        ],
        [
            pair,
            pl.BlockSpec((2, t, 128), lambda i: (0, 0, 0)),
            pl.BlockSpec((2, 1, h), lambda i: (0, 0, i)),
        ],
        [sds((2, t, n), F32), sds((2, t, 128), F32), sds((2, 1, n), F32)],
        30 * t * n,
        24 * t * n,
    )(dq, dk, raw, scales, gains, cosine, sine)


def raw_back_kernel(place_ref, u_ref, raw_ref, s_ref, in_ref, g_ref, dv_ref, w_ref, d_ref, *outs):
    t, n = dv_ref.shape

    @pl.when(pl.program_id(0) == 0)
    def _():
        for i in range(2):
            hat = raw_ref[i] * s_ref[i]
            d_ref[:, i * n : (i + 1) * n] = (
                s_ref[i] * (u_ref[i] * g_ref[i] - hat * in_ref[i])
            ).astype(BF16)
        d_ref[:, 2 * n :] = dv_ref[...]

    pb, _, ds, _ = w_ref.shape
    w = jnp.concatenate([w_ref[:, c].reshape(pb * ds, n) for c in range(3)], 1)
    y = nt(d_ref[...], w).astype(BF16)
    rows = outs[0].shape[0]
    outs[0][...] = y[:rows]
    for r, o in enumerate(outs):
        for q in range(len(outs)):

            @pl.when(place_ref[r] == q * rows)
            def _():
                o[...] = y[q * rows : (q + 1) * rows]


def raw_back(places, u, raw, scales, inner, gains, dv, w, pieces):
    t, n = dv.shape
    p, _, ds, _ = w.shape
    d = p * ds
    pb = max(1, 2 * TILE // ds)
    return call(
        raw_back_kernel,
        "raw_back",
        (p // pb,),
        [
            fixed((2, t, n)),
            fixed((2, t, n)),
            fixed((2, t, 1)),
            fixed((2, t, 1)),
            fixed((2, 1, n)),
            fixed((t, n)),
            pl.BlockSpec((pb, 3, ds, n), lambda g, *_: (g, 0, 0, 0)),
        ],
        [pl.BlockSpec((t, 3 * n), lambda g, *_: (0, 0))]
        + [pl.BlockSpec((t // pieces, pb * ds), lambda g, *_: (0, g))] * pieces,
        [sds((t, 3 * n), BF16)] + [sds((t // pieces, d), BF16)] * pieces,
        6 * t * d * n,
        2 * (3 * d * n + t * d) + 20 * t * n,
        prefetch=1,
    )(places, u, raw, scales, inner, gains, dv, w)


def qkv_grad_kernel(n_ref, d_ref, o_ref):
    pb, _, ds, n = o_ref.shape
    grads = tn(n_ref[...], d_ref[...]).astype(BF16)
    for c in range(3):
        o_ref[:, c] = grads[:, c * n : (c + 1) * n].reshape(pb, ds, n)


def qkv_grads(normed, grad, p):
    t, d = normed.shape
    n = grad.shape[1] // 3
    ds = d // p
    pb = max(1, TILE // ds)
    return call(
        qkv_grad_kernel,
        "qkv_grad",
        (p // pb,),
        [pl.BlockSpec((t, pb * ds), lambda g: (0, g)), fixed((t, 3 * n))],
        pl.BlockSpec((pb, 3, ds, n), lambda g: (g, 0, 0, 0)),
        sds((p, 3, ds, n), BF16),
        6 * t * d * n,
        2 * (3 * d * n + t * d + 3 * t * n),
    )(normed, grad)


def swap(value, axis):
    return lax.ppermute(value, axis, [(0, 1), (1, 0)])


def spread(value):
    rows = swap(value, "row")
    return (value, swap(value, "core"), rows, swap(rows, "core"))


def across(value, k):
    size = lax.axis_size("tp")
    return lax.ppermute(value, "tp", [(i, i ^ k) for i in range(size)])


def total(pieces):
    return sum(v.astype(F32) for v in pieces)


def add(*values):
    return total(values).astype(values[0].dtype)


def cut(value, pieces):
    rows = value.shape[0] // pieces
    return [value[r * rows : (r + 1) * rows] for r in range(pieces)]


def join(*pieces):
    return jnp.concatenate(pieces, 0)


class Crossing:
    def __init__(self, first, second):
        self.one, self.two = first, second
        self.far = swap(first[3], "row"), swap(second[3], "fsdp")
        self.near = swap(first[1], "row"), swap(second[2], "fsdp")

    def half(self, line):
        sums = line(
            lambda a, b, c, d, e, f, g, h: (add(a, b), add(c, d), add(e, f), add(g, h)),
            self.one[2],
            self.far[0],
            self.two[1],
            self.far[1],
            self.one[0],
            self.near[0],
            self.two[0],
            self.near[1],
        )
        self.last = swap(sums[0], "fsdp"), swap(sums[1], "row")
        self.kept = sums[2:]

    def done(self, line):
        return line(lambda a, b, c, d: (add(a, b), add(c, d)), self.kept[0], self.last[0], self.kept[1], self.last[1])


class Line:
    def __init__(self):
        self.last = None

    def __call__(self, step, *operands):
        leaves, form = jax.tree.flatten(operands)
        spots = [i for i, v in enumerate(leaves) if isinstance(v, jax.Array)]
        if self.last is not None:
            kept, self.last = lax.optimization_barrier(([leaves[i] for i in spots], self.last))
            for i, v in zip(spots, kept):
                leaves[i] = v
        result = step(*jax.tree.unflatten(form, leaves))
        self.last = min(jax.tree.leaves(result), key=lambda v: v.size)
        return result

    def sums(self, own, core, pieces, first=None):
        mine, theirs = cut(own, pieces), cut(swap(core, "core"), pieces)
        last = across(self(add, mine[3], theirs[3]), 1)
        near = self(add, mine[2], theirs[2], last)
        beside, first = self(lambda a, b, c, d: (add(a, b), add(c, d)), mine[1], theirs[1], mine[0], theirs[0])
        return [first, across(beside, 1), across(near, 2)]


def in_place_kernel(place_ref, *refs):
    for r, piece in enumerate(refs[:-1]):

        @pl.when(pl.program_id(0) == r)
        def _():
            refs[-1][...] = piece[...]


def in_place(pieces, places):
    rows, d = pieces[0].shape
    count = len(pieces)
    return call(
        in_place_kernel,
        "inplace",
        (count,),
        [fixed((rows, d))] * count,
        pl.BlockSpec((rows, d), lambda r, place: (place[r] // rows, 0)),
        sds((rows * count, d), pieces[0].dtype),
        0,
        4 * rows * count * d,
        prefetch=1,
    )(places, *pieces)


def meet(value):
    value = value + across(value, 1)
    return value + across(value, 2)


def relative(value, places, pieces):
    rows = value.shape[0] // pieces
    return [lax.dynamic_slice_in_dim(value, places[r], rows, 0) for r in range(pieces)]


def body(
    inputs,
    prefix,
    expert_ids,
    norm_gains,
    qkv_weight,
    out_weight,
    router_weight,
    gate_up_weight,
    down_weight,
    cotangent,
    *,
    chunks,
):
    sequences, length, width = inputs.shape
    t = sequences * length
    tp = lax.axis_size("tp")
    quarter = t // tp
    column = lax.axis_index("tp")
    core = lax.axis_index("core")
    ctx = lax.axis_index("row") * 2 + core
    experts = router_weight.shape[1]
    group = experts // 2
    starts = [sum(chunks[:k]) for k in range(len(chunks))]
    x = inputs.reshape(t, width)
    places = jnp.stack([column ^ r for r in range(tp)]).astype(jnp.int32) * quarter
    x_q = lax.dynamic_slice_in_dim(x, column * quarter, quarter, 0)

    line = Line()
    attn_local = jnp.concatenate([qkv_weight, out_weight[None]], 0)
    attn_w = lax.all_gather(attn_local, PLANE, axis=0, tiled=False)
    triple = jnp.concatenate([gate_up_weight, down_weight[:, None]], 1)
    ds, f = triple.shape[2:]
    grouped = triple.reshape(2, group, 3, ds, f)
    ws = []
    for begin, e in zip(starts, chunks):
        mine = lax.all_to_all(grouped[:, begin : begin + e], "core", 0, 0, tiled=True)
        ws.append(lax.all_gather(mine, FR, axis=0, tiled=False).reshape(-1, e, 3, ds, f))
    gains_low = lax.all_gather(norm_gains, PLANE, axis=1, tiled=True)
    router = lax.all_gather(router_weight, PLANE, axis=0, tiled=True)
    cots = relative(cotangent.reshape(t, width), places, tp)
    c0 = join(*cots)
    c1 = swap(c0, "core")
    attn_w, gains_low, router, c0 = lax.optimization_barrier((attn_w, gains_low, router, c0))
    p = attn_w.shape[0]

    gains = gains_low.astype(F32)
    n = attn_w.shape[3]
    router_rows = jnp.concatenate([router.T, jnp.zeros((128 - experts, width), BF16)], 0)

    own_gains = lax.dynamic_slice_in_dim(gains[2:4], column * n, n, 1)[:, None, :]
    halves = jnp.arange(0, HEAD_DIM, 2).astype(F32) / HEAD_DIM
    inverse = 1.0 / THETA**halves
    positions = ctx * length + jnp.arange(length, dtype=jnp.int32)
    angles = positions.astype(F32)[:, None] * inverse[None, :]
    cosine = jnp.concatenate([jnp.cos(angles)] * 2, 1)
    sine = jnp.concatenate([-jnp.sin(angles), jnp.sin(angles)], 1)
    offsets = jnp.stack([ctx, ctx ^ 1, ctx ^ 2, ctx ^ 3, ctx]).astype(jnp.int32) * length
    scal = jnp.concatenate([offsets, prefix.astype(jnp.int32)])
    ids_q = lax.dynamic_slice_in_dim(expert_ids.reshape(t, -1), column * quarter, quarter, 0)
    normed_one, raw, values, squares = line(qkv_project, x, gains[0:1], attn_w)
    v_blocks = spread(values)
    scales = lax.rsqrt(meet(squares[:, :, 0]) / width + EPSILON)[:, :, None]
    queries, keys = line(prepare, raw, scales, own_gains, cosine, sine)
    k_blocks = spread(keys)
    blocks = k_blocks + v_blocks
    heads = line(attend, scal, queries, blocks, length)
    sums = line(project_out, places, heads, attn_w, tp)
    near = line(add, sums[2], across(sums[3], 1))
    sums = [sums[0], across(sums[1], 1), across(near, 2)]
    mid, ext, probs, chosen = line(norm_two, x_q, sums, gains[1:2], router_rows, ids_q, experts)
    far = across(ext, 2)
    near = across(ext, 1)
    x0 = line(join, ext, near, far, across(far, 1))
    x1 = swap(x0, "core")

    xs, cs = [x0, x1], [c0, c1]
    blocks_in = jnp.arange(width // TILE, dtype=jnp.int32)
    square = lax.axis_size("fsdp") == 2 and lax.axis_size("row") == 2
    chip = lax.axis_index("fsdp") * 2 + lax.axis_index("row")
    by_chip = blocks_in
    if square:
        share = width // TILE // 8
        chips, cores, inner = jnp.meshgrid(jnp.arange(4), jnp.arange(2), jnp.arange(share), indexing="ij")
        by_chip = (((chips ^ chip) * 2 + cores) * share + inner).reshape(-1).astype(jnp.int32)
    hid, dgu, side, grads = [], [], [], []
    dx = []

    def up(k):
        first = (core * group + starts[k]).astype(jnp.int32)[None]
        for kept, made in zip((hid, dgu, side), line(expert_up, first, xs, cs, ws[k])):
            kept.append(made)

    def back(k, before):
        gates = side if k == len(chunks) - 1 else []
        return line(expert_down, [dgu[k]], [ws[k]], 0, 2, gates, before, 2, "expert_dx")

    def weight_grad(k, relative_chips):
        sides = 4 if relative_chips else 1
        columns = by_chip if relative_chips else blocks_in
        made = line(expert_grads, columns, xs, cs, [hid[k]], [dgu[k]], p, chunks[k], sides)
        if relative_chips:
            return made
        made = made[0].reshape(-1, 2, chunks[k], 3, ds, f)
        return lax.optimization_barrier(lax.psum_scatter(made, FR, scatter_dimension=0, tiled=False))

    for k in range(len(chunks)):
        up(k)
        dx = back(k, dx)
        if k < len(chunks) - 1:
            grads.append(weight_grad(k, False))
    d_normed = line.sums(*dx, tp)
    moe = line(expert_down, hid, ws, 2, 1, [], [], 2, "expert_out")
    tail = weight_grad(len(chunks) - 1, square)
    if square:
        middle = chunks[-1] // 2
        tail = Crossing([v[:, :middle] for v in tail], [v[:, middle:] for v in tail])

    d_mid, d_mid_low, gain_two, grad_router = line(
        norm_two_back, d_normed, mid, ext, probs, chosen, cots[0], gains[1:2], router_rows
    )
    far = across(d_mid_low, 2)
    near = across(d_mid_low, 1)
    d_mid_low = line(join, d_mid_low, near, far, across(far, 1))
    own, beside = cut(moe[0], tp), cut(swap(moe[1], "core"), tp)
    last = across(line(add, own[3], beside[3]), 1)

    d_heads = line(heads_grad, places, d_mid_low, attn_w, tp)
    near = line(add, own[2], beside[2], last)
    next_one = line(add, own[1], beside[1])
    moe = [across(next_one, 1), across(near, 2)]
    dq, b0, b1, b2, b3 = line(attend_back, scal, queries, blocks, d_heads, length)
    r1 = swap(b1, "core")
    r2 = swap(line(add, b2, swap(b3, "core")), "row")
    out = line(lambda *v: total(v).astype(BF16), mid, own[0], beside[0], *moe)
    out_far = across(out, 2)
    out_near = across(out, 1)
    grad_out = line(out_weight_grad, places, d_mid_low, heads, p, tp)
    d_kv = line(lambda *v: total(v), b0, r1, r2)
    u, inner, gain_qk = line(unturn, dq, d_kv[0], raw, scales, own_gains, cosine, sine)
    grad_out, grads[0], u = lax.optimization_barrier((grad_out, grads[0], u))
    grad_out = lax.psum_scatter(grad_out, PLANE, scatter_dimension=0, tiled=False)
    if square:
        tail.half(line)

    def parted(k):
        own, other = line(
            lambda v: [lax.dynamic_index_in_dim(v, c, 0, keepdims=False) for c in (core, core ^ 1)], grads[k]
        )
        return own, swap(other, "core")

    def settled(k, pair, kept):
        steps = jnp.arange(chunks[k] // 2, dtype=jnp.int32)
        spots = jnp.concatenate([(c * group + starts[k]) // 2 + steps for c in (core, core ^ 1)])
        return line(settle, spots.astype(jnp.int32), pair, kept, experts)

    pairs = [parted(0)]
    inner = (meet(inner[:, :, 0]) / width)[:, :, None]
    out_both = across(out_far, 1)
    outputs = line(in_place, [out, out_near, out_far, out_both], places).reshape(inputs.shape)
    d_raw, *d_one = line(
        raw_back, places, u, raw, scales, inner, own_gains, d_kv[1].astype(BF16), attn_w, tp
    )
    last = across(d_one[3], 1)
    near = line(add, d_one[2], last)
    d_one = [d_one[0], across(d_one[1], 1), across(near, 2)]
    grad_qkv = line(qkv_grads, normed_one, d_raw, p)
    grad_in, gain_one = line(norm_one_back, d_one, x_q, d_mid, gains[0:1])
    far = across(grad_in, 2)
    near = across(grad_in, 1)
    grad_qkv, gain_one = lax.optimization_barrier((grad_qkv, gain_one))
    grad_qkv = lax.psum_scatter(grad_qkv, PLANE, scatter_dimension=0, tiled=False)
    placed = lax.dynamic_update_slice_in_dim(
        jnp.zeros((2, width), F32), gain_qk[:, 0, :], column * n, 1
    )

    small = line(lambda *v: jnp.concatenate(v, 0), grad_router[:experts], gain_one, gain_two, placed)
    rows = small.shape[0]
    small = small.reshape(rows, p, ds).transpose(1, 0, 2)
    small = jnp.sum(lax.all_to_all(small, PLANE, 0, 0, tiled=True), 0)
    other = across(small, 1)
    both = across(far, 1)
    kept = settled(0, pairs[0], [])
    grads.append(jnp.concatenate(tail.done(line), 1) if square else tail)
    pairs.append(parted(1))
    owned_gate_up, owned_down = settled(1, pairs[1], kept)
    small = line(lambda a, b: a + b, small, other)
    other = across(small, 2)
    grad_inputs = line(in_place, [grad_in, near, far, both], places).reshape(inputs.shape)
    small = line(lambda a, b: a + b, small, other)
    owned_gains = small[experts:]
    owned_router = small[:experts].T
    return (
        outputs,
        grad_inputs,
        owned_gains,
        grad_qkv.astype(F32),
        grad_out.astype(F32),
        owned_router,
        owned_gate_up,
        owned_down,
    )


def solution(mesh):
    fsdp, ctx, tp = (mesh.shape[a] for a in ("fsdp", "ctx", "tp"))
    fine = Mesh(mesh.devices.reshape(fsdp, ctx // 2, 2, tp), EVERY)
    tokens = P("fsdp", ("row", "core"), None)
    weights = (
        P(None, PLANE),
        P(None, PLANE, "tp"),
        P(PLANE, "tp"),
        P(PLANE, None),
        P(None, None, PLANE, "tp"),
        P(None, PLANE, "tp"),
    )
    return jax.shard_map(
        functools.partial(body, chunks=(6, 2)),
        mesh=fine,
        in_specs=(tokens, P("fsdp"), tokens) + weights + (tokens,),
        out_specs=(tokens, tokens) + weights,
        check_vma=False,
    )
```

```python
import functools

import jax
import jax.numpy as jnp
from jax import lax
from jax.experimental import pallas as pl
from jax.experimental.pallas import tpu as pltpu
from jax.sharding import Mesh, PartitionSpec as P

HEAD_DIM = 128
EPSILON = 1e-05
THETA = 10000.0
TILE = 256
F32 = jnp.float32
BF16 = jnp.bfloat16
FR = ("fsdp", "row")
LANES = 128
PLANE = ("fsdp", "row", "core")
EVERY = ("fsdp", "row", "core", "tp")


def nn(a, b):
    return lax.dot_general(a, b, (((1,), (0,)), ((), ())), preferred_element_type=F32)


def nt(a, b):
    return lax.dot_general(a, b, (((1,), (1,)), ((), ())), preferred_element_type=F32)


def tn(a, b):
    return lax.dot_general(a, b, (((0,), (0,)), ((), ())), preferred_element_type=F32)


def call(kernel, name, grid, in_specs, out_specs, out_shape, flops, moved, scratch=(), prefetch=0, limit=56, aliases=None):
    return pl.pallas_call(
        kernel,
        name=name,
        out_shape=out_shape,
        grid_spec=pltpu.PrefetchScalarGridSpec(
            num_scalar_prefetch=prefetch,
            grid=grid,
            in_specs=in_specs,
            out_specs=out_specs,
            scratch_shapes=list(scratch),
        ),
        input_output_aliases=aliases or {},
        compiler_params=pltpu.CompilerParams(
            dimension_semantics=("arbitrary",) * len(grid), vmem_limit_bytes=limit << 20
        ),
        cost_estimate=pl.CostEstimate(flops=int(flops), bytes_accessed=int(moved), transcendentals=0),
    )


def fixed(shape):
    return pl.BlockSpec(shape, lambda *a: (0,) * len(shape), pipeline_mode=pl.Buffered(1))


def sds(shape, dtype):
    return jax.ShapeDtypeStruct(shape, dtype)


def qkv_kernel(x_ref, g_ref, w_ref, n_ref, raw_ref, v_ref, sq_ref):
    c = pl.program_id(0)

    @pl.when(c == 0)
    def _():
        x = x_ref[...].astype(F32)
        r = lax.rsqrt(jnp.mean(x * x, -1, keepdims=True) + EPSILON)
        n_ref[...] = (x * r * g_ref[...]).astype(BF16)

    w = w_ref[...]
    y = nn(n_ref[...], w.reshape(w.shape[0] * w.shape[2], w.shape[3]))

    @pl.when(c < 2)
    def _():
        raw_ref[0] = y
        sq_ref[0] = jnp.broadcast_to(jnp.sum(y * y, -1, keepdims=True), sq_ref.shape[1:])

    @pl.when(c == 2)
    def _():
        v_ref[...] = y.astype(BF16)


def qkv_project(x, gain, w):
    t, d = x.shape
    p, _, ds, n = w.shape
    return call(
        qkv_kernel,
        "qkv",
        (3,),
        [
            fixed((t, d)),
            fixed((1, d)),
            pl.BlockSpec((p, 1, ds, n), lambda c: (0, c, 0, 0)),
        ],
        [
            pl.BlockSpec((t, d), lambda c: (0, 0)),
            pl.BlockSpec((1, t, n), lambda c: (jnp.minimum(c, 1), 0, 0)),
            pl.BlockSpec((t, n), lambda c: (0, 0)),
            pl.BlockSpec((1, t, 128), lambda c: (jnp.minimum(c, 1), 0, 0)),
        ],
        [sds((t, d), BF16), sds((2, t, n), F32), sds((t, n), BF16), sds((2, t, 128), F32)],
        6 * t * d * n,
        2 * (3 * d * n + 2 * t * d) + 10 * t * n,
    )(x, gain, w)


def turn(v, cosine, sine):
    half = v.shape[-1] // 2
    return v * cosine + pltpu.roll(v, half, 1) * sine


def prep_kernel(raw_ref, s_ref, g_ref, cos_ref, sin_ref, q_ref, k_ref):
    reps = raw_ref.shape[1] // cos_ref.shape[0]
    cosine = jnp.concatenate([cos_ref[...]] * reps, 0)
    sine = jnp.concatenate([sin_ref[...]] * reps, 0)
    q = raw_ref[0] * s_ref[0] * g_ref[0]
    k = raw_ref[1] * s_ref[1] * g_ref[1]
    q_ref[...] = turn(q, cosine, sine).astype(BF16)
    k_ref[...] = turn(k, cosine, sine).astype(BF16)


def prepare(raw, scales, gains, cosine, sine):
    _, t, n = raw.shape
    h = HEAD_DIM
    length = cosine.shape[0]
    return call(
        prep_kernel,
        "prep",
        (n // h,),
        [
            pl.BlockSpec((2, t, h), lambda i: (0, 0, i)),
            fixed((2, t, 1)),
            pl.BlockSpec((2, 1, h), lambda i: (0, 0, i)),
            fixed((length, h)),
            fixed((length, h)),
        ],
        [pl.BlockSpec((t, h), lambda i: (0, i))] * 2,
        [sds((t, n), BF16)] * 2,
        20 * t * n,
        12 * t * n,
    )(raw, scales, gains, cosine, sine)


def masked_probs(s, scal_ref, q, ks):
    length = q.shape[0]
    prefix = scal_ref[5 + s]
    rows = lax.broadcasted_iota(jnp.int32, (length, length), 0) + scal_ref[4]
    columns = lax.broadcasted_iota(jnp.int32, (length, length), 1)
    pieces = []
    for b, k in enumerate(ks):
        place = columns + scal_ref[b]
        visible = (place <= rows) | (place < prefix)
        pieces.append(jnp.where(visible, nt(q, k) * HEAD_DIM ** (-0.5), -1e30))
    scores = jnp.concatenate(pieces, 1)
    expo = jnp.exp(scores - jnp.max(scores, -1, keepdims=True))
    return expo / jnp.sum(expo, -1, keepdims=True)


def attend_kernel(scal_ref, q_ref, *refs):
    o_ref = refs[8]
    probs = masked_probs(pl.program_id(0), scal_ref, q_ref[...], [r[...] for r in refs[:4]])
    v = jnp.concatenate([r[...] for r in refs[4:8]], 0)
    o_ref[...] = nn(probs.astype(BF16), v).astype(BF16)


def attend(scal, q, blocks, length):
    t, n = q.shape
    h = HEAD_DIM
    one = pl.BlockSpec((length, h), lambda s, i, *_: (s, i))
    return call(
        attend_kernel,
        "attend",
        (t // length, n // h),
        [one] * 9,
        one,
        sds((t, n), BF16),
        16 * t * n * length,
        24 * t * n,
        prefetch=1,
    )(scal, q, *blocks)


def attend_back_kernel(scal_ref, q_ref, *refs):
    g_ref, dq_ref, outs = refs[8], refs[9], refs[10:]
    length = q_ref.shape[0]
    q = q_ref[...]
    grad = g_ref[...]
    probs = masked_probs(pl.program_id(0), scal_ref, q, [r[...] for r in refs[:4]])
    k = jnp.concatenate([r[...] for r in refs[:4]], 0)
    v = jnp.concatenate([r[...] for r in refs[4:8]], 0)
    d_probs = nt(grad, v)
    inner = jnp.sum(probs * d_probs, -1, keepdims=True)
    d_scores = (probs * (d_probs - inner)).astype(BF16)
    scale = HEAD_DIM ** (-0.5)
    dq_ref[...] = nn(d_scores, k) * scale
    dk = (tn(d_scores, q) * scale).astype(BF16)
    dv = tn(probs.astype(BF16), grad).astype(BF16)
    for b, o in enumerate(outs):
        o[0] = dk[b * length : (b + 1) * length]
        o[1] = dv[b * length : (b + 1) * length]


def attend_back(scal, q, blocks, grad, length):
    t, n = q.shape
    h = HEAD_DIM
    one = pl.BlockSpec((length, h), lambda s, i, *_: (s, i))
    two = pl.BlockSpec((2, length, h), lambda s, i, *_: (0, s, i))
    return call(
        attend_back_kernel,
        "attend_back",
        (t // length, n // h),
        [one] * 10,
        [one] + [two] * 4,
        [sds((t, n), F32)] + [sds((2, t, n), BF16)] * 4,
        40 * t * n * length,
        48 * t * n,
        prefetch=1,
    )(scal, q, *blocks, grad)


def out_kernel(place_ref, h_ref, w_ref, *outs):
    w = w_ref[...]
    w = w.reshape(-1, w.shape[-1])
    rows = outs[0].shape[0]
    heads = jnp.concatenate(
        [h_ref[pl.ds(pl.multiple_of(place_ref[r], rows), rows), :] for r in range(len(outs))], 0
    )
    y = nt(heads, w).astype(BF16)
    for r, o in enumerate(outs):
        o[...] = y[r * rows : (r + 1) * rows]


def project_out(places, heads, w, pieces):
    t, n = heads.shape
    p, _, ds, _ = w.shape
    pb = max(1, 2 * TILE // ds)
    return call(
        out_kernel,
        "outproj",
        (p // pb,),
        [fixed((t, n)), pl.BlockSpec((pb, 1, ds, n), lambda g, *_: (g, 3, 0, 0))],
        [pl.BlockSpec((t // pieces, pb * ds), lambda g, *_: (0, g))] * pieces,
        [sds((t // pieces, p * ds), BF16)] * pieces,
        2 * t * n * p * ds,
        2 * (t * n + n * p * ds + t * p * ds),
        prefetch=1,
    )(places, heads, w)


def d_heads_kernel(place_ref, g_ref, w_ref, o_ref, *, pieces):
    w = w_ref[...]
    y = nn(g_ref[...], w.reshape(w.shape[0] * w.shape[2], w.shape[3])).astype(BF16)
    rows = y.shape[0] // pieces
    for r in range(pieces):
        o_ref[pl.ds(pl.multiple_of(place_ref[r], rows), rows), :] = y[r * rows : (r + 1) * rows]


def heads_grad(places, grad, w, pieces):
    t, d = grad.shape
    p, _, ds, n = w.shape
    return call(
        functools.partial(d_heads_kernel, pieces=pieces),
        "dheads",
        (1,),
        [fixed((t, d)), pl.BlockSpec((p, 1, ds, n), lambda g, *_: (0, 3, 0, 0), pipeline_mode=pl.Buffered(1))],
        fixed((t, n)),
        sds((t, n), BF16),
        2 * t * n * d,
        2 * (t * n + n * d + t * d),
        prefetch=1,
    )(places, grad, w)


def grad_out_kernel(place_ref, g_ref, h_ref, o_ref, *, pieces):
    rows = g_ref.shape[0] // pieces
    heads = jnp.concatenate(
        [h_ref[pl.ds(pl.multiple_of(place_ref[r], rows), rows), :] for r in range(pieces)], 0
    )
    o_ref[...] = tn(g_ref[...], heads).astype(BF16).reshape(o_ref.shape)


def out_weight_grad(places, grad, heads, p, pieces):
    t, d = grad.shape
    n = heads.shape[1]
    ds = d // p
    pb = max(1, TILE // ds)
    return call(
        functools.partial(grad_out_kernel, pieces=pieces),
        "gradout",
        (p // pb,),
        [pl.BlockSpec((t, pb * ds), lambda g, *_: (0, g)), fixed((t, n))],
        pl.BlockSpec((pb, 1, ds, n), lambda g, *_: (g, 3, 0, 0)),
        sds((p, 4, ds, n), BF16),
        2 * t * n * d,
        2 * (t * n + n * d + t * d),
        prefetch=1,
    )(places, grad, heads)


def norm_two_kernel(x_ref, a_ref, b_ref, c_ref, g_ref, w_ref, ids_ref, mid_ref, ext_ref, probs_ref, chosen_ref, *, experts):
    mid = x_ref[...].astype(F32) + a_ref[...].astype(F32) + b_ref[...].astype(F32) + c_ref[...].astype(F32)
    mid_ref[...] = mid
    d = mid.shape[1]
    r = lax.rsqrt(jnp.mean(mid * mid, -1, keepdims=True) + EPSILON)
    low = (mid * r * g_ref[...]).astype(BF16)
    ext_ref[:, :d] = low
    logits = nt(low, w_ref[...])
    lane = lax.broadcasted_iota(jnp.int32, logits.shape, 1)
    logits = jnp.where(lane < experts, logits, -1e30)
    expo = jnp.exp(logits - jnp.max(logits, -1, keepdims=True))
    probs = expo / jnp.sum(expo, -1, keepdims=True)
    chosen = jnp.zeros_like(probs)
    for j in range(ids_ref.shape[1]):
        chosen += (ids_ref[:, j : j + 1] == lane).astype(F32)
    probs_ref[...] = probs
    chosen_ref[...] = chosen
    gates = probs * chosen
    high = gates.astype(BF16)
    rest = (gates - high.astype(F32)).astype(BF16)
    ext_ref[:, d:] = jnp.concatenate([high[:, : LANES // 2], rest[:, : LANES // 2]], 1)


def norm_two(x, sums, gain, router, ids, experts):
    t, d = x.shape
    return call(
        functools.partial(norm_two_kernel, experts=experts),
        "norm_two",
        (1,),
        [fixed((t, d))] * 4 + [fixed((1, d)), fixed(router.shape), fixed(ids.shape)],
        [fixed((t, d)), fixed((t, d + LANES)), fixed((t, LANES)), fixed((t, LANES))],
        [sds((t, d), F32), sds((t, d + LANES), BF16), sds((t, LANES), F32), sds((t, LANES), F32)],
        2 * t * d * LANES,
        14 * t * d,
    )(x, *sums, gain, router, ids)


def norm_two_back_kernel(a_ref, b_ref, c_ref, mid_ref, ext_ref, probs_ref, chosen_ref, cot_ref, g_ref, w_ref, *outs):
    mid_grad_ref, low_ref, gain_ref, router_ref = outs
    d = mid_ref.shape[1]
    du = a_ref[...].astype(F32) + b_ref[...].astype(F32) + c_ref[...].astype(F32)
    probs = probs_ref[...]
    masked = du[:, d:] * chosen_ref[...]
    d_logits = (probs * (masked - jnp.sum(probs * masked, -1, keepdims=True))).astype(BF16)
    router_ref[...] = tn(d_logits, ext_ref[:, :d])
    u = du[:, :d] + nn(d_logits, w_ref[...])
    mid = mid_ref[...]
    r = lax.rsqrt(jnp.mean(mid * mid, -1, keepdims=True) + EPSILON)
    hat = mid * r
    gain_ref[...] = jnp.sum(u * hat, 0, keepdims=True)
    w = u * g_ref[...]
    grad = cot_ref[...].astype(F32) + r * (w - hat * jnp.mean(w * hat, -1, keepdims=True))
    mid_grad_ref[...] = grad
    low_ref[...] = grad.astype(BF16)


def norm_two_back(sums, mid, ext, probs, chosen, cot, gain, router):
    t, d = mid.shape
    wide = fixed((t, d + LANES))
    return call(
        norm_two_back_kernel,
        "norm_two_back",
        (1,),
        [wide] * 3
        + [fixed((t, d)), wide, fixed((t, LANES)), fixed((t, LANES)), fixed((t, d)), fixed((1, d)), fixed(router.shape)],
        [fixed((t, d)), fixed((t, d)), fixed((1, d)), fixed((LANES, d))],
        [sds((t, d), F32), sds((t, d), BF16), sds((1, d), F32), sds((LANES, d), F32)],
        4 * t * d * LANES,
        20 * t * d,
    )(*sums, mid, ext, probs, chosen, cot, gain, router)


def norm_one_back_kernel(a_ref, b_ref, c_ref, x_ref, mid_grad_ref, g_ref, o_ref, gain_ref):
    u = a_ref[...].astype(F32) + b_ref[...].astype(F32) + c_ref[...].astype(F32)
    x = x_ref[...].astype(F32)
    r = lax.rsqrt(jnp.mean(x * x, -1, keepdims=True) + EPSILON)
    hat = x * r
    gain_ref[...] = jnp.sum(u * hat, 0, keepdims=True)
    w = u * g_ref[...]
    o_ref[...] = (mid_grad_ref[...] + r * (w - hat * jnp.mean(w * hat, -1, keepdims=True))).astype(BF16)


def norm_one_back(sums, x, mid_grad, gain):
    t, d = x.shape
    return call(
        norm_one_back_kernel,
        "norm_one_back",
        (1,),
        [fixed((t, d))] * 5 + [fixed((1, d))],
        [fixed((t, d)), fixed((1, d))],
        [sds((t, d), BF16), sds((1, d), F32)],
        20 * t * d,
        14 * t * d,
    )(*sums, x, mid_grad, gain)


def expert_kernel(first_ref, *refs, parts):
    xs, cs, w_ref = refs[:parts], refs[parts : 2 * parts], refs[2 * parts]
    hid_ref, dgu_ref, dg_ref = refs[2 * parts + 1 :]
    e = pl.program_id(0)
    t = cs[0].shape[0]
    d = cs[0].shape[1]

    @pl.when(e == 0)
    def _():
        dg_ref[...] = jnp.zeros_like(dg_ref)

    f = w_ref.shape[4]
    me = first_ref[0] + e
    lane = lax.broadcasted_iota(jnp.int32, (t, LANES), 1)
    for part, (x_ref, c_ref) in enumerate(zip(xs, cs)):

        def block(x_ref=x_ref, c_ref=c_ref, to=slice(part * t, (part + 1) * t)):
            x = x_ref[:, :d]
            a = nn(x, w_ref[:, 0, 0].reshape(d, f))
            b = nn(x, w_ref[:, 0, 1].reshape(d, f))
            dh = nn(c_ref[...], w_ref[:, 0, 2].reshape(d, f))
            mine = (lane == me) | (lane == me + LANES // 2)
            gate = jnp.sum(jnp.where(mine, x_ref[:, d:].astype(F32), 0.0), -1, keepdims=True)
            sigma = jax.nn.sigmoid(a)
            swish = a * sigma
            act = swish * b
            hid_ref[to, :] = (gate * act).astype(BF16)
            d_gate = jnp.sum(dh * act, -1, keepdims=True)
            dg_ref[to, :] += jnp.where(lane == me, d_gate, 0.0)
            inner = dh * gate
            dgu_ref[to, :f] = (inner * b * sigma * (1.0 + a * (1.0 - sigma))).astype(BF16)
            dgu_ref[to, f:] = (inner * swish).astype(BF16)

        block()


def expert_up(first, xs, cs, w):
    t, d = cs[0].shape
    parts = len(cs)
    p, e, _, ds, f = w.shape
    every = parts * t
    return call(
        functools.partial(expert_kernel, parts=parts),
        "expert_up",
        (e,),
        [fixed(x.shape) for x in xs]
        + [fixed((t, d))] * parts
        + [pl.BlockSpec((p, 1, 3, ds, f), lambda i, *_: (0, i, 0, 0, 0))],
        [
            pl.BlockSpec((every, f), lambda i, *_: (0, i)),
            pl.BlockSpec((every, 2 * f), lambda i, *_: (0, i)),
            pl.BlockSpec((every, LANES), lambda i, *_: (0, 0)),
        ],
        [sds((every, e * f), BF16), sds((every, e * 2 * f), BF16), sds((every, LANES), F32)],
        6 * every * d * f * e,
        2 * (3 * d * f * e + 2 * every * d + 3 * every * f * e),
        prefetch=1,
    )(first, *xs, *cs, w)


def expert_grad_kernel(*refs, parts):
    xs, cs, hid_ref, dgu_ref, o_ref = refs[:parts], refs[parts : 2 * parts], *refs[2 * parts :]
    pb, e, _, ds, f = o_ref.shape
    x = jnp.concatenate([r[...] for r in xs], 0)
    c = jnp.concatenate([r[...] for r in cs], 0)
    both = tn(x, dgu_ref[...]).astype(BF16)
    down = tn(c, hid_ref[...]).astype(BF16)
    for i in range(e):
        o_ref[:, i, 0] = both[:, 2 * i * f : (2 * i + 1) * f].reshape(pb, ds, f)
        o_ref[:, i, 1] = both[:, (2 * i + 1) * f : (2 * i + 2) * f].reshape(pb, ds, f)
        o_ref[:, i, 2] = down[:, i * f : (i + 1) * f].reshape(pb, ds, f)


def expert_grads(xs, cs, hid, dgu, p, e):
    t, d = cs[0].shape
    parts = len(cs)
    ds = d // p
    f = hid.shape[1] // e
    pb = max(1, TILE // ds)
    column = pl.BlockSpec((t, pb * ds), lambda g: (0, g))
    return call(
        functools.partial(expert_grad_kernel, parts=parts),
        "expert_grad",
        (p // pb,),
        [column] * (2 * parts) + [fixed(hid.shape), fixed(dgu.shape)],
        pl.BlockSpec((pb, e, 3, ds, f), lambda g: (g, 0, 0, 0, 0)),
        sds((p, e, 3, ds, f), BF16),
        6 * parts * t * d * f * e,
        2 * (3 * d * f * e + 2 * parts * t * d + 3 * parts * t * f * e),
    )(*xs, *cs, hid, dgu)


def settle_kernel(spot_ref, *refs, pieces):
    gate_up_ref, down_ref = refs[-2:]
    each = pl.num_programs(0) // pieces
    for r in range(pieces):

        @pl.when(pl.program_id(0) // each == r)
        def _():
            gate_up_ref[...] = refs[r][:, :2].astype(F32)
            down_ref[...] = refs[r][:, 2].astype(F32)


def settle(spots, pieces, kept, experts):
    e, _, ds, f = pieces[0].shape
    count = len(pieces)
    each = e // 2

    def piece(r):
        return pl.BlockSpec((2, 3, ds, f), lambda g, spot: (jnp.clip(g - r * each, 0, each - 1), 0, 0, 0))

    return call(
        functools.partial(settle_kernel, pieces=count),
        "settle",
        (count * each,),
        [piece(r) for r in range(count)] + [pl.BlockSpec(memory_space=pl.ANY)] * len(kept),
        [
            pl.BlockSpec((2, 2, ds, f), lambda g, spot: (spot[g], 0, 0, 0)),
            pl.BlockSpec((2, ds, f), lambda g, spot: (spot[g], 0, 0)),
        ],
        [sds((experts, 2, ds, f), F32), sds((experts, ds, f), F32)],
        0,
        18 * count * e * ds * f,
        prefetch=1,
        aliases={1 + count + i: i for i in range(len(kept))},
    )(spots, *pieces, *kept)


def down_kernel(*refs, planes, chunks, sides, begun):
    acts, ws = refs[:chunks], refs[chunks : 2 * chunks]
    gates = refs[2 * chunks : 2 * chunks + sides]
    before = refs[2 * chunks + sides : 2 * chunks + sides + begun]
    outs = refs[2 * chunks + sides + begun :]
    g = pl.program_id(0)
    pb, _, _, ds, f = ws[0].shape
    wide = pb * ds
    rows = outs[0].shape[0]
    joined = [
        jnp.concatenate([w[:, i, c].reshape(wide, f) for i in range(w.shape[1]) for c in range(planes)], 1)
        for w in ws
    ]
    to = pl.ds(pl.multiple_of(g * wide, wide), wide)
    for part, o in enumerate(outs):
        own = slice(part * rows, (part + 1) * rows)
        value = sum(nt(a[own, :], w) for a, w in zip(acts, joined))
        if begun:
            value += before[part][...].astype(F32)
        o[:, to] = value.astype(BF16)
    if sides:

        @pl.when(g == 0)
        def _():
            for part, o in enumerate(outs):
                own = slice(part * rows, (part + 1) * rows)
                o[:, o.shape[1] - LANES :] = sum(s[own, :] for s in gates).astype(BF16)


def expert_down(acts, ws, plane, planes, gates, before, parts, name):
    every = acts[0].shape[0]
    p, _, _, ds, f = ws[0].shape
    k = sum(a.shape[1] for a in acts)
    t = every // parts
    chunks = len(acts)
    d = p * ds + (LANES if gates else 0)
    pb = max(1, 2 * TILE // ds)
    return call(
        functools.partial(down_kernel, planes=planes, chunks=chunks, sides=len(gates), begun=len(before)),
        name,
        (p // pb,),
        [fixed(a.shape) for a in acts]
        + [pl.BlockSpec((pb, w.shape[1], planes, ds, f), lambda g: (g, 0, plane, 0, 0)) for w in ws]
        + [fixed((every, LANES))] * len(gates)
        + [pl.BlockSpec((t, pb * ds), lambda g: (0, g))] * len(before),
        [pl.BlockSpec((t, d), lambda g: (0, 0))] * parts,
        [sds((t, d), BF16)] * parts,
        2 * every * k * p * ds,
        2 * (every * k + k * p * ds) + 2 * every * d,
    )(*acts, *ws, *gates, *before)


def unturn_kernel(dq_ref, dk_ref, raw_ref, s_ref, g_ref, cos_ref, sin_ref, u_ref, in_ref, gg_ref):
    h = pl.program_id(0)
    reps = raw_ref.shape[1] // cos_ref.shape[0]
    cosine = jnp.concatenate([cos_ref[...]] * reps, 0)
    sine = jnp.concatenate([sin_ref[...]] * reps, 0)
    for i, grad in enumerate((dq_ref[...], dk_ref[...])):
        u = turn(grad, cosine, -sine)
        hat = raw_ref[i] * s_ref[i]
        product = u * hat
        u_ref[i] = u
        gg_ref[i] = jnp.sum(product, 0, keepdims=True)
        row = jnp.broadcast_to(jnp.sum(product * g_ref[i], -1, keepdims=True), in_ref.shape[1:])

        @pl.when(h == 0)
        def _():
            in_ref[i] = row

        @pl.when(h != 0)
        def _():
            in_ref[i] += row


def unturn(dq, dk, raw, scales, gains, cosine, sine):
    _, t, n = raw.shape
    h = HEAD_DIM
    length = cosine.shape[0]
    column = pl.BlockSpec((t, h), lambda i: (0, i))
    pair = pl.BlockSpec((2, t, h), lambda i: (0, 0, i))
    return call(
        unturn_kernel,
        "unturn",
        (n // h,),
        [
            column,
            column,
            pair,
            fixed((2, t, 1)),
            pl.BlockSpec((2, 1, h), lambda i: (0, 0, i)),
            fixed((length, h)),
            fixed((length, h)),
        ],
        [
            pair,
            pl.BlockSpec((2, t, 128), lambda i: (0, 0, 0)),
            pl.BlockSpec((2, 1, h), lambda i: (0, 0, i)),
        ],
        [sds((2, t, n), F32), sds((2, t, 128), F32), sds((2, 1, n), F32)],
        30 * t * n,
        24 * t * n,
    )(dq, dk, raw, scales, gains, cosine, sine)


def raw_back_kernel(place_ref, u_ref, raw_ref, s_ref, in_ref, g_ref, dv_ref, w_ref, d_ref, *outs):
    t, n = dv_ref.shape

    @pl.when(pl.program_id(0) == 0)
    def _():
        for i in range(2):
            hat = raw_ref[i] * s_ref[i]
            d_ref[:, i * n : (i + 1) * n] = (
                s_ref[i] * (u_ref[i] * g_ref[i] - hat * in_ref[i])
            ).astype(BF16)
        d_ref[:, 2 * n :] = dv_ref[...]

    pb, _, ds, _ = w_ref.shape
    w = jnp.concatenate([w_ref[:, c].reshape(pb * ds, n) for c in range(3)], 1)
    y = nt(d_ref[...], w).astype(BF16)
    rows = outs[0].shape[0]
    outs[0][...] = y[:rows]
    for r, o in enumerate(outs):
        for q in range(len(outs)):

            @pl.when(place_ref[r] == q * rows)
            def _():
                o[...] = y[q * rows : (q + 1) * rows]


def raw_back(places, u, raw, scales, inner, gains, dv, w, pieces):
    t, n = dv.shape
    p, _, ds, _ = w.shape
    d = p * ds
    pb = max(1, 2 * TILE // ds)
    return call(
        raw_back_kernel,
        "raw_back",
        (p // pb,),
        [
            fixed((2, t, n)),
            fixed((2, t, n)),
            fixed((2, t, 1)),
            fixed((2, t, 1)),
            fixed((2, 1, n)),
            fixed((t, n)),
            pl.BlockSpec((pb, 3, ds, n), lambda g, *_: (g, 0, 0, 0)),
        ],
        [pl.BlockSpec((t, 3 * n), lambda g, *_: (0, 0))]
        + [pl.BlockSpec((t // pieces, pb * ds), lambda g, *_: (0, g))] * pieces,
        [sds((t, 3 * n), BF16)] + [sds((t // pieces, d), BF16)] * pieces,
        6 * t * d * n,
        2 * (3 * d * n + t * d) + 20 * t * n,
        prefetch=1,
    )(places, u, raw, scales, inner, gains, dv, w)


def qkv_grad_kernel(n_ref, d_ref, kept_ref, o_ref):
    pb, _, ds, n = o_ref.shape
    grads = tn(n_ref[...], d_ref[...]).astype(BF16)
    for c in range(3):
        o_ref[:, c] = grads[:, c * n : (c + 1) * n].reshape(pb, ds, n)


def qkv_grads(normed, grad, kept, p):
    t, d = normed.shape
    n = grad.shape[1] // 3
    ds = d // p
    pb = max(1, TILE // ds)
    return call(
        qkv_grad_kernel,
        "qkv_grad",
        (p // pb,),
        [
            pl.BlockSpec((t, pb * ds), lambda g: (0, g)),
            fixed((t, 3 * n)),
            pl.BlockSpec(memory_space=pl.ANY),
        ],
        pl.BlockSpec((pb, 3, ds, n), lambda g: (g, 0, 0, 0)),
        sds(kept.shape, BF16),
        6 * t * d * n,
        2 * (3 * d * n + t * d + 3 * t * n),
        aliases={2: 0},
    )(normed, grad, kept)


def swap(value, axis):
    return lax.ppermute(value, axis, [(0, 1), (1, 0)])


def spread(value):
    rows = swap(value, "row")
    return (value, swap(value, "core"), rows, swap(rows, "core"))


def across(value, k):
    size = lax.axis_size("tp")
    return lax.ppermute(value, "tp", [(i, i ^ k) for i in range(size)])


def total(pieces):
    return sum(v.astype(F32) for v in pieces)


def add(*values):
    return total(values).astype(values[0].dtype)


def cut(value, pieces):
    rows = value.shape[0] // pieces
    return [value[r * rows : (r + 1) * rows] for r in range(pieces)]


def join(*pieces):
    return jnp.concatenate(pieces, 0)


class Line:
    def __init__(self):
        self.last = None

    def __call__(self, step, *operands):
        leaves, form = jax.tree.flatten(operands)
        spots = [i for i, v in enumerate(leaves) if isinstance(v, jax.Array)]
        if self.last is not None:
            kept, self.last = lax.optimization_barrier(([leaves[i] for i in spots], self.last))
            for i, v in zip(spots, kept):
                leaves[i] = v
        result = step(*jax.tree.unflatten(form, leaves))
        self.last = jax.tree.leaves(result)
        return result

    def sums(self, own, core, pieces, first=None):
        mine, theirs = cut(own, pieces), cut(swap(core, "core"), pieces)
        last = across(self(add, mine[3], theirs[3]), 1)
        near = self(add, mine[2], theirs[2], last)
        beside, first = self(lambda a, b, c, d: (add(a, b), add(c, d)), mine[1], theirs[1], mine[0], theirs[0])
        return [first, across(beside, 1), across(near, 2)]


def in_place_kernel(place_ref, *refs, count):
    for r, piece in enumerate(refs[:count]):

        @pl.when(pl.program_id(0) == r)
        def _():
            refs[-1][...] = piece[...]


def in_place(places, pieces, kept, total_rows):
    rows, d = pieces[0].shape
    count = len(pieces)
    return call(
        functools.partial(in_place_kernel, count=count),
        "inplace",
        (count,),
        [fixed((rows, d))] * count + [pl.BlockSpec(memory_space=pl.ANY)] * len(kept),
        pl.BlockSpec((rows, d), lambda r, place: (place[r] // rows, 0)),
        sds((total_rows, d), pieces[0].dtype),
        0,
        4 * rows * count * d,
        prefetch=1,
        aliases={1 + count: 0} if kept else None,
    )(places, *pieces, *kept)


def meet(value):
    value = value + across(value, 1)
    return value + across(value, 2)


def relative(value, places, pieces):
    rows = value.shape[0] // pieces
    return [lax.dynamic_slice_in_dim(value, places[r], rows, 0) for r in range(pieces)]


def body(
    inputs,
    prefix,
    expert_ids,
    norm_gains,
    qkv_weight,
    out_weight,
    router_weight,
    gate_up_weight,
    down_weight,
    cotangent,
    *,
    chunks,
):
    sequences, length, width = inputs.shape
    t = sequences * length
    tp = lax.axis_size("tp")
    quarter = t // tp
    column = lax.axis_index("tp")
    core = lax.axis_index("core")
    ctx = lax.axis_index("row") * 2 + core
    experts = router_weight.shape[1]
    group = experts // 2
    starts = [sum(chunks[:k]) for k in range(len(chunks))]
    x = inputs.reshape(t, width)
    places = jnp.stack([column ^ r for r in range(tp)]).astype(jnp.int32) * quarter
    x_q = lax.dynamic_slice_in_dim(x, column * quarter, quarter, 0)

    line = Line()
    attn_local = jnp.concatenate([qkv_weight, out_weight[None]], 0)
    attn_w = lax.all_gather(attn_local, PLANE, axis=0, tiled=False)
    triple = jnp.concatenate([gate_up_weight, down_weight[:, None]], 1)
    ds, f = triple.shape[2:]
    grouped = triple.reshape(2, group, 3, ds, f)
    ws = []
    for begin, e in zip(starts, chunks):
        mine = lax.all_to_all(grouped[:, begin : begin + e], "core", 0, 0, tiled=True)
        ws.append(lax.all_gather(mine, FR, axis=0, tiled=False).reshape(-1, e, 3, ds, f))
    gains_low = lax.all_gather(norm_gains, PLANE, axis=1, tiled=True)
    router = lax.all_gather(router_weight, PLANE, axis=0, tiled=True)
    cots = relative(cotangent.reshape(t, width), places, tp)
    c0 = join(*cots)
    c1 = swap(c0, "core")
    attn_w, gains_low, router, c0 = lax.optimization_barrier((attn_w, gains_low, router, c0))
    p = attn_w.shape[0]

    gains = gains_low.astype(F32)
    n = attn_w.shape[3]
    router_rows = jnp.concatenate([router.T, jnp.zeros((128 - experts, width), BF16)], 0)

    own_gains = lax.dynamic_slice_in_dim(gains[2:4], column * n, n, 1)[:, None, :]
    halves = jnp.arange(0, HEAD_DIM, 2).astype(F32) / HEAD_DIM
    inverse = 1.0 / THETA**halves
    positions = ctx * length + jnp.arange(length, dtype=jnp.int32)
    angles = positions.astype(F32)[:, None] * inverse[None, :]
    cosine = jnp.concatenate([jnp.cos(angles)] * 2, 1)
    sine = jnp.concatenate([-jnp.sin(angles), jnp.sin(angles)], 1)
    offsets = jnp.stack([ctx, ctx ^ 1, ctx ^ 2, ctx ^ 3, ctx]).astype(jnp.int32) * length
    scal = jnp.concatenate([offsets, prefix.astype(jnp.int32)])
    ids_q = lax.dynamic_slice_in_dim(expert_ids.reshape(t, -1), column * quarter, quarter, 0)
    normed_one, raw, values, squares = line(qkv_project, x, gains[0:1], attn_w)
    v_blocks = spread(values)
    scales = lax.rsqrt(meet(squares[:, :, 0]) / width + EPSILON)[:, :, None]
    queries, keys = line(prepare, raw, scales, own_gains, cosine, sine)
    k_blocks = spread(keys)
    blocks = k_blocks + v_blocks
    heads = line(attend, scal, queries, blocks, length)
    sums = line(project_out, places, heads, attn_w, tp)
    near = line(add, sums[2], across(sums[3], 1))
    sums = [sums[0], across(sums[1], 1), across(near, 2)]
    mid, ext, probs, chosen = line(norm_two, x_q, sums, gains[1:2], router_rows, ids_q, experts)
    far = across(ext, 2)
    near = across(ext, 1)
    x0 = line(join, ext, near, far, across(far, 1))
    x1 = swap(x0, "core")

    xs, cs = [x0, x1], [c0, c1]
    blocks_in = jnp.arange(width // TILE, dtype=jnp.int32)
    hid, dgu, side, grads = [], [], [], []
    dx = []

    def up(k):
        first = (core * group + starts[k]).astype(jnp.int32)[None]
        for kept, made in zip((hid, dgu, side), line(expert_up, first, xs, cs, ws[k])):
            kept.append(made)

    def back(k, before):
        gates = side if k == len(chunks) - 1 else []
        return line(expert_down, [dgu[k]], [ws[k]], 0, 2, gates, before, 2, "expert_dx")

    def weight_grad(k):
        return line(expert_grads, xs, cs, hid[k], dgu[k], p, chunks[k])

    def to_owners(made, k, after):
        made, after = lax.optimization_barrier((made, after))
        made = made.reshape(-1, 2, chunks[k], 3, ds, f)
        return lax.optimization_barrier(lax.psum_scatter(made, FR, scatter_dimension=0, tiled=False))

    for k in range(len(chunks)):
        up(k)
        dx = back(k, dx)
        if k < len(chunks) - 1:
            made = weight_grad(k)
            grads.append(to_owners(made, k, ()))
    d_normed = line.sums(*dx, tp)
    moe = line(expert_down, hid, ws, 2, 1, [], [], 2, "expert_out")
    late = weight_grad(len(chunks) - 1)

    d_mid, d_mid_low, gain_two, grad_router = line(
        norm_two_back, d_normed, mid, ext, probs, chosen, cots[0], gains[1:2], router_rows
    )
    far = across(d_mid_low, 2)
    near = across(d_mid_low, 1)
    d_mid_low = line(join, d_mid_low, near, far, across(far, 1))
    own, beside = cut(moe[0], tp), cut(swap(moe[1], "core"), tp)
    last = across(line(add, own[3], beside[3]), 1)

    d_heads = line(heads_grad, places, d_mid_low, attn_w, tp)
    grads.append(to_owners(late, len(chunks) - 1, d_heads))
    dq, b0, b1, b2, b3 = line(attend_back, scal, queries, blocks, d_heads, length)
    r1 = swap(b1, "core")
    r3 = swap(b3, "core")
    near = line(add, own[2], beside[2], last)
    next_one = line(add, own[1], beside[1])
    moe = [across(next_one, 1), across(near, 2)]
    r2 = swap(line(add, b2, r3), "row")
    grad_attn = line(out_weight_grad, places, d_mid_low, heads, p, tp)
    out = line(lambda *v: total(v).astype(BF16), mid, own[0], beside[0], *moe)
    out_far = across(out, 2)
    out_near = across(out, 1)
    d_kv = line(lambda *v: total(v), b0, r1, r2)
    out_far, d_kv = lax.optimization_barrier((out_far, d_kv))
    out_both = across(out_far, 1)
    u, inner, gain_qk = line(unturn, dq, d_kv[0], raw, scales, own_gains, cosine, sine)
    outputs = line(in_place, places, [out, out_near, out_far, out_both], [], t).reshape(inputs.shape)

    def parted(k):
        own, other = line(
            lambda v: [lax.dynamic_index_in_dim(v, c, 0, keepdims=False) for c in (core, core ^ 1)], grads[k]
        )
        return own, swap(other, "core")

    def settled(k, pair, kept):
        steps = jnp.arange(chunks[k] // 2, dtype=jnp.int32)
        spots = jnp.concatenate([(c * group + starts[k]) // 2 + steps for c in (core, core ^ 1)])
        return line(settle, spots.astype(jnp.int32), pair, kept, experts)

    inner = (meet(inner[:, :, 0]) / width)[:, :, None]
    d_raw, *d_one = line(
        raw_back, places, u, raw, scales, inner, own_gains, d_kv[1].astype(BF16), attn_w, tp
    )
    last = across(d_one[3], 1)
    near = line(add, d_one[2], last)
    d_one = [d_one[0], across(d_one[1], 1), across(near, 2)]
    grad_attn = line(qkv_grads, normed_one, d_raw, grad_attn, p)
    pairs = [parted(0)]
    grad_in, gain_one = line(norm_one_back, d_one, x_q, d_mid, gains[0:1])
    far = across(grad_in, 2)
    near = across(grad_in, 1)
    grad_attn, gain_one = lax.optimization_barrier((grad_attn, gain_one))
    grad_attn = lax.psum_scatter(grad_attn, PLANE, scatter_dimension=0, tiled=False)
    placed = lax.dynamic_update_slice_in_dim(
        jnp.zeros((2, width), F32), gain_qk[:, 0, :], column * n, 1
    )

    small = line(lambda *v: jnp.concatenate(v, 0), grad_router[:experts], gain_one, gain_two, placed)
    rows = small.shape[0]
    small = small.reshape(rows, p, ds).transpose(1, 0, 2)
    small = jnp.sum(lax.all_to_all(small, PLANE, 0, 0, tiled=True), 0)
    other = across(small, 1)
    both = across(far, 1)
    kept = settled(0, pairs[0], [])
    placed_in = line(in_place, places[:2], [grad_in, near], [], t)
    pairs.append(parted(1))
    owned_gate_up, owned_down = settled(1, pairs[1], kept)
    small = line(lambda a, b: a + b, small, other)
    other = across(small, 2)
    grad_inputs = line(in_place, places[2:], [far, both], [placed_in], t).reshape(inputs.shape)
    small = line(lambda a, b: a + b, small, other)
    owned_gains = small[experts:]
    owned_router = small[:experts].T
    return (
        outputs,
        grad_inputs,
        owned_gains,
        grad_attn[:3].astype(F32),
        grad_attn[3].astype(F32),
        owned_router,
        owned_gate_up,
        owned_down,
    )


def solution(mesh):
    fsdp, ctx, tp = (mesh.shape[a] for a in ("fsdp", "ctx", "tp"))
    fine = Mesh(mesh.devices.reshape(fsdp, ctx // 2, 2, tp), EVERY)
    tokens = P("fsdp", ("row", "core"), None)
    weights = (
        P(None, PLANE),
        P(None, PLANE, "tp"),
        P(PLANE, "tp"),
        P(PLANE, None),
        P(None, None, PLANE, "tp"),
        P(None, PLANE, "tp"),
    )
    return jax.shard_map(
        functools.partial(body, chunks=(6, 2)),
        mesh=fine,
        in_specs=(tokens, P("fsdp"), tokens) + weights + (tokens,),
        out_specs=(tokens, tokens) + weights,
        check_vma=False,
    )
```

```python
import functools

import jax
import jax.numpy as jnp
from jax import lax
from jax.experimental import pallas as pl
from jax.experimental.pallas import tpu as pltpu
from jax.sharding import Mesh, PartitionSpec as P

HEAD_DIM = 128
EPSILON = 1e-05
THETA = 10000.0
TILE = 256
F32 = jnp.float32
BF16 = jnp.bfloat16
FR = ("fsdp", "row")
LANES = 128
PLANE = ("fsdp", "row", "core")
EVERY = ("fsdp", "row", "core", "tp")


def nn(a, b):
    return lax.dot_general(a, b, (((1,), (0,)), ((), ())), preferred_element_type=F32)


def nt(a, b):
    return lax.dot_general(a, b, (((1,), (1,)), ((), ())), preferred_element_type=F32)


def tn(a, b):
    return lax.dot_general(a, b, (((0,), (0,)), ((), ())), preferred_element_type=F32)


def call(kernel, name, grid, in_specs, out_specs, out_shape, flops, moved, scratch=(), prefetch=0, limit=56, aliases=None):
    return pl.pallas_call(
        kernel,
        name=name,
        out_shape=out_shape,
        grid_spec=pltpu.PrefetchScalarGridSpec(
            num_scalar_prefetch=prefetch,
            grid=grid,
            in_specs=in_specs,
            out_specs=out_specs,
            scratch_shapes=list(scratch),
        ),
        input_output_aliases=aliases or {},
        compiler_params=pltpu.CompilerParams(
            dimension_semantics=("arbitrary",) * len(grid), vmem_limit_bytes=limit << 20
        ),
        cost_estimate=pl.CostEstimate(flops=int(flops), bytes_accessed=int(moved), transcendentals=0),
    )


def fixed(shape):
    return pl.BlockSpec(shape, lambda *a: (0,) * len(shape), pipeline_mode=pl.Buffered(1))


def sds(shape, dtype):
    return jax.ShapeDtypeStruct(shape, dtype)


def qkv_kernel(x_ref, g_ref, w_ref, n_ref, raw_ref, v_ref, sq_ref):
    c = pl.program_id(0)

    @pl.when(c == 0)
    def _():
        x = x_ref[...].astype(F32)
        r = lax.rsqrt(jnp.mean(x * x, -1, keepdims=True) + EPSILON)
        n_ref[...] = (x * r * g_ref[...]).astype(BF16)

    w = w_ref[...]
    y = nn(n_ref[...], w.reshape(w.shape[0] * w.shape[2], w.shape[3]))

    @pl.when(c < 2)
    def _():
        raw_ref[0] = y
        sq_ref[0] = jnp.broadcast_to(jnp.sum(y * y, -1, keepdims=True), sq_ref.shape[1:])

    @pl.when(c == 2)
    def _():
        v_ref[...] = y.astype(BF16)


def qkv_project(x, gain, w):
    t, d = x.shape
    p, _, ds, n = w.shape
    return call(
        qkv_kernel,
        "qkv",
        (3,),
        [
            fixed((t, d)),
            fixed((1, d)),
            pl.BlockSpec((p, 1, ds, n), lambda c: (0, c, 0, 0)),
        ],
        [
            pl.BlockSpec((t, d), lambda c: (0, 0)),
            pl.BlockSpec((1, t, n), lambda c: (jnp.minimum(c, 1), 0, 0)),
            pl.BlockSpec((t, n), lambda c: (0, 0)),
            pl.BlockSpec((1, t, 128), lambda c: (jnp.minimum(c, 1), 0, 0)),
        ],
        [sds((t, d), BF16), sds((2, t, n), F32), sds((t, n), BF16), sds((2, t, 128), F32)],
        6 * t * d * n,
        2 * (3 * d * n + 2 * t * d) + 10 * t * n,
    )(x, gain, w)


def turn(v, cosine, sine):
    half = v.shape[-1] // 2
    return v * cosine + pltpu.roll(v, half, 1) * sine


def prep_kernel(raw_ref, s_ref, g_ref, cos_ref, sin_ref, q_ref, k_ref):
    reps = raw_ref.shape[1] // cos_ref.shape[0]
    cosine = jnp.concatenate([cos_ref[...]] * reps, 0)
    sine = jnp.concatenate([sin_ref[...]] * reps, 0)
    q = raw_ref[0] * s_ref[0] * g_ref[0]
    k = raw_ref[1] * s_ref[1] * g_ref[1]
    q_ref[...] = turn(q, cosine, sine).astype(BF16)
    k_ref[...] = turn(k, cosine, sine).astype(BF16)


def prepare(raw, scales, gains, cosine, sine):
    _, t, n = raw.shape
    h = HEAD_DIM
    length = cosine.shape[0]
    return call(
        prep_kernel,
        "prep",
        (n // h,),
        [
            pl.BlockSpec((2, t, h), lambda i: (0, 0, i)),
            fixed((2, t, 1)),
            pl.BlockSpec((2, 1, h), lambda i: (0, 0, i)),
            fixed((length, h)),
            fixed((length, h)),
        ],
        [pl.BlockSpec((t, h), lambda i: (0, i))] * 2,
        [sds((t, n), BF16)] * 2,
        20 * t * n,
        12 * t * n,
    )(raw, scales, gains, cosine, sine)


def masked_probs(s, scal_ref, q, ks):
    length = q.shape[0]
    prefix = scal_ref[5 + s]
    rows = lax.broadcasted_iota(jnp.int32, (length, length), 0) + scal_ref[4]
    columns = lax.broadcasted_iota(jnp.int32, (length, length), 1)
    pieces = []
    for b, k in enumerate(ks):
        place = columns + scal_ref[b]
        visible = (place <= rows) | (place < prefix)
        pieces.append(jnp.where(visible, nt(q, k) * HEAD_DIM ** (-0.5), -1e30))
    scores = jnp.concatenate(pieces, 1)
    expo = jnp.exp(scores - jnp.max(scores, -1, keepdims=True))
    return expo / jnp.sum(expo, -1, keepdims=True)


def attend_kernel(scal_ref, q_ref, *refs):
    o_ref = refs[8]
    probs = masked_probs(pl.program_id(0), scal_ref, q_ref[...], [r[...] for r in refs[:4]])
    v = jnp.concatenate([r[...] for r in refs[4:8]], 0)
    o_ref[...] = nn(probs.astype(BF16), v).astype(BF16)


def attend(scal, q, blocks, length):
    t, n = q.shape
    h = HEAD_DIM
    one = pl.BlockSpec((length, h), lambda s, i, *_: (s, i))
    return call(
        attend_kernel,
        "attend",
        (t // length, n // h),
        [one] * 9,
        one,
        sds((t, n), BF16),
        16 * t * n * length,
        24 * t * n,
        prefetch=1,
    )(scal, q, *blocks)


def attend_back_kernel(scal_ref, q_ref, *refs):
    g_ref, dq_ref, outs = refs[8], refs[9], refs[10:]
    length = q_ref.shape[0]
    q = q_ref[...]
    grad = g_ref[...]
    probs = masked_probs(pl.program_id(0), scal_ref, q, [r[...] for r in refs[:4]])
    k = jnp.concatenate([r[...] for r in refs[:4]], 0)
    v = jnp.concatenate([r[...] for r in refs[4:8]], 0)
    d_probs = nt(grad, v)
    inner = jnp.sum(probs * d_probs, -1, keepdims=True)
    d_scores = (probs * (d_probs - inner)).astype(BF16)
    scale = HEAD_DIM ** (-0.5)
    dq_ref[...] = nn(d_scores, k) * scale
    dk = (tn(d_scores, q) * scale).astype(BF16)
    dv = tn(probs.astype(BF16), grad).astype(BF16)
    for b, o in enumerate(outs):
        o[0] = dk[b * length : (b + 1) * length]
        o[1] = dv[b * length : (b + 1) * length]


def attend_back(scal, q, blocks, grad, length):
    t, n = q.shape
    h = HEAD_DIM
    one = pl.BlockSpec((length, h), lambda s, i, *_: (s, i))
    two = pl.BlockSpec((2, length, h), lambda s, i, *_: (0, s, i))
    return call(
        attend_back_kernel,
        "attend_back",
        (t // length, n // h),
        [one] * 10,
        [one] + [two] * 4,
        [sds((t, n), F32)] + [sds((2, t, n), BF16)] * 4,
        40 * t * n * length,
        48 * t * n,
        prefetch=1,
    )(scal, q, *blocks, grad)


def out_kernel(place_ref, h_ref, w_ref, *outs):
    w = w_ref[...]
    w = w.reshape(-1, w.shape[-1])
    rows = outs[0].shape[0]
    heads = jnp.concatenate(
        [h_ref[pl.ds(pl.multiple_of(place_ref[r], rows), rows), :] for r in range(len(outs))], 0
    )
    y = nt(heads, w).astype(BF16)
    for r, o in enumerate(outs):
        o[...] = y[r * rows : (r + 1) * rows]


def project_out(places, heads, w, pieces):
    t, n = heads.shape
    p, _, ds, _ = w.shape
    pb = max(1, 2 * TILE // ds)
    return call(
        out_kernel,
        "outproj",
        (p // pb,),
        [fixed((t, n)), pl.BlockSpec((pb, 1, ds, n), lambda g, *_: (g, 3, 0, 0))],
        [pl.BlockSpec((t // pieces, pb * ds), lambda g, *_: (0, g))] * pieces,
        [sds((t // pieces, p * ds), BF16)] * pieces,
        2 * t * n * p * ds,
        2 * (t * n + n * p * ds + t * p * ds),
        prefetch=1,
    )(places, heads, w)


def d_heads_kernel(place_ref, g_ref, w_ref, o_ref, *, pieces):
    w = w_ref[...]
    y = nn(g_ref[...], w.reshape(w.shape[0] * w.shape[2], w.shape[3])).astype(BF16)
    rows = y.shape[0] // pieces
    for r in range(pieces):
        o_ref[pl.ds(pl.multiple_of(place_ref[r], rows), rows), :] = y[r * rows : (r + 1) * rows]


def heads_grad(places, grad, w, pieces):
    t, d = grad.shape
    p, _, ds, n = w.shape
    return call(
        functools.partial(d_heads_kernel, pieces=pieces),
        "dheads",
        (1,),
        [fixed((t, d)), pl.BlockSpec((p, 1, ds, n), lambda g, *_: (0, 3, 0, 0), pipeline_mode=pl.Buffered(1))],
        fixed((t, n)),
        sds((t, n), BF16),
        2 * t * n * d,
        2 * (t * n + n * d + t * d),
        prefetch=1,
    )(places, grad, w)


def grad_out_kernel(place_ref, g_ref, h_ref, o_ref, *, pieces):
    rows = g_ref.shape[0] // pieces
    heads = jnp.concatenate(
        [h_ref[pl.ds(pl.multiple_of(place_ref[r], rows), rows), :] for r in range(pieces)], 0
    )
    o_ref[...] = tn(g_ref[...], heads).astype(BF16).reshape(o_ref.shape)


def out_weight_grad(places, grad, heads, p, pieces):
    t, d = grad.shape
    n = heads.shape[1]
    ds = d // p
    pb = max(1, TILE // ds)
    return call(
        functools.partial(grad_out_kernel, pieces=pieces),
        "gradout",
        (p // pb,),
        [pl.BlockSpec((t, pb * ds), lambda g, *_: (0, g)), fixed((t, n))],
        pl.BlockSpec((pb, 1, ds, n), lambda g, *_: (g, 3, 0, 0)),
        sds((p, 4, ds, n), BF16),
        2 * t * n * d,
        2 * (t * n + n * d + t * d),
        prefetch=1,
    )(places, grad, heads)


def norm_two_kernel(x_ref, a_ref, b_ref, c_ref, g_ref, w_ref, ids_ref, mid_ref, ext_ref, probs_ref, chosen_ref, *, experts):
    mid = x_ref[...].astype(F32) + a_ref[...].astype(F32) + b_ref[...].astype(F32) + c_ref[...].astype(F32)
    mid_ref[...] = mid
    d = mid.shape[1]
    r = lax.rsqrt(jnp.mean(mid * mid, -1, keepdims=True) + EPSILON)
    low = (mid * r * g_ref[...]).astype(BF16)
    ext_ref[:, :d] = low
    logits = nt(low, w_ref[...])
    lane = lax.broadcasted_iota(jnp.int32, logits.shape, 1)
    logits = jnp.where(lane < experts, logits, -1e30)
    expo = jnp.exp(logits - jnp.max(logits, -1, keepdims=True))
    probs = expo / jnp.sum(expo, -1, keepdims=True)
    chosen = jnp.zeros_like(probs)
    for j in range(ids_ref.shape[1]):
        chosen += (ids_ref[:, j : j + 1] == lane).astype(F32)
    probs_ref[...] = probs
    chosen_ref[...] = chosen
    gates = probs * chosen
    high = gates.astype(BF16)
    rest = (gates - high.astype(F32)).astype(BF16)
    ext_ref[:, d:] = jnp.concatenate([high[:, : LANES // 2], rest[:, : LANES // 2]], 1)


def norm_two(x, sums, gain, router, ids, experts):
    t, d = x.shape
    return call(
        functools.partial(norm_two_kernel, experts=experts),
        "norm_two",
        (1,),
        [fixed((t, d))] * 4 + [fixed((1, d)), fixed(router.shape), fixed(ids.shape)],
        [fixed((t, d)), fixed((t, d + LANES)), fixed((t, LANES)), fixed((t, LANES))],
        [sds((t, d), F32), sds((t, d + LANES), BF16), sds((t, LANES), F32), sds((t, LANES), F32)],
        2 * t * d * LANES,
        14 * t * d,
    )(x, *sums, gain, router, ids)


def norm_two_back_kernel(a_ref, b_ref, c_ref, mid_ref, ext_ref, probs_ref, chosen_ref, cot_ref, g_ref, w_ref, *outs):
    mid_grad_ref, low_ref, gain_ref, router_ref = outs
    d = mid_ref.shape[1]
    du = a_ref[...].astype(F32) + b_ref[...].astype(F32) + c_ref[...].astype(F32)
    probs = probs_ref[...]
    masked = du[:, d:] * chosen_ref[...]
    d_logits = (probs * (masked - jnp.sum(probs * masked, -1, keepdims=True))).astype(BF16)
    router_ref[...] = tn(d_logits, ext_ref[:, :d])
    u = du[:, :d] + nn(d_logits, w_ref[...])
    mid = mid_ref[...]
    r = lax.rsqrt(jnp.mean(mid * mid, -1, keepdims=True) + EPSILON)
    hat = mid * r
    gain_ref[...] = jnp.sum(u * hat, 0, keepdims=True)
    w = u * g_ref[...]
    grad = cot_ref[...].astype(F32) + r * (w - hat * jnp.mean(w * hat, -1, keepdims=True))
    mid_grad_ref[...] = grad
    low_ref[...] = grad.astype(BF16)


def norm_two_back(sums, mid, ext, probs, chosen, cot, gain, router):
    t, d = mid.shape
    wide = fixed((t, d + LANES))
    return call(
        norm_two_back_kernel,
        "norm_two_back",
        (1,),
        [wide] * 3
        + [fixed((t, d)), wide, fixed((t, LANES)), fixed((t, LANES)), fixed((t, d)), fixed((1, d)), fixed(router.shape)],
        [fixed((t, d)), fixed((t, d)), fixed((1, d)), fixed((LANES, d))],
        [sds((t, d), F32), sds((t, d), BF16), sds((1, d), F32), sds((LANES, d), F32)],
        4 * t * d * LANES,
        20 * t * d,
    )(*sums, mid, ext, probs, chosen, cot, gain, router)


def norm_one_back_kernel(a_ref, b_ref, c_ref, x_ref, mid_grad_ref, g_ref, o_ref, gain_ref):
    u = a_ref[...].astype(F32) + b_ref[...].astype(F32) + c_ref[...].astype(F32)
    x = x_ref[...].astype(F32)
    r = lax.rsqrt(jnp.mean(x * x, -1, keepdims=True) + EPSILON)
    hat = x * r
    gain_ref[...] = jnp.sum(u * hat, 0, keepdims=True)
    w = u * g_ref[...]
    o_ref[...] = (mid_grad_ref[...] + r * (w - hat * jnp.mean(w * hat, -1, keepdims=True))).astype(BF16)


def norm_one_back(sums, x, mid_grad, gain):
    t, d = x.shape
    return call(
        norm_one_back_kernel,
        "norm_one_back",
        (1,),
        [fixed((t, d))] * 5 + [fixed((1, d))],
        [fixed((t, d)), fixed((1, d))],
        [sds((t, d), BF16), sds((1, d), F32)],
        20 * t * d,
        14 * t * d,
    )(*sums, x, mid_grad, gain)


def expert_kernel(first_ref, *refs, parts):
    xs, cs, w_ref = refs[:parts], refs[parts : 2 * parts], refs[2 * parts]
    hid_ref, dgu_ref, dg_ref = refs[2 * parts + 1 :]
    e = pl.program_id(0)
    t = cs[0].shape[0]
    d = cs[0].shape[1]

    @pl.when(e == 0)
    def _():
        dg_ref[...] = jnp.zeros_like(dg_ref)

    f = w_ref.shape[4]
    me = first_ref[0] + e
    lane = lax.broadcasted_iota(jnp.int32, (t, LANES), 1)
    for part, (x_ref, c_ref) in enumerate(zip(xs, cs)):

        def block(x_ref=x_ref, c_ref=c_ref, to=slice(part * t, (part + 1) * t)):
            x = x_ref[:, :d]
            a = nn(x, w_ref[:, 0, 0].reshape(d, f))
            b = nn(x, w_ref[:, 0, 1].reshape(d, f))
            dh = nn(c_ref[...], w_ref[:, 0, 2].reshape(d, f))
            mine = (lane == me) | (lane == me + LANES // 2)
            gate = jnp.sum(jnp.where(mine, x_ref[:, d:].astype(F32), 0.0), -1, keepdims=True)
            sigma = jax.nn.sigmoid(a)
            swish = a * sigma
            act = swish * b
            hid_ref[to, :] = (gate * act).astype(BF16)
            d_gate = jnp.sum(dh * act, -1, keepdims=True)
            dg_ref[to, :] += jnp.where(lane == me, d_gate, 0.0)
            inner = dh * gate
            dgu_ref[to, :f] = (inner * b * sigma * (1.0 + a * (1.0 - sigma))).astype(BF16)
            dgu_ref[to, f:] = (inner * swish).astype(BF16)

        block()


def expert_up(first, xs, cs, w):
    t, d = cs[0].shape
    parts = len(cs)
    p, e, _, ds, f = w.shape
    every = parts * t
    return call(
        functools.partial(expert_kernel, parts=parts),
        "expert_up",
        (e,),
        [fixed(x.shape) for x in xs]
        + [fixed((t, d))] * parts
        + [pl.BlockSpec((p, 1, 3, ds, f), lambda i, *_: (0, i, 0, 0, 0))],
        [
            pl.BlockSpec((every, f), lambda i, *_: (0, i)),
            pl.BlockSpec((every, 2 * f), lambda i, *_: (0, i)),
            pl.BlockSpec((every, LANES), lambda i, *_: (0, 0)),
        ],
        [sds((every, e * f), BF16), sds((every, e * 2 * f), BF16), sds((every, LANES), F32)],
        6 * every * d * f * e,
        2 * (3 * d * f * e + 2 * every * d + 3 * every * f * e),
        prefetch=1,
    )(first, *xs, *cs, w)


def expert_grad_kernel(*refs, parts):
    xs, cs, hid_ref, dgu_ref, o_ref = refs[:parts], refs[parts : 2 * parts], *refs[2 * parts :]
    pb, e, _, ds, f = o_ref.shape
    x = jnp.concatenate([r[...] for r in xs], 0)
    c = jnp.concatenate([r[...] for r in cs], 0)
    both = tn(x, dgu_ref[...]).astype(BF16)
    down = tn(c, hid_ref[...]).astype(BF16)
    for i in range(e):
        o_ref[:, i, 0] = both[:, 2 * i * f : (2 * i + 1) * f].reshape(pb, ds, f)
        o_ref[:, i, 1] = both[:, (2 * i + 1) * f : (2 * i + 2) * f].reshape(pb, ds, f)
        o_ref[:, i, 2] = down[:, i * f : (i + 1) * f].reshape(pb, ds, f)


def expert_grads(xs, cs, hid, dgu, p, e):
    t, d = cs[0].shape
    parts = len(cs)
    ds = d // p
    f = hid.shape[1] // e
    pb = max(1, TILE // ds)
    column = pl.BlockSpec((t, pb * ds), lambda g: (0, g))
    return call(
        functools.partial(expert_grad_kernel, parts=parts),
        "expert_grad",
        (p // pb,),
        [column] * (2 * parts) + [fixed(hid.shape), fixed(dgu.shape)],
        pl.BlockSpec((pb, e, 3, ds, f), lambda g: (g, 0, 0, 0, 0)),
        sds((p, e, 3, ds, f), BF16),
        6 * parts * t * d * f * e,
        2 * (3 * d * f * e + 2 * parts * t * d + 3 * parts * t * f * e),
    )(*xs, *cs, hid, dgu)


def settle_kernel(spot_ref, *refs, pieces):
    gate_up_ref, down_ref = refs[-2:]
    each = pl.num_programs(0) // pieces
    for r in range(pieces):

        @pl.when(pl.program_id(0) // each == r)
        def _():
            gate_up_ref[...] = refs[r][:, :2].astype(F32)
            down_ref[...] = refs[r][:, 2].astype(F32)


def settle(spots, pieces, kept, experts):
    e, _, ds, f = pieces[0].shape
    count = len(pieces)
    each = e // 2

    def piece(r):
        return pl.BlockSpec((2, 3, ds, f), lambda g, spot: (jnp.clip(g - r * each, 0, each - 1), 0, 0, 0))

    return call(
        functools.partial(settle_kernel, pieces=count),
        "settle",
        (count * each,),
        [piece(r) for r in range(count)] + [pl.BlockSpec(memory_space=pl.ANY)] * len(kept),
        [
            pl.BlockSpec((2, 2, ds, f), lambda g, spot: (spot[g], 0, 0, 0)),
            pl.BlockSpec((2, ds, f), lambda g, spot: (spot[g], 0, 0)),
        ],
        [sds((experts, 2, ds, f), F32), sds((experts, ds, f), F32)],
        0,
        18 * count * e * ds * f,
        prefetch=1,
        aliases={1 + count + i: i for i in range(len(kept))},
    )(spots, *pieces, *kept)


def down_kernel(*refs, planes, chunks, sides, begun):
    acts, ws = refs[:chunks], refs[chunks : 2 * chunks]
    gates = refs[2 * chunks : 2 * chunks + sides]
    before = refs[2 * chunks + sides : 2 * chunks + sides + begun]
    outs = refs[2 * chunks + sides + begun :]
    g = pl.program_id(0)
    pb, _, _, ds, f = ws[0].shape
    wide = pb * ds
    rows = outs[0].shape[0]
    joined = [
        jnp.concatenate([w[:, i, c].reshape(wide, f) for i in range(w.shape[1]) for c in range(planes)], 1)
        for w in ws
    ]
    to = pl.ds(pl.multiple_of(g * wide, wide), wide)
    for part, o in enumerate(outs):
        own = slice(part * rows, (part + 1) * rows)
        value = sum(nt(a[own, :], w) for a, w in zip(acts, joined))
        if begun:
            value += before[part][...].astype(F32)
        o[:, to] = value.astype(BF16)
    if sides:

        @pl.when(g == 0)
        def _():
            for part, o in enumerate(outs):
                own = slice(part * rows, (part + 1) * rows)
                o[:, o.shape[1] - LANES :] = sum(s[own, :] for s in gates).astype(BF16)


def expert_down(acts, ws, plane, planes, gates, before, parts, name):
    every = acts[0].shape[0]
    p, _, _, ds, f = ws[0].shape
    k = sum(a.shape[1] for a in acts)
    t = every // parts
    chunks = len(acts)
    d = p * ds + (LANES if gates else 0)
    pb = max(1, 2 * TILE // ds)
    return call(
        functools.partial(down_kernel, planes=planes, chunks=chunks, sides=len(gates), begun=len(before)),
        name,
        (p // pb,),
        [fixed(a.shape) for a in acts]
        + [pl.BlockSpec((pb, w.shape[1], planes, ds, f), lambda g: (g, 0, plane, 0, 0)) for w in ws]
        + [fixed((every, LANES))] * len(gates)
        + [pl.BlockSpec((t, pb * ds), lambda g: (0, g))] * len(before),
        [pl.BlockSpec((t, d), lambda g: (0, 0))] * parts,
        [sds((t, d), BF16)] * parts,
        2 * every * k * p * ds,
        2 * (every * k + k * p * ds) + 2 * every * d,
    )(*acts, *ws, *gates, *before)


def unturn_kernel(dq_ref, dk_ref, raw_ref, s_ref, g_ref, cos_ref, sin_ref, u_ref, in_ref, gg_ref):
    h = pl.program_id(0)
    reps = raw_ref.shape[1] // cos_ref.shape[0]
    cosine = jnp.concatenate([cos_ref[...]] * reps, 0)
    sine = jnp.concatenate([sin_ref[...]] * reps, 0)
    for i, grad in enumerate((dq_ref[...], dk_ref[...])):
        u = turn(grad, cosine, -sine)
        hat = raw_ref[i] * s_ref[i]
        product = u * hat
        u_ref[i] = u
        gg_ref[i] = jnp.sum(product, 0, keepdims=True)
        row = jnp.broadcast_to(jnp.sum(product * g_ref[i], -1, keepdims=True), in_ref.shape[1:])

        @pl.when(h == 0)
        def _():
            in_ref[i] = row

        @pl.when(h != 0)
        def _():
            in_ref[i] += row


def unturn(dq, dk, raw, scales, gains, cosine, sine):
    _, t, n = raw.shape
    h = HEAD_DIM
    length = cosine.shape[0]
    column = pl.BlockSpec((t, h), lambda i: (0, i))
    pair = pl.BlockSpec((2, t, h), lambda i: (0, 0, i))
    return call(
        unturn_kernel,
        "unturn",
        (n // h,),
        [
            column,
            column,
            pair,
            fixed((2, t, 1)),
            pl.BlockSpec((2, 1, h), lambda i: (0, 0, i)),
            fixed((length, h)),
            fixed((length, h)),
        ],
        [
            pair,
            pl.BlockSpec((2, t, 128), lambda i: (0, 0, 0)),
            pl.BlockSpec((2, 1, h), lambda i: (0, 0, i)),
        ],
        [sds((2, t, n), F32), sds((2, t, 128), F32), sds((2, 1, n), F32)],
        30 * t * n,
        24 * t * n,
    )(dq, dk, raw, scales, gains, cosine, sine)


def raw_back_kernel(place_ref, u_ref, raw_ref, s_ref, in_ref, g_ref, dv_ref, w_ref, d_ref, *outs):
    t, n = dv_ref.shape

    @pl.when(pl.program_id(0) == 0)
    def _():
        for i in range(2):
            hat = raw_ref[i] * s_ref[i]
            d_ref[:, i * n : (i + 1) * n] = (
                s_ref[i] * (u_ref[i] * g_ref[i] - hat * in_ref[i])
            ).astype(BF16)
        d_ref[:, 2 * n :] = dv_ref[...]

    pb, _, ds, _ = w_ref.shape
    w = jnp.concatenate([w_ref[:, c].reshape(pb * ds, n) for c in range(3)], 1)
    y = nt(d_ref[...], w).astype(BF16)
    rows = outs[0].shape[0]
    outs[0][...] = y[:rows]
    for r, o in enumerate(outs):
        for q in range(len(outs)):

            @pl.when(place_ref[r] == q * rows)
            def _():
                o[...] = y[q * rows : (q + 1) * rows]


def raw_back(places, u, raw, scales, inner, gains, dv, w, pieces):
    t, n = dv.shape
    p, _, ds, _ = w.shape
    d = p * ds
    pb = max(1, 2 * TILE // ds)
    return call(
        raw_back_kernel,
        "raw_back",
        (p // pb,),
        [
            fixed((2, t, n)),
            fixed((2, t, n)),
            fixed((2, t, 1)),
            fixed((2, t, 1)),
            fixed((2, 1, n)),
            fixed((t, n)),
            pl.BlockSpec((pb, 3, ds, n), lambda g, *_: (g, 0, 0, 0)),
        ],
        [pl.BlockSpec((t, 3 * n), lambda g, *_: (0, 0))]
        + [pl.BlockSpec((t // pieces, pb * ds), lambda g, *_: (0, g))] * pieces,
        [sds((t, 3 * n), BF16)] + [sds((t // pieces, d), BF16)] * pieces,
        6 * t * d * n,
        2 * (3 * d * n + t * d) + 20 * t * n,
        prefetch=1,
    )(places, u, raw, scales, inner, gains, dv, w)


def qkv_grad_kernel(n_ref, d_ref, kept_ref, o_ref):
    pb, _, ds, n = o_ref.shape
    grads = tn(n_ref[...], d_ref[...]).astype(BF16)
    for c in range(3):
        o_ref[:, c] = grads[:, c * n : (c + 1) * n].reshape(pb, ds, n)


def qkv_grads(normed, grad, kept, p):
    t, d = normed.shape
    n = grad.shape[1] // 3
    ds = d // p
    pb = max(1, TILE // ds)
    return call(
        qkv_grad_kernel,
        "qkv_grad",
        (p // pb,),
        [
            pl.BlockSpec((t, pb * ds), lambda g: (0, g)),
            fixed((t, 3 * n)),
            pl.BlockSpec(memory_space=pl.ANY),
        ],
        pl.BlockSpec((pb, 3, ds, n), lambda g: (g, 0, 0, 0)),
        sds(kept.shape, BF16),
        6 * t * d * n,
        2 * (3 * d * n + t * d + 3 * t * n),
        aliases={2: 0},
    )(normed, grad, kept)


def swap(value, axis):
    return lax.ppermute(value, axis, [(0, 1), (1, 0)])


def spread(value):
    rows = swap(value, "row")
    return (value, swap(value, "core"), rows, swap(rows, "core"))


def across(value, k):
    size = lax.axis_size("tp")
    return lax.ppermute(value, "tp", [(i, i ^ k) for i in range(size)])


def total(pieces):
    return sum(v.astype(F32) for v in pieces)


def add(*values):
    return total(values).astype(values[0].dtype)


def cut(value, pieces):
    rows = value.shape[0] // pieces
    return [value[r * rows : (r + 1) * rows] for r in range(pieces)]


def join(*pieces):
    return jnp.concatenate(pieces, 0)


class Line:
    def __init__(self):
        self.last = None

    def __call__(self, step, *operands):
        leaves, form = jax.tree.flatten(operands)
        spots = [i for i, v in enumerate(leaves) if isinstance(v, jax.Array)]
        if self.last is not None:
            kept, self.last = lax.optimization_barrier(([leaves[i] for i in spots], self.last))
            for i, v in zip(spots, kept):
                leaves[i] = v
        result = step(*jax.tree.unflatten(form, leaves))
        self.last = jax.tree.leaves(result)
        return result

    def sums(self, own, core, pieces, first=None):
        mine, theirs = cut(own, pieces), cut(swap(core, "core"), pieces)
        last = across(self(add, mine[3], theirs[3]), 1)
        near = self(add, mine[2], theirs[2], last)
        beside, first = self(lambda a, b, c, d: (add(a, b), add(c, d)), mine[1], theirs[1], mine[0], theirs[0])
        return [first, across(beside, 1), across(near, 2)]


def in_place_kernel(place_ref, *refs, count):
    for r, piece in enumerate(refs[:count]):

        @pl.when(pl.program_id(0) == r)
        def _():
            refs[-1][...] = piece[...]


def in_place(places, pieces, kept, total_rows):
    rows, d = pieces[0].shape
    count = len(pieces)
    return call(
        functools.partial(in_place_kernel, count=count),
        "inplace",
        (count,),
        [fixed((rows, d))] * count + [pl.BlockSpec(memory_space=pl.ANY)] * len(kept),
        pl.BlockSpec((rows, d), lambda r, place: (place[r] // rows, 0)),
        sds((total_rows, d), pieces[0].dtype),
        0,
        4 * rows * count * d,
        prefetch=1,
        aliases={1 + count: 0} if kept else None,
    )(places, *pieces, *kept)


def meet(value):
    value = value + across(value, 1)
    return value + across(value, 2)


def relative(value, places, pieces):
    rows = value.shape[0] // pieces
    return [lax.dynamic_slice_in_dim(value, places[r], rows, 0) for r in range(pieces)]


def body(
    inputs,
    prefix,
    expert_ids,
    norm_gains,
    qkv_weight,
    out_weight,
    router_weight,
    gate_up_weight,
    down_weight,
    cotangent,
    *,
    chunks,
):
    sequences, length, width = inputs.shape
    t = sequences * length
    tp = lax.axis_size("tp")
    quarter = t // tp
    column = lax.axis_index("tp")
    core = lax.axis_index("core")
    ctx = lax.axis_index("row") * 2 + core
    experts = router_weight.shape[1]
    group = experts // 2
    starts = [sum(chunks[:k]) for k in range(len(chunks))]
    x = inputs.reshape(t, width)
    places = jnp.stack([column ^ r for r in range(tp)]).astype(jnp.int32) * quarter
    x_q = lax.dynamic_slice_in_dim(x, column * quarter, quarter, 0)

    line = Line()
    attn_local = jnp.concatenate([qkv_weight, out_weight[None]], 0)
    attn_w = lax.all_gather(attn_local, PLANE, axis=0, tiled=False)
    triple = jnp.concatenate([gate_up_weight, down_weight[:, None]], 1)
    ds, f = triple.shape[2:]
    grouped = triple.reshape(2, group, 3, ds, f)
    ws = []
    for begin, e in zip(starts, chunks):
        mine = lax.all_to_all(grouped[:, begin : begin + e], "core", 0, 0, tiled=True)
        ws.append(lax.all_gather(mine, FR, axis=0, tiled=False).reshape(-1, e, 3, ds, f))
    gains_low = lax.all_gather(norm_gains, PLANE, axis=1, tiled=True)
    router = lax.all_gather(router_weight, PLANE, axis=0, tiled=True)
    cots = relative(cotangent.reshape(t, width), places, tp)
    c0 = join(*cots)
    c1 = swap(c0, "core")
    attn_w, gains_low, router, c0 = lax.optimization_barrier((attn_w, gains_low, router, c0))
    p = attn_w.shape[0]

    gains = gains_low.astype(F32)
    n = attn_w.shape[3]
    router_rows = jnp.concatenate([router.T, jnp.zeros((128 - experts, width), BF16)], 0)

    own_gains = lax.dynamic_slice_in_dim(gains[2:4], column * n, n, 1)[:, None, :]
    halves = jnp.arange(0, HEAD_DIM, 2).astype(F32) / HEAD_DIM
    inverse = 1.0 / THETA**halves
    positions = ctx * length + jnp.arange(length, dtype=jnp.int32)
    angles = positions.astype(F32)[:, None] * inverse[None, :]
    cosine = jnp.concatenate([jnp.cos(angles)] * 2, 1)
    sine = jnp.concatenate([-jnp.sin(angles), jnp.sin(angles)], 1)
    offsets = jnp.stack([ctx, ctx ^ 1, ctx ^ 2, ctx ^ 3, ctx]).astype(jnp.int32) * length
    scal = jnp.concatenate([offsets, prefix.astype(jnp.int32)])
    ids_q = lax.dynamic_slice_in_dim(expert_ids.reshape(t, -1), column * quarter, quarter, 0)
    normed_one, raw, values, squares = line(qkv_project, x, gains[0:1], attn_w)
    v_blocks = spread(values)
    scales = lax.rsqrt(meet(squares[:, :, 0]) / width + EPSILON)[:, :, None]
    scales, values = lax.optimization_barrier((scales, v_blocks[2]))
    v_blocks = v_blocks[:2] + (values,) + v_blocks[3:]
    queries, keys = line(prepare, raw, scales, own_gains, cosine, sine)
    k_blocks = spread(keys)
    blocks = k_blocks + v_blocks
    heads = line(attend, scal, queries, blocks, length)
    sums = line(project_out, places, heads, attn_w, tp)
    near = line(add, sums[2], across(sums[3], 1))
    sums = [sums[0], across(sums[1], 1), across(near, 2)]
    mid, ext, probs, chosen = line(norm_two, x_q, sums, gains[1:2], router_rows, ids_q, experts)
    far = across(ext, 2)
    near = across(ext, 1)
    x0 = line(join, ext, near, far, across(far, 1))
    x1 = swap(x0, "core")

    xs, cs = [x0, x1], [c0, c1]
    blocks_in = jnp.arange(width // TILE, dtype=jnp.int32)
    hid, dgu, side, grads = [], [], [], []
    dx = []

    def up(k):
        first = (core * group + starts[k]).astype(jnp.int32)[None]
        for kept, made in zip((hid, dgu, side), line(expert_up, first, xs, cs, ws[k])):
            kept.append(made)

    def back(k, before):
        gates = side if k == len(chunks) - 1 else []
        return line(expert_down, [dgu[k]], [ws[k]], 0, 2, gates, before, 2, "expert_dx")

    def weight_grad(k):
        return line(expert_grads, xs, cs, hid[k], dgu[k], p, chunks[k])

    def to_owners(made, k, after):
        made, after = lax.optimization_barrier((made, after))
        made = made.reshape(-1, 2, chunks[k], 3, ds, f)
        return lax.optimization_barrier(lax.psum_scatter(made, FR, scatter_dimension=0, tiled=False))

    for k in range(len(chunks)):
        up(k)
        dx = back(k, dx)
        if k < len(chunks) - 1:
            made = weight_grad(k)
            grads.append(to_owners(made, k, ()))
    d_normed = line.sums(*dx, tp)
    moe = line(expert_down, hid, ws, 2, 1, [], [], 2, "expert_out")
    late = weight_grad(len(chunks) - 1)

    d_mid, d_mid_low, gain_two, grad_router = line(
        norm_two_back, d_normed, mid, ext, probs, chosen, cots[0], gains[1:2], router_rows
    )
    far = across(d_mid_low, 2)
    near = across(d_mid_low, 1)
    d_mid_low = line(join, d_mid_low, near, far, across(far, 1))
    own, beside = cut(moe[0], tp), cut(swap(moe[1], "core"), tp)
    last = across(line(add, own[3], beside[3]), 1)

    d_heads = line(heads_grad, places, d_mid_low, attn_w, tp)
    grads.append(to_owners(late, len(chunks) - 1, d_heads))
    dq, b0, b1, b2, b3 = line(attend_back, scal, queries, blocks, d_heads, length)
    r1 = swap(b1, "core")
    r3 = swap(b3, "core")
    near = line(add, own[2], beside[2], last)
    next_one = line(add, own[1], beside[1])
    moe = [across(next_one, 1), across(near, 2)]
    r2 = swap(line(add, b2, r3), "row")
    grad_attn = line(out_weight_grad, places, d_mid_low, heads, p, tp)
    out = line(lambda *v: total(v).astype(BF16), mid, own[0], beside[0], *moe)
    out_far = across(out, 2)
    out_near = across(out, 1)
    d_kv = line(lambda *v: total(v), b0, r1, r2)
    out_far, d_kv = lax.optimization_barrier((out_far, d_kv))
    out_both = across(out_far, 1)
    u, inner, gain_qk = line(unturn, dq, d_kv[0], raw, scales, own_gains, cosine, sine)
    outputs = line(in_place, places, [out, out_near, out_far, out_both], [], t).reshape(inputs.shape)

    def parted(k):
        own, other = line(
            lambda v: [lax.dynamic_index_in_dim(v, c, 0, keepdims=False) for c in (core, core ^ 1)], grads[k]
        )
        return own, swap(other, "core")

    def settled(k, pair, kept):
        steps = jnp.arange(chunks[k] // 2, dtype=jnp.int32)
        spots = jnp.concatenate([(c * group + starts[k]) // 2 + steps for c in (core, core ^ 1)])
        return line(settle, spots.astype(jnp.int32), pair, kept, experts)

    inner = (meet(inner[:, :, 0]) / width)[:, :, None]
    d_raw, *d_one = line(
        raw_back, places, u, raw, scales, inner, own_gains, d_kv[1].astype(BF16), attn_w, tp
    )
    last = across(d_one[3], 1)
    grad_attn = line(qkv_grads, normed_one, d_raw, grad_attn, p)
    grad_attn = lax.psum_scatter(grad_attn, PLANE, scatter_dimension=0, tiled=False)
    pairs = [parted(0)]
    near = line(add, d_one[2], last)
    d_one = [d_one[0], across(d_one[1], 1), across(near, 2)]
    grad_in, gain_one = line(norm_one_back, d_one, x_q, d_mid, gains[0:1])
    far = across(grad_in, 2)
    near = across(grad_in, 1)
    placed = lax.dynamic_update_slice_in_dim(
        jnp.zeros((2, width), F32), gain_qk[:, 0, :], column * n, 1
    )

    small = line(lambda *v: jnp.concatenate(v, 0), grad_router[:experts], gain_one, gain_two, placed)
    rows = small.shape[0]
    small = small.reshape(rows, p, ds).transpose(1, 0, 2)
    small = jnp.sum(lax.all_to_all(small, PLANE, 0, 0, tiled=True), 0)
    other = across(small, 1)
    both = across(far, 1)
    kept = settled(0, pairs[0], [])
    placed_in = line(in_place, places[:2], [grad_in, near], [], t)
    pairs.append(parted(1))
    owned_gate_up, owned_down = settled(1, pairs[1], kept)
    small = line(lambda a, b: a + b, small, other)
    other = across(small, 2)
    grad_inputs = line(in_place, places[2:], [far, both], [placed_in], t).reshape(inputs.shape)
    grad_attn, grad_inputs = lax.optimization_barrier((grad_attn, grad_inputs))
    small = line(lambda a, b: a + b, small, other)
    owned_gains = small[experts:]
    owned_router = small[:experts].T
    return (
        outputs,
        grad_inputs,
        owned_gains,
        grad_attn[:3].astype(F32),
        grad_attn[3].astype(F32),
        owned_router,
        owned_gate_up,
        owned_down,
    )


def solution(mesh):
    fsdp, ctx, tp = (mesh.shape[a] for a in ("fsdp", "ctx", "tp"))
    fine = Mesh(mesh.devices.reshape(fsdp, ctx // 2, 2, tp), EVERY)
    tokens = P("fsdp", ("row", "core"), None)
    weights = (
        P(None, PLANE),
        P(None, PLANE, "tp"),
        P(PLANE, "tp"),
        P(PLANE, None),
        P(None, None, PLANE, "tp"),
        P(None, PLANE, "tp"),
    )
    return jax.shard_map(
        functools.partial(body, chunks=(6, 2)),
        mesh=fine,
        in_specs=(tokens, P("fsdp"), tokens) + weights + (tokens,),
        out_specs=(tokens, tokens) + weights,
        check_vma=False,
    )
```

```python
import functools

import jax
import jax.numpy as jnp
from jax import lax
from jax.experimental import pallas as pl
from jax.experimental.pallas import tpu as pltpu
from jax.sharding import Mesh, PartitionSpec as P

HEAD_DIM = 128
EPSILON = 1e-05
THETA = 10000.0
TILE = 256
F32 = jnp.float32
BF16 = jnp.bfloat16
FR = ("fsdp", "row")
LANES = 128
PLANE = ("fsdp", "row", "core")
EVERY = ("fsdp", "row", "core", "tp")


def nn(a, b):
    return lax.dot_general(a, b, (((1,), (0,)), ((), ())), preferred_element_type=F32)


def nt(a, b):
    return lax.dot_general(a, b, (((1,), (1,)), ((), ())), preferred_element_type=F32)


def tn(a, b):
    return lax.dot_general(a, b, (((0,), (0,)), ((), ())), preferred_element_type=F32)


def call(kernel, name, grid, in_specs, out_specs, out_shape, flops, moved, scratch=(), prefetch=0, limit=56, aliases=None):
    return pl.pallas_call(
        kernel,
        name=name,
        out_shape=out_shape,
        grid_spec=pltpu.PrefetchScalarGridSpec(
            num_scalar_prefetch=prefetch,
            grid=grid,
            in_specs=in_specs,
            out_specs=out_specs,
            scratch_shapes=list(scratch),
        ),
        input_output_aliases=aliases or {},
        compiler_params=pltpu.CompilerParams(
            dimension_semantics=("arbitrary",) * len(grid), vmem_limit_bytes=limit << 20
        ),
        cost_estimate=pl.CostEstimate(flops=int(flops), bytes_accessed=int(moved), transcendentals=0),
    )


def fixed(shape):
    return pl.BlockSpec(shape, lambda *a: (0,) * len(shape), pipeline_mode=pl.Buffered(1))


def sds(shape, dtype):
    return jax.ShapeDtypeStruct(shape, dtype)


def qkv_kernel(x_ref, g_ref, w_ref, n_ref, raw_ref, v_ref, sq_ref):
    c = pl.program_id(0)

    @pl.when(c == 0)
    def _():
        x = x_ref[...].astype(F32)
        r = lax.rsqrt(jnp.mean(x * x, -1, keepdims=True) + EPSILON)
        n_ref[...] = (x * r * g_ref[...]).astype(BF16)

    w = w_ref[...]
    y = nn(n_ref[...], w.reshape(w.shape[0] * w.shape[2], w.shape[3]))

    @pl.when(c < 2)
    def _():
        raw_ref[0] = y
        sq_ref[0] = jnp.broadcast_to(jnp.sum(y * y, -1, keepdims=True), sq_ref.shape[1:])

    @pl.when(c == 2)
    def _():
        v_ref[...] = y.astype(BF16)


def qkv_project(x, gain, w):
    t, d = x.shape
    p, _, ds, n = w.shape
    return call(
        qkv_kernel,
        "qkv",
        (3,),
        [
            fixed((t, d)),
            fixed((1, d)),
            pl.BlockSpec((p, 1, ds, n), lambda c: (0, c, 0, 0)),
        ],
        [
            pl.BlockSpec((t, d), lambda c: (0, 0)),
            pl.BlockSpec((1, t, n), lambda c: (jnp.minimum(c, 1), 0, 0)),
            pl.BlockSpec((t, n), lambda c: (0, 0)),
            pl.BlockSpec((1, t, 128), lambda c: (jnp.minimum(c, 1), 0, 0)),
        ],
        [sds((t, d), BF16), sds((2, t, n), F32), sds((t, n), BF16), sds((2, t, 128), F32)],
        6 * t * d * n,
        2 * (3 * d * n + 2 * t * d) + 10 * t * n,
    )(x, gain, w)


def turn(v, cosine, sine):
    half = v.shape[-1] // 2
    return v * cosine + pltpu.roll(v, half, 1) * sine


def prep_kernel(raw_ref, s_ref, g_ref, cos_ref, sin_ref, q_ref, k_ref):
    reps = raw_ref.shape[1] // cos_ref.shape[0]
    cosine = jnp.concatenate([cos_ref[...]] * reps, 0)
    sine = jnp.concatenate([sin_ref[...]] * reps, 0)
    q = raw_ref[0] * s_ref[0] * g_ref[0]
    k = raw_ref[1] * s_ref[1] * g_ref[1]
    q_ref[...] = turn(q, cosine, sine).astype(BF16)
    k_ref[...] = turn(k, cosine, sine).astype(BF16)


def prepare(raw, scales, gains, cosine, sine):
    _, t, n = raw.shape
    h = HEAD_DIM
    length = cosine.shape[0]
    return call(
        prep_kernel,
        "prep",
        (n // h,),
        [
            pl.BlockSpec((2, t, h), lambda i: (0, 0, i)),
            fixed((2, t, 1)),
            pl.BlockSpec((2, 1, h), lambda i: (0, 0, i)),
            fixed((length, h)),
            fixed((length, h)),
        ],
        [pl.BlockSpec((t, h), lambda i: (0, i))] * 2,
        [sds((t, n), BF16)] * 2,
        20 * t * n,
        12 * t * n,
    )(raw, scales, gains, cosine, sine)


def masked_probs(s, scal_ref, q, ks):
    length = q.shape[0]
    prefix = scal_ref[5 + s]
    rows = lax.broadcasted_iota(jnp.int32, (length, length), 0) + scal_ref[4]
    columns = lax.broadcasted_iota(jnp.int32, (length, length), 1)
    pieces = []
    for b, k in enumerate(ks):
        place = columns + scal_ref[b]
        visible = (place <= rows) | (place < prefix)
        pieces.append(jnp.where(visible, nt(q, k) * HEAD_DIM ** (-0.5), -1e30))
    scores = jnp.concatenate(pieces, 1)
    expo = jnp.exp(scores - jnp.max(scores, -1, keepdims=True))
    return expo / jnp.sum(expo, -1, keepdims=True)


def attend_kernel(scal_ref, q_ref, *refs):
    o_ref = refs[8]
    probs = masked_probs(pl.program_id(0), scal_ref, q_ref[...], [r[...] for r in refs[:4]])
    v = jnp.concatenate([r[...] for r in refs[4:8]], 0)
    o_ref[...] = nn(probs.astype(BF16), v).astype(BF16)


def attend(scal, q, blocks, length):
    t, n = q.shape
    h = HEAD_DIM
    one = pl.BlockSpec((length, h), lambda s, i, *_: (s, i))
    return call(
        attend_kernel,
        "attend",
        (t // length, n // h),
        [one] * 9,
        one,
        sds((t, n), BF16),
        16 * t * n * length,
        24 * t * n,
        prefetch=1,
    )(scal, q, *blocks)


def attend_back_kernel(scal_ref, q_ref, *refs):
    g_ref, dq_ref, outs = refs[8], refs[9], refs[10:]
    length = q_ref.shape[0]
    q = q_ref[...]
    grad = g_ref[...]
    probs = masked_probs(pl.program_id(0), scal_ref, q, [r[...] for r in refs[:4]])
    k = jnp.concatenate([r[...] for r in refs[:4]], 0)
    v = jnp.concatenate([r[...] for r in refs[4:8]], 0)
    d_probs = nt(grad, v)
    inner = jnp.sum(probs * d_probs, -1, keepdims=True)
    d_scores = (probs * (d_probs - inner)).astype(BF16)
    scale = HEAD_DIM ** (-0.5)
    dq_ref[...] = nn(d_scores, k) * scale
    dk = (tn(d_scores, q) * scale).astype(BF16)
    dv = tn(probs.astype(BF16), grad).astype(BF16)
    for b, o in enumerate(outs):
        o[0] = dk[b * length : (b + 1) * length]
        o[1] = dv[b * length : (b + 1) * length]


def attend_back(scal, q, blocks, grad, length):
    t, n = q.shape
    h = HEAD_DIM
    one = pl.BlockSpec((length, h), lambda s, i, *_: (s, i))
    two = pl.BlockSpec((2, length, h), lambda s, i, *_: (0, s, i))
    return call(
        attend_back_kernel,
        "attend_back",
        (t // length, n // h),
        [one] * 10,
        [one] + [two] * 4,
        [sds((t, n), F32)] + [sds((2, t, n), BF16)] * 4,
        40 * t * n * length,
        48 * t * n,
        prefetch=1,
    )(scal, q, *blocks, grad)


def out_kernel(place_ref, h_ref, w_ref, *outs):
    w = w_ref[...]
    w = w.reshape(-1, w.shape[-1])
    rows = outs[0].shape[0]
    heads = jnp.concatenate(
        [h_ref[pl.ds(pl.multiple_of(place_ref[r], rows), rows), :] for r in range(len(outs))], 0
    )
    y = nt(heads, w).astype(BF16)
    for r, o in enumerate(outs):
        o[...] = y[r * rows : (r + 1) * rows]


def project_out(places, heads, w, pieces):
    t, n = heads.shape
    p, _, ds, _ = w.shape
    pb = max(1, 2 * TILE // ds)
    return call(
        out_kernel,
        "outproj",
        (p // pb,),
        [fixed((t, n)), pl.BlockSpec((pb, 1, ds, n), lambda g, *_: (g, 3, 0, 0))],
        [pl.BlockSpec((t // pieces, pb * ds), lambda g, *_: (0, g))] * pieces,
        [sds((t // pieces, p * ds), BF16)] * pieces,
        2 * t * n * p * ds,
        2 * (t * n + n * p * ds + t * p * ds),
        prefetch=1,
    )(places, heads, w)


def d_heads_kernel(place_ref, g_ref, w_ref, o_ref, *, pieces):
    w = w_ref[...]
    y = nn(g_ref[...], w.reshape(w.shape[0] * w.shape[2], w.shape[3])).astype(BF16)
    rows = y.shape[0] // pieces
    for r in range(pieces):
        o_ref[pl.ds(pl.multiple_of(place_ref[r], rows), rows), :] = y[r * rows : (r + 1) * rows]


def heads_grad(places, grad, w, pieces):
    t, d = grad.shape
    p, _, ds, n = w.shape
    return call(
        functools.partial(d_heads_kernel, pieces=pieces),
        "dheads",
        (1,),
        [fixed((t, d)), pl.BlockSpec((p, 1, ds, n), lambda g, *_: (0, 3, 0, 0), pipeline_mode=pl.Buffered(1))],
        fixed((t, n)),
        sds((t, n), BF16),
        2 * t * n * d,
        2 * (t * n + n * d + t * d),
        prefetch=1,
    )(places, grad, w)


def grad_out_kernel(place_ref, g_ref, h_ref, o_ref, *, pieces):
    rows = g_ref.shape[0] // pieces
    heads = jnp.concatenate(
        [h_ref[pl.ds(pl.multiple_of(place_ref[r], rows), rows), :] for r in range(pieces)], 0
    )
    o_ref[...] = tn(g_ref[...], heads).astype(BF16).reshape(o_ref.shape)


def out_weight_grad(places, grad, heads, p, pieces):
    t, d = grad.shape
    n = heads.shape[1]
    ds = d // p
    pb = max(1, TILE // ds)
    return call(
        functools.partial(grad_out_kernel, pieces=pieces),
        "gradout",
        (p // pb,),
        [pl.BlockSpec((t, pb * ds), lambda g, *_: (0, g)), fixed((t, n))],
        pl.BlockSpec((pb, 1, ds, n), lambda g, *_: (g, 3, 0, 0)),
        sds((p, 4, ds, n), BF16),
        2 * t * n * d,
        2 * (t * n + n * d + t * d),
        prefetch=1,
    )(places, grad, heads)


def norm_two_kernel(x_ref, a_ref, b_ref, c_ref, g_ref, w_ref, ids_ref, mid_ref, ext_ref, probs_ref, chosen_ref, *, experts):
    mid = x_ref[...].astype(F32) + a_ref[...].astype(F32) + b_ref[...].astype(F32) + c_ref[...].astype(F32)
    mid_ref[...] = mid
    d = mid.shape[1]
    r = lax.rsqrt(jnp.mean(mid * mid, -1, keepdims=True) + EPSILON)
    low = (mid * r * g_ref[...]).astype(BF16)
    ext_ref[:, :d] = low
    logits = nt(low, w_ref[...])
    lane = lax.broadcasted_iota(jnp.int32, logits.shape, 1)
    logits = jnp.where(lane < experts, logits, -1e30)
    expo = jnp.exp(logits - jnp.max(logits, -1, keepdims=True))
    probs = expo / jnp.sum(expo, -1, keepdims=True)
    chosen = jnp.zeros_like(probs)
    for j in range(ids_ref.shape[1]):
        chosen += (ids_ref[:, j : j + 1] == lane).astype(F32)
    probs_ref[...] = probs
    chosen_ref[...] = chosen
    gates = probs * chosen
    high = gates.astype(BF16)
    rest = (gates - high.astype(F32)).astype(BF16)
    ext_ref[:, d:] = jnp.concatenate([high[:, : LANES // 2], rest[:, : LANES // 2]], 1)


def norm_two(x, sums, gain, router, ids, experts):
    t, d = x.shape
    return call(
        functools.partial(norm_two_kernel, experts=experts),
        "norm_two",
        (1,),
        [fixed((t, d))] * 4 + [fixed((1, d)), fixed(router.shape), fixed(ids.shape)],
        [fixed((t, d)), fixed((t, d + LANES)), fixed((t, LANES)), fixed((t, LANES))],
        [sds((t, d), F32), sds((t, d + LANES), BF16), sds((t, LANES), F32), sds((t, LANES), F32)],
        2 * t * d * LANES,
        14 * t * d,
    )(x, *sums, gain, router, ids)


def norm_two_back_kernel(a_ref, b_ref, c_ref, mid_ref, ext_ref, probs_ref, chosen_ref, cot_ref, g_ref, w_ref, *outs):
    mid_grad_ref, low_ref, gain_ref, router_ref = outs
    d = mid_ref.shape[1]
    du = a_ref[...].astype(F32) + b_ref[...].astype(F32) + c_ref[...].astype(F32)
    probs = probs_ref[...]
    masked = du[:, d:] * chosen_ref[...]
    d_logits = (probs * (masked - jnp.sum(probs * masked, -1, keepdims=True))).astype(BF16)
    router_ref[...] = tn(d_logits, ext_ref[:, :d])
    u = du[:, :d] + nn(d_logits, w_ref[...])
    mid = mid_ref[...]
    r = lax.rsqrt(jnp.mean(mid * mid, -1, keepdims=True) + EPSILON)
    hat = mid * r
    gain_ref[...] = jnp.sum(u * hat, 0, keepdims=True)
    w = u * g_ref[...]
    grad = cot_ref[...].astype(F32) + r * (w - hat * jnp.mean(w * hat, -1, keepdims=True))
    mid_grad_ref[...] = grad
    low_ref[...] = grad.astype(BF16)


def norm_two_back(sums, mid, ext, probs, chosen, cot, gain, router):
    t, d = mid.shape
    wide = fixed((t, d + LANES))
    return call(
        norm_two_back_kernel,
        "norm_two_back",
        (1,),
        [wide] * 3
        + [fixed((t, d)), wide, fixed((t, LANES)), fixed((t, LANES)), fixed((t, d)), fixed((1, d)), fixed(router.shape)],
        [fixed((t, d)), fixed((t, d)), fixed((1, d)), fixed((LANES, d))],
        [sds((t, d), F32), sds((t, d), BF16), sds((1, d), F32), sds((LANES, d), F32)],
        4 * t * d * LANES,
        20 * t * d,
    )(*sums, mid, ext, probs, chosen, cot, gain, router)


def norm_one_back_kernel(a_ref, b_ref, c_ref, x_ref, mid_grad_ref, g_ref, o_ref, gain_ref):
    u = a_ref[...].astype(F32) + b_ref[...].astype(F32) + c_ref[...].astype(F32)
    x = x_ref[...].astype(F32)
    r = lax.rsqrt(jnp.mean(x * x, -1, keepdims=True) + EPSILON)
    hat = x * r
    gain_ref[...] = jnp.sum(u * hat, 0, keepdims=True)
    w = u * g_ref[...]
    o_ref[...] = (mid_grad_ref[...] + r * (w - hat * jnp.mean(w * hat, -1, keepdims=True))).astype(BF16)


def norm_one_back(sums, x, mid_grad, gain):
    t, d = x.shape
    return call(
        norm_one_back_kernel,
        "norm_one_back",
        (1,),
        [fixed((t, d))] * 5 + [fixed((1, d))],
        [fixed((t, d)), fixed((1, d))],
        [sds((t, d), BF16), sds((1, d), F32)],
        20 * t * d,
        14 * t * d,
    )(*sums, x, mid_grad, gain)


def expert_kernel(first_ref, *refs, parts):
    xs, cs, w_ref = refs[:parts], refs[parts : 2 * parts], refs[2 * parts]
    hid_ref, dgu_ref, dg_ref = refs[2 * parts + 1 :]
    e = pl.program_id(0)
    t = cs[0].shape[0]
    d = cs[0].shape[1]

    @pl.when(e == 0)
    def _():
        dg_ref[...] = jnp.zeros_like(dg_ref)

    f = w_ref.shape[4]
    me = first_ref[0] + e
    lane = lax.broadcasted_iota(jnp.int32, (t, LANES), 1)
    for part, (x_ref, c_ref) in enumerate(zip(xs, cs)):

        def block(x_ref=x_ref, c_ref=c_ref, to=slice(part * t, (part + 1) * t)):
            x = x_ref[:, :d]
            a = nn(x, w_ref[:, 0, 0].reshape(d, f))
            b = nn(x, w_ref[:, 0, 1].reshape(d, f))
            dh = nn(c_ref[...], w_ref[:, 0, 2].reshape(d, f))
            mine = (lane == me) | (lane == me + LANES // 2)
            gate = jnp.sum(jnp.where(mine, x_ref[:, d:].astype(F32), 0.0), -1, keepdims=True)
            sigma = jax.nn.sigmoid(a)
            swish = a * sigma
            act = swish * b
            hid_ref[to, :] = (gate * act).astype(BF16)
            d_gate = jnp.sum(dh * act, -1, keepdims=True)
            dg_ref[to, :] += jnp.where(lane == me, d_gate, 0.0)
            inner = dh * gate
            dgu_ref[to, :f] = (inner * b * sigma * (1.0 + a * (1.0 - sigma))).astype(BF16)
            dgu_ref[to, f:] = (inner * swish).astype(BF16)

        block()


def expert_up(first, xs, cs, w):
    t, d = cs[0].shape
    parts = len(cs)
    p, e, _, ds, f = w.shape
    every = parts * t
    return call(
        functools.partial(expert_kernel, parts=parts),
        "expert_up",
        (e,),
        [fixed(x.shape) for x in xs]
        + [fixed((t, d))] * parts
        + [pl.BlockSpec((p, 1, 3, ds, f), lambda i, *_: (0, i, 0, 0, 0))],
        [
            pl.BlockSpec((every, f), lambda i, *_: (0, i)),
            pl.BlockSpec((every, 2 * f), lambda i, *_: (0, i)),
            pl.BlockSpec((every, LANES), lambda i, *_: (0, 0)),
        ],
        [sds((every, e * f), BF16), sds((every, e * 2 * f), BF16), sds((every, LANES), F32)],
        6 * every * d * f * e,
        2 * (3 * d * f * e + 2 * every * d + 3 * every * f * e),
        prefetch=1,
    )(first, *xs, *cs, w)


def expert_grad_kernel(*refs, parts):
    xs, cs, hid_ref, dgu_ref, o_ref = refs[:parts], refs[parts : 2 * parts], *refs[2 * parts :]
    pb, e, _, ds, f = o_ref.shape
    x = jnp.concatenate([r[...] for r in xs], 0)
    c = jnp.concatenate([r[...] for r in cs], 0)
    both = tn(x, dgu_ref[...]).astype(BF16)
    down = tn(c, hid_ref[...]).astype(BF16)
    for i in range(e):
        o_ref[:, i, 0] = both[:, 2 * i * f : (2 * i + 1) * f].reshape(pb, ds, f)
        o_ref[:, i, 1] = both[:, (2 * i + 1) * f : (2 * i + 2) * f].reshape(pb, ds, f)
        o_ref[:, i, 2] = down[:, i * f : (i + 1) * f].reshape(pb, ds, f)


def expert_grads(xs, cs, hid, dgu, p, e):
    t, d = cs[0].shape
    parts = len(cs)
    ds = d // p
    f = hid.shape[1] // e
    pb = max(1, TILE // ds)
    column = pl.BlockSpec((t, pb * ds), lambda g: (0, g))
    return call(
        functools.partial(expert_grad_kernel, parts=parts),
        "expert_grad",
        (p // pb,),
        [column] * (2 * parts) + [fixed(hid.shape), fixed(dgu.shape)],
        pl.BlockSpec((pb, e, 3, ds, f), lambda g: (g, 0, 0, 0, 0)),
        sds((p, e, 3, ds, f), BF16),
        6 * parts * t * d * f * e,
        2 * (3 * d * f * e + 2 * parts * t * d + 3 * parts * t * f * e),
    )(*xs, *cs, hid, dgu)


def settle_kernel(spot_ref, *refs, pieces):
    gate_up_ref, down_ref = refs[-2:]
    each = pl.num_programs(0) // pieces
    for r in range(pieces):

        @pl.when(pl.program_id(0) // each == r)
        def _():
            gate_up_ref[...] = refs[r][:, :2].astype(F32)
            down_ref[...] = refs[r][:, 2].astype(F32)


def settle(spots, pieces, kept, experts):
    e, _, ds, f = pieces[0].shape
    count = len(pieces)
    each = e // 2

    def piece(r):
        return pl.BlockSpec((2, 3, ds, f), lambda g, spot: (jnp.clip(g - r * each, 0, each - 1), 0, 0, 0))

    return call(
        functools.partial(settle_kernel, pieces=count),
        "settle",
        (count * each,),
        [piece(r) for r in range(count)] + [pl.BlockSpec(memory_space=pl.ANY)] * len(kept),
        [
            pl.BlockSpec((2, 2, ds, f), lambda g, spot: (spot[g], 0, 0, 0)),
            pl.BlockSpec((2, ds, f), lambda g, spot: (spot[g], 0, 0)),
        ],
        [sds((experts, 2, ds, f), F32), sds((experts, ds, f), F32)],
        0,
        18 * count * e * ds * f,
        prefetch=1,
        aliases={1 + count + i: i for i in range(len(kept))},
    )(spots, *pieces, *kept)


def down_kernel(*refs, planes, chunks, sides, begun):
    acts, ws = refs[:chunks], refs[chunks : 2 * chunks]
    gates = refs[2 * chunks : 2 * chunks + sides]
    before = refs[2 * chunks + sides : 2 * chunks + sides + begun]
    outs = refs[2 * chunks + sides + begun :]
    g = pl.program_id(0)
    pb, _, _, ds, f = ws[0].shape
    wide = pb * ds
    rows = outs[0].shape[0]
    joined = [
        jnp.concatenate([w[:, i, c].reshape(wide, f) for i in range(w.shape[1]) for c in range(planes)], 1)
        for w in ws
    ]
    to = pl.ds(pl.multiple_of(g * wide, wide), wide)
    for part, o in enumerate(outs):
        own = slice(part * rows, (part + 1) * rows)
        value = sum(nt(a[own, :], w) for a, w in zip(acts, joined))
        if begun:
            value += before[part][...].astype(F32)
        o[:, to] = value.astype(BF16)
    if sides:

        @pl.when(g == 0)
        def _():
            for part, o in enumerate(outs):
                own = slice(part * rows, (part + 1) * rows)
                o[:, o.shape[1] - LANES :] = sum(s[own, :] for s in gates).astype(BF16)


def expert_down(acts, ws, plane, planes, gates, before, parts, name):
    every = acts[0].shape[0]
    p, _, _, ds, f = ws[0].shape
    k = sum(a.shape[1] for a in acts)
    t = every // parts
    chunks = len(acts)
    d = p * ds + (LANES if gates else 0)
    pb = max(1, 2 * TILE // ds)
    return call(
        functools.partial(down_kernel, planes=planes, chunks=chunks, sides=len(gates), begun=len(before)),
        name,
        (p // pb,),
        [fixed(a.shape) for a in acts]
        + [pl.BlockSpec((pb, w.shape[1], planes, ds, f), lambda g: (g, 0, plane, 0, 0)) for w in ws]
        + [fixed((every, LANES))] * len(gates)
        + [pl.BlockSpec((t, pb * ds), lambda g: (0, g))] * len(before),
        [pl.BlockSpec((t, d), lambda g: (0, 0))] * parts,
        [sds((t, d), BF16)] * parts,
        2 * every * k * p * ds,
        2 * (every * k + k * p * ds) + 2 * every * d,
    )(*acts, *ws, *gates, *before)


def unturn_kernel(dq_ref, dk_ref, raw_ref, s_ref, g_ref, cos_ref, sin_ref, u_ref, in_ref, gg_ref):
    h = pl.program_id(0)
    reps = raw_ref.shape[1] // cos_ref.shape[0]
    cosine = jnp.concatenate([cos_ref[...]] * reps, 0)
    sine = jnp.concatenate([sin_ref[...]] * reps, 0)
    for i, grad in enumerate((dq_ref[...], dk_ref[...])):
        u = turn(grad, cosine, -sine)
        hat = raw_ref[i] * s_ref[i]
        product = u * hat
        u_ref[i] = u
        gg_ref[i] = jnp.sum(product, 0, keepdims=True)
        row = jnp.broadcast_to(jnp.sum(product * g_ref[i], -1, keepdims=True), in_ref.shape[1:])

        @pl.when(h == 0)
        def _():
            in_ref[i] = row

        @pl.when(h != 0)
        def _():
            in_ref[i] += row


def unturn(dq, dk, raw, scales, gains, cosine, sine):
    _, t, n = raw.shape
    h = HEAD_DIM
    length = cosine.shape[0]
    column = pl.BlockSpec((t, h), lambda i: (0, i))
    pair = pl.BlockSpec((2, t, h), lambda i: (0, 0, i))
    return call(
        unturn_kernel,
        "unturn",
        (n // h,),
        [
            column,
            column,
            pair,
            fixed((2, t, 1)),
            pl.BlockSpec((2, 1, h), lambda i: (0, 0, i)),
            fixed((length, h)),
            fixed((length, h)),
        ],
        [
            pair,
            pl.BlockSpec((2, t, 128), lambda i: (0, 0, 0)),
            pl.BlockSpec((2, 1, h), lambda i: (0, 0, i)),
        ],
        [sds((2, t, n), F32), sds((2, t, 128), F32), sds((2, 1, n), F32)],
        30 * t * n,
        24 * t * n,
    )(dq, dk, raw, scales, gains, cosine, sine)


def raw_back_kernel(place_ref, u_ref, raw_ref, s_ref, in_ref, g_ref, dv_ref, w_ref, d_ref, *outs):
    t, n = dv_ref.shape

    @pl.when(pl.program_id(0) == 0)
    def _():
        for i in range(2):
            hat = raw_ref[i] * s_ref[i]
            d_ref[:, i * n : (i + 1) * n] = (
                s_ref[i] * (u_ref[i] * g_ref[i] - hat * in_ref[i])
            ).astype(BF16)
        d_ref[:, 2 * n :] = dv_ref[...]

    pb, _, ds, _ = w_ref.shape
    w = jnp.concatenate([w_ref[:, c].reshape(pb * ds, n) for c in range(3)], 1)
    y = nt(d_ref[...], w).astype(BF16)
    rows = outs[0].shape[0]
    outs[0][...] = y[:rows]
    for r, o in enumerate(outs):
        for q in range(len(outs)):

            @pl.when(place_ref[r] == q * rows)
            def _():
                o[...] = y[q * rows : (q + 1) * rows]


def raw_back(places, u, raw, scales, inner, gains, dv, w, pieces):
    t, n = dv.shape
    p, _, ds, _ = w.shape
    d = p * ds
    pb = max(1, 2 * TILE // ds)
    return call(
        raw_back_kernel,
        "raw_back",
        (p // pb,),
        [
            fixed((2, t, n)),
            fixed((2, t, n)),
            fixed((2, t, 1)),
            fixed((2, t, 1)),
            fixed((2, 1, n)),
            fixed((t, n)),
            pl.BlockSpec((pb, 3, ds, n), lambda g, *_: (g, 0, 0, 0)),
        ],
        [pl.BlockSpec((t, 3 * n), lambda g, *_: (0, 0))]
        + [pl.BlockSpec((t // pieces, pb * ds), lambda g, *_: (0, g))] * pieces,
        [sds((t, 3 * n), BF16)] + [sds((t // pieces, d), BF16)] * pieces,
        6 * t * d * n,
        2 * (3 * d * n + t * d) + 20 * t * n,
        prefetch=1,
    )(places, u, raw, scales, inner, gains, dv, w)


def qkv_grad_kernel(n_ref, d_ref, kept_ref, o_ref):
    pb, _, ds, n = o_ref.shape
    grads = tn(n_ref[...], d_ref[...]).astype(BF16)
    for c in range(3):
        o_ref[:, c] = grads[:, c * n : (c + 1) * n].reshape(pb, ds, n)


def qkv_grads(normed, grad, kept, p):
    t, d = normed.shape
    n = grad.shape[1] // 3
    ds = d // p
    pb = max(1, TILE // ds)
    return call(
        qkv_grad_kernel,
        "qkv_grad",
        (p // pb,),
        [
            pl.BlockSpec((t, pb * ds), lambda g: (0, g)),
            fixed((t, 3 * n)),
            pl.BlockSpec(memory_space=pl.ANY),
        ],
        pl.BlockSpec((pb, 3, ds, n), lambda g: (g, 0, 0, 0)),
        sds(kept.shape, BF16),
        6 * t * d * n,
        2 * (3 * d * n + t * d + 3 * t * n),
        aliases={2: 0},
    )(normed, grad, kept)


def swap(value, axis):
    return lax.ppermute(value, axis, [(0, 1), (1, 0)])


def spread(value):
    rows = swap(value, "row")
    return (value, swap(value, "core"), rows, swap(rows, "core"))


def across(value, k):
    size = lax.axis_size("tp")
    return lax.ppermute(value, "tp", [(i, i ^ k) for i in range(size)])


def total(pieces):
    return sum(v.astype(F32) for v in pieces)


def add(*values):
    return total(values).astype(values[0].dtype)


def cut(value, pieces):
    rows = value.shape[0] // pieces
    return [value[r * rows : (r + 1) * rows] for r in range(pieces)]


def join(*pieces):
    return jnp.concatenate(pieces, 0)


class Line:
    def __init__(self):
        self.last = None

    def __call__(self, step, *operands):
        leaves, form = jax.tree.flatten(operands)
        spots = [i for i, v in enumerate(leaves) if isinstance(v, jax.Array)]
        if self.last is not None:
            kept, self.last = lax.optimization_barrier(([leaves[i] for i in spots], self.last))
            for i, v in zip(spots, kept):
                leaves[i] = v
        result = step(*jax.tree.unflatten(form, leaves))
        self.last = jax.tree.leaves(result)
        return result

    def sums(self, own, core, pieces, first=None):
        mine, theirs = cut(own, pieces), cut(swap(core, "core"), pieces)
        last = across(self(add, mine[3], theirs[3]), 1)
        near = self(add, mine[2], theirs[2], last)
        beside, first = self(lambda a, b, c, d: (add(a, b), add(c, d)), mine[1], theirs[1], mine[0], theirs[0])
        return [first, across(beside, 1), across(near, 2)]


def in_place_kernel(place_ref, *refs, count):
    for r, piece in enumerate(refs[:count]):

        @pl.when(pl.program_id(0) == r)
        def _():
            refs[-1][...] = piece[...]


def in_place(places, pieces, kept, total_rows):
    rows, d = pieces[0].shape
    count = len(pieces)
    return call(
        functools.partial(in_place_kernel, count=count),
        "inplace",
        (count,),
        [fixed((rows, d))] * count + [pl.BlockSpec(memory_space=pl.ANY)] * len(kept),
        pl.BlockSpec((rows, d), lambda r, place: (place[r] // rows, 0)),
        sds((total_rows, d), pieces[0].dtype),
        0,
        4 * rows * count * d,
        prefetch=1,
        aliases={1 + count: 0} if kept else None,
    )(places, *pieces, *kept)


def meet(value):
    value = value + across(value, 1)
    return value + across(value, 2)


def relative(value, places, pieces):
    rows = value.shape[0] // pieces
    return [lax.dynamic_slice_in_dim(value, places[r], rows, 0) for r in range(pieces)]


def body(
    inputs,
    prefix,
    expert_ids,
    norm_gains,
    qkv_weight,
    out_weight,
    router_weight,
    gate_up_weight,
    down_weight,
    cotangent,
    *,
    chunks,
):
    sequences, length, width = inputs.shape
    t = sequences * length
    tp = lax.axis_size("tp")
    quarter = t // tp
    column = lax.axis_index("tp")
    core = lax.axis_index("core")
    ctx = lax.axis_index("row") * 2 + core
    experts = router_weight.shape[1]
    group = experts // 2
    starts = [sum(chunks[:k]) for k in range(len(chunks))]
    x = inputs.reshape(t, width)
    places = jnp.stack([column ^ r for r in range(tp)]).astype(jnp.int32) * quarter
    x_q = lax.dynamic_slice_in_dim(x, column * quarter, quarter, 0)

    line = Line()
    attn_local = jnp.concatenate([qkv_weight, out_weight[None]], 0)
    attn_w = lax.all_gather(attn_local, PLANE, axis=0, tiled=False)
    triple = jnp.concatenate([gate_up_weight, down_weight[:, None]], 1)
    ds, f = triple.shape[2:]
    grouped = triple.reshape(2, group, 3, ds, f)
    ws = []
    for begin, e in zip(starts, chunks):
        mine = lax.all_to_all(grouped[:, begin : begin + e], "core", 0, 0, tiled=True)
        ws.append(lax.all_gather(mine, FR, axis=0, tiled=False).reshape(-1, e, 3, ds, f))
    gains_low = lax.all_gather(norm_gains, PLANE, axis=1, tiled=True)
    router = lax.all_gather(router_weight, PLANE, axis=0, tiled=True)
    cots = relative(cotangent.reshape(t, width), places, tp)
    c0 = join(*cots)
    c1 = swap(c0, "core")
    attn_w, gains_low, router, c0 = lax.optimization_barrier((attn_w, gains_low, router, c0))
    p = attn_w.shape[0]

    gains = gains_low.astype(F32)
    n = attn_w.shape[3]
    router_rows = jnp.concatenate([router.T, jnp.zeros((128 - experts, width), BF16)], 0)

    own_gains = lax.dynamic_slice_in_dim(gains[2:4], column * n, n, 1)[:, None, :]
    halves = jnp.arange(0, HEAD_DIM, 2).astype(F32) / HEAD_DIM
    inverse = 1.0 / THETA**halves
    positions = ctx * length + jnp.arange(length, dtype=jnp.int32)
    angles = positions.astype(F32)[:, None] * inverse[None, :]
    cosine = jnp.concatenate([jnp.cos(angles)] * 2, 1)
    sine = jnp.concatenate([-jnp.sin(angles), jnp.sin(angles)], 1)
    offsets = jnp.stack([ctx, ctx ^ 1, ctx ^ 2, ctx ^ 3, ctx]).astype(jnp.int32) * length
    scal = jnp.concatenate([offsets, prefix.astype(jnp.int32)])
    ids_q = lax.dynamic_slice_in_dim(expert_ids.reshape(t, -1), column * quarter, quarter, 0)
    normed_one, raw, values, squares = line(qkv_project, x, gains[0:1], attn_w)
    v_blocks = spread(values)
    scales = lax.rsqrt(meet(squares[:, :, 0]) / width + EPSILON)[:, :, None]
    scales, values = lax.optimization_barrier((scales, v_blocks[2]))
    v_blocks = v_blocks[:2] + (values,) + v_blocks[3:]
    queries, keys = line(prepare, raw, scales, own_gains, cosine, sine)
    k_blocks = spread(keys)
    blocks = k_blocks + v_blocks
    heads = line(attend, scal, queries, blocks, length)
    sums = line(project_out, places, heads, attn_w, tp)
    near = line(add, sums[2], across(sums[3], 1))
    sums = [sums[0], across(sums[1], 1), across(near, 2)]
    mid, ext, probs, chosen = line(norm_two, x_q, sums, gains[1:2], router_rows, ids_q, experts)
    far = across(ext, 2)
    near = across(ext, 1)
    x0 = line(join, ext, near, far, across(far, 1))
    x1 = swap(x0, "core")

    xs, cs = [x0, x1], [c0, c1]
    blocks_in = jnp.arange(width // TILE, dtype=jnp.int32)
    hid, dgu, side, grads = [], [], [], []
    dx = []

    def up(k):
        first = (core * group + starts[k]).astype(jnp.int32)[None]
        for kept, made in zip((hid, dgu, side), line(expert_up, first, xs, cs, ws[k])):
            kept.append(made)

    def back(k, before):
        gates = side if k == len(chunks) - 1 else []
        return line(expert_down, [dgu[k]], [ws[k]], 0, 2, gates, before, 2, "expert_dx")

    def weight_grad(k):
        return line(expert_grads, xs, cs, hid[k], dgu[k], p, chunks[k])

    def to_owners(made, k, after):
        made, after = lax.optimization_barrier((made, after))
        made = made.reshape(-1, 2, chunks[k], 3, ds, f)
        return lax.optimization_barrier(lax.psum_scatter(made, FR, scatter_dimension=0, tiled=False))

    for k in range(len(chunks)):
        up(k)
        dx = back(k, dx)
        if k < len(chunks) - 1:
            made = weight_grad(k)
            grads.append(to_owners(made, k, ()))
    d_normed = line.sums(*dx, tp)
    moe = line(expert_down, hid, ws, 2, 1, [], [], 2, "expert_out")
    late = weight_grad(len(chunks) - 1)

    d_mid, d_mid_low, gain_two, grad_router = line(
        norm_two_back, d_normed, mid, ext, probs, chosen, cots[0], gains[1:2], router_rows
    )
    far = across(d_mid_low, 2)
    near = across(d_mid_low, 1)
    d_mid_low = line(join, d_mid_low, near, far, across(far, 1))
    own, beside = cut(moe[0], tp), cut(swap(moe[1], "core"), tp)
    last = across(line(add, own[3], beside[3]), 1)

    d_heads = line(heads_grad, places, d_mid_low, attn_w, tp)
    grads.append(to_owners(late, len(chunks) - 1, d_heads))
    dq, b0, b1, b2, b3 = line(attend_back, scal, queries, blocks, d_heads, length)
    r1 = swap(b1, "core")
    r3 = swap(b3, "core")
    near = line(add, own[2], beside[2], last)
    next_one = line(add, own[1], beside[1])
    moe = [across(next_one, 1), across(near, 2)]
    r2 = swap(line(add, b2, r3), "row")
    grad_attn = line(out_weight_grad, places, d_mid_low, heads, p, tp)
    out = line(lambda *v: total(v).astype(BF16), mid, own[0], beside[0], *moe)
    out_far = across(out, 2)
    out_near = across(out, 1)
    def parted(k):
        own, other = line(
            lambda v: [lax.dynamic_index_in_dim(v, c, 0, keepdims=False) for c in (core, core ^ 1)], grads[k]
        )
        return own, swap(other, "core")

    def settled(k, pair, kept):
        steps = jnp.arange(chunks[k] // 2, dtype=jnp.int32)
        spots = jnp.concatenate([(c * group + starts[k]) // 2 + steps for c in (core, core ^ 1)])
        return line(settle, spots.astype(jnp.int32), pair, kept, experts)

    pairs = [parted(0)]
    d_kv = line(lambda *v: total(v), b0, r1, r2)
    out_far, d_kv = lax.optimization_barrier((out_far, d_kv))
    out_both = across(out_far, 1)
    u, inner, gain_qk = line(unturn, dq, d_kv[0], raw, scales, own_gains, cosine, sine)
    outputs = line(in_place, places, [out, out_near, out_far, out_both], [], t).reshape(inputs.shape)

    inner = (meet(inner[:, :, 0]) / width)[:, :, None]
    d_raw, *d_one = line(
        raw_back, places, u, raw, scales, inner, own_gains, d_kv[1].astype(BF16), attn_w, tp
    )
    last = across(d_one[3], 1)
    grad_attn = line(qkv_grads, normed_one, d_raw, grad_attn, p)
    grad_attn = grad_attn.reshape((-1, 2) + grad_attn.shape[1:])
    theirs = line(lambda v: lax.dynamic_index_in_dim(v, core ^ 1, 1, keepdims=False), grad_attn)
    theirs = swap(theirs, "core")
    near = line(add, d_one[2], last)
    d_one = [d_one[0], across(d_one[1], 1), across(near, 2)]
    grad_attn = line(
        lambda v, w: add(lax.dynamic_index_in_dim(v, core, 1, keepdims=False), w), grad_attn, theirs
    )
    grad_in, gain_one = line(norm_one_back, d_one, x_q, d_mid, gains[0:1])
    grad_attn, gain_one = lax.optimization_barrier((grad_attn, gain_one))
    grad_attn = lax.optimization_barrier(lax.psum_scatter(grad_attn, FR, scatter_dimension=0, tiled=False))
    far = across(grad_in, 2)
    placed = lax.dynamic_update_slice_in_dim(
        jnp.zeros((2, width), F32), gain_qk[:, 0, :], column * n, 1
    )

    small = line(lambda *v: jnp.concatenate(v, 0), grad_router[:experts], gain_one, gain_two, placed)
    near, small = lax.optimization_barrier((grad_in, small))
    near = across(near, 1)
    rows = small.shape[0]
    small = small.reshape(rows, p, ds).transpose(1, 0, 2)
    small = jnp.sum(lax.all_to_all(small, PLANE, 0, 0, tiled=True), 0)
    other = across(small, 1)
    both = across(far, 1)
    kept = settled(0, pairs[0], [])
    placed_in = line(in_place, places[:2], [grad_in, near], [], t)
    pairs.append(parted(1))
    owned_gate_up, owned_down = settled(1, pairs[1], kept)
    small = line(lambda a, b: a + b, small, other)
    other = across(small, 2)
    grad_inputs = line(in_place, places[2:], [far, both], [placed_in], t).reshape(inputs.shape)
    grad_attn, grad_inputs = lax.optimization_barrier((grad_attn, grad_inputs))
    small = line(lambda a, b: a + b, small, other)
    owned_gains = small[experts:]
    owned_router = small[:experts].T
    return (
        outputs,
        grad_inputs,
        owned_gains,
        grad_attn[:3].astype(F32),
        grad_attn[3].astype(F32),
        owned_router,
        owned_gate_up,
        owned_down,
    )


def solution(mesh):
    fsdp, ctx, tp = (mesh.shape[a] for a in ("fsdp", "ctx", "tp"))
    fine = Mesh(mesh.devices.reshape(fsdp, ctx // 2, 2, tp), EVERY)
    tokens = P("fsdp", ("row", "core"), None)
    weights = (
        P(None, PLANE),
        P(None, PLANE, "tp"),
        P(PLANE, "tp"),
        P(PLANE, None),
        P(None, None, PLANE, "tp"),
        P(None, PLANE, "tp"),
    )
    return jax.shard_map(
        functools.partial(body, chunks=(6, 2)),
        mesh=fine,
        in_specs=(tokens, P("fsdp"), tokens) + weights + (tokens,),
        out_specs=(tokens, tokens) + weights,
        check_vma=False,
    )
```

```python
import functools

import jax
import jax.numpy as jnp
from jax import lax
from jax.experimental import pallas as pl
from jax.experimental.pallas import tpu as pltpu
from jax.sharding import Mesh, PartitionSpec as P

HEAD_DIM = 128
EPSILON = 1e-05
THETA = 10000.0
TILE = 256
F32 = jnp.float32
BF16 = jnp.bfloat16
FR = ("fsdp", "row")
LANES = 128
PLANE = ("fsdp", "row", "core")
EVERY = ("fsdp", "row", "core", "tp")


def nn(a, b):
    return lax.dot_general(a, b, (((1,), (0,)), ((), ())), preferred_element_type=F32)


def nt(a, b):
    return lax.dot_general(a, b, (((1,), (1,)), ((), ())), preferred_element_type=F32)


def tn(a, b):
    return lax.dot_general(a, b, (((0,), (0,)), ((), ())), preferred_element_type=F32)


def call(kernel, name, grid, in_specs, out_specs, out_shape, flops, moved, scratch=(), prefetch=0, limit=56, aliases=None):
    return pl.pallas_call(
        kernel,
        name=name,
        out_shape=out_shape,
        grid_spec=pltpu.PrefetchScalarGridSpec(
            num_scalar_prefetch=prefetch,
            grid=grid,
            in_specs=in_specs,
            out_specs=out_specs,
            scratch_shapes=list(scratch),
        ),
        input_output_aliases=aliases or {},
        compiler_params=pltpu.CompilerParams(
            dimension_semantics=("arbitrary",) * len(grid), vmem_limit_bytes=limit << 20
        ),
        cost_estimate=pl.CostEstimate(flops=int(flops), bytes_accessed=int(moved), transcendentals=0),
    )


def fixed(shape):
    return pl.BlockSpec(shape, lambda *a: (0,) * len(shape), pipeline_mode=pl.Buffered(1))


def sds(shape, dtype):
    return jax.ShapeDtypeStruct(shape, dtype)


def qkv_kernel(x_ref, g_ref, w_ref, n_ref, raw_ref, v_ref, sq_ref):
    c = pl.program_id(0)

    @pl.when(c == 0)
    def _():
        x = x_ref[...].astype(F32)
        r = lax.rsqrt(jnp.mean(x * x, -1, keepdims=True) + EPSILON)
        n_ref[...] = (x * r * g_ref[...]).astype(BF16)

    w = w_ref[...]
    y = nn(n_ref[...], w.reshape(w.shape[0] * w.shape[2], w.shape[3]))

    @pl.when(c < 2)
    def _():
        raw_ref[0] = y
        sq_ref[0] = jnp.broadcast_to(jnp.sum(y * y, -1, keepdims=True), sq_ref.shape[1:])

    @pl.when(c == 2)
    def _():
        v_ref[...] = y.astype(BF16)


def qkv_project(x, gain, w):
    t, d = x.shape
    p, _, ds, n = w.shape
    return call(
        qkv_kernel,
        "qkv",
        (3,),
        [
            fixed((t, d)),
            fixed((1, d)),
            pl.BlockSpec((p, 1, ds, n), lambda c: (0, c, 0, 0)),
        ],
        [
            pl.BlockSpec((t, d), lambda c: (0, 0)),
            pl.BlockSpec((1, t, n), lambda c: (jnp.minimum(c, 1), 0, 0)),
            pl.BlockSpec((t, n), lambda c: (0, 0)),
            pl.BlockSpec((1, t, 128), lambda c: (jnp.minimum(c, 1), 0, 0)),
        ],
        [sds((t, d), BF16), sds((2, t, n), F32), sds((t, n), BF16), sds((2, t, 128), F32)],
        6 * t * d * n,
        2 * (3 * d * n + 2 * t * d) + 10 * t * n,
    )(x, gain, w)


def turn(v, cosine, sine):
    half = v.shape[-1] // 2
    return v * cosine + pltpu.roll(v, half, 1) * sine


def prep_kernel(raw_ref, s_ref, g_ref, cos_ref, sin_ref, q_ref, k_ref):
    reps = raw_ref.shape[1] // cos_ref.shape[0]
    cosine = jnp.concatenate([cos_ref[...]] * reps, 0)
    sine = jnp.concatenate([sin_ref[...]] * reps, 0)
    q = raw_ref[0] * s_ref[0] * g_ref[0]
    k = raw_ref[1] * s_ref[1] * g_ref[1]
    q_ref[...] = turn(q, cosine, sine).astype(BF16)
    k_ref[...] = turn(k, cosine, sine).astype(BF16)


def prepare(raw, scales, gains, cosine, sine):
    _, t, n = raw.shape
    h = HEAD_DIM
    length = cosine.shape[0]
    return call(
        prep_kernel,
        "prep",
        (n // h,),
        [
            pl.BlockSpec((2, t, h), lambda i: (0, 0, i)),
            fixed((2, t, 1)),
            pl.BlockSpec((2, 1, h), lambda i: (0, 0, i)),
            fixed((length, h)),
            fixed((length, h)),
        ],
        [pl.BlockSpec((t, h), lambda i: (0, i))] * 2,
        [sds((t, n), BF16)] * 2,
        20 * t * n,
        12 * t * n,
    )(raw, scales, gains, cosine, sine)


def masked_probs(s, scal_ref, q, ks):
    length = q.shape[0]
    prefix = scal_ref[5 + s]
    rows = lax.broadcasted_iota(jnp.int32, (length, length), 0) + scal_ref[4]
    columns = lax.broadcasted_iota(jnp.int32, (length, length), 1)
    pieces = []
    for b, k in enumerate(ks):
        place = columns + scal_ref[b]
        visible = (place <= rows) | (place < prefix)
        pieces.append(jnp.where(visible, nt(q, k) * HEAD_DIM ** (-0.5), -1e30))
    scores = jnp.concatenate(pieces, 1)
    expo = jnp.exp(scores - jnp.max(scores, -1, keepdims=True))
    return expo / jnp.sum(expo, -1, keepdims=True)


def attend_kernel(scal_ref, q_ref, *refs):
    o_ref = refs[8]
    probs = masked_probs(pl.program_id(0), scal_ref, q_ref[...], [r[...] for r in refs[:4]])
    v = jnp.concatenate([r[...] for r in refs[4:8]], 0)
    o_ref[...] = nn(probs.astype(BF16), v).astype(BF16)


def attend(scal, q, blocks, length):
    t, n = q.shape
    h = HEAD_DIM
    one = pl.BlockSpec((length, h), lambda s, i, *_: (s, i))
    return call(
        attend_kernel,
        "attend",
        (t // length, n // h),
        [one] * 9,
        one,
        sds((t, n), BF16),
        16 * t * n * length,
        24 * t * n,
        prefetch=1,
    )(scal, q, *blocks)


def attend_back_kernel(scal_ref, q_ref, *refs):
    g_ref, dq_ref, outs = refs[8], refs[9], refs[10:]
    length = q_ref.shape[0]
    q = q_ref[...]
    grad = g_ref[...]
    probs = masked_probs(pl.program_id(0), scal_ref, q, [r[...] for r in refs[:4]])
    k = jnp.concatenate([r[...] for r in refs[:4]], 0)
    v = jnp.concatenate([r[...] for r in refs[4:8]], 0)
    d_probs = nt(grad, v)
    inner = jnp.sum(probs * d_probs, -1, keepdims=True)
    d_scores = (probs * (d_probs - inner)).astype(BF16)
    scale = HEAD_DIM ** (-0.5)
    dq_ref[...] = nn(d_scores, k) * scale
    dk = (tn(d_scores, q) * scale).astype(BF16)
    dv = tn(probs.astype(BF16), grad).astype(BF16)
    for b, o in enumerate(outs):
        o[0] = dk[b * length : (b + 1) * length]
        o[1] = dv[b * length : (b + 1) * length]


def attend_back(scal, q, blocks, grad, length):
    t, n = q.shape
    h = HEAD_DIM
    one = pl.BlockSpec((length, h), lambda s, i, *_: (s, i))
    two = pl.BlockSpec((2, length, h), lambda s, i, *_: (0, s, i))
    return call(
        attend_back_kernel,
        "attend_back",
        (t // length, n // h),
        [one] * 10,
        [one] + [two] * 4,
        [sds((t, n), F32)] + [sds((2, t, n), BF16)] * 4,
        40 * t * n * length,
        48 * t * n,
        prefetch=1,
    )(scal, q, *blocks, grad)


def out_kernel(place_ref, h_ref, w_ref, *outs):
    w = w_ref[...]
    w = w.reshape(-1, w.shape[-1])
    rows = outs[0].shape[0]
    heads = jnp.concatenate(
        [h_ref[pl.ds(pl.multiple_of(place_ref[r], rows), rows), :] for r in range(len(outs))], 0
    )
    y = nt(heads, w).astype(BF16)
    for r, o in enumerate(outs):
        o[...] = y[r * rows : (r + 1) * rows]


def project_out(places, heads, w, pieces):
    t, n = heads.shape
    p, _, ds, _ = w.shape
    pb = max(1, 2 * TILE // ds)
    return call(
        out_kernel,
        "outproj",
        (p // pb,),
        [fixed((t, n)), pl.BlockSpec((pb, 1, ds, n), lambda g, *_: (g, 3, 0, 0))],
        [pl.BlockSpec((t // pieces, pb * ds), lambda g, *_: (0, g))] * pieces,
        [sds((t // pieces, p * ds), BF16)] * pieces,
        2 * t * n * p * ds,
        2 * (t * n + n * p * ds + t * p * ds),
        prefetch=1,
    )(places, heads, w)


def d_heads_kernel(place_ref, g_ref, w_ref, o_ref, *, pieces):
    w = w_ref[...]
    y = nn(g_ref[...], w.reshape(w.shape[0] * w.shape[2], w.shape[3])).astype(BF16)
    rows = y.shape[0] // pieces
    for r in range(pieces):
        o_ref[pl.ds(pl.multiple_of(place_ref[r], rows), rows), :] = y[r * rows : (r + 1) * rows]


def heads_grad(places, grad, w, pieces):
    t, d = grad.shape
    p, _, ds, n = w.shape
    return call(
        functools.partial(d_heads_kernel, pieces=pieces),
        "dheads",
        (1,),
        [fixed((t, d)), pl.BlockSpec((p, 1, ds, n), lambda g, *_: (0, 3, 0, 0), pipeline_mode=pl.Buffered(1))],
        fixed((t, n)),
        sds((t, n), BF16),
        2 * t * n * d,
        2 * (t * n + n * d + t * d),
        prefetch=1,
    )(places, grad, w)


def grad_out_kernel(place_ref, g_ref, h_ref, o_ref, *, pieces):
    rows = g_ref.shape[0] // pieces
    heads = jnp.concatenate(
        [h_ref[pl.ds(pl.multiple_of(place_ref[r], rows), rows), :] for r in range(pieces)], 0
    )
    o_ref[...] = tn(g_ref[...], heads).astype(BF16).reshape(o_ref.shape)


def out_weight_grad(places, grad, heads, p, pieces):
    t, d = grad.shape
    n = heads.shape[1]
    ds = d // p
    pb = max(1, TILE // ds)
    return call(
        functools.partial(grad_out_kernel, pieces=pieces),
        "gradout",
        (p // pb,),
        [pl.BlockSpec((t, pb * ds), lambda g, *_: (0, g)), fixed((t, n))],
        pl.BlockSpec((pb, 1, ds, n), lambda g, *_: (g, 3, 0, 0)),
        sds((p, 4, ds, n), BF16),
        2 * t * n * d,
        2 * (t * n + n * d + t * d),
        prefetch=1,
    )(places, grad, heads)


def norm_two_kernel(x_ref, a_ref, b_ref, c_ref, g_ref, w_ref, ids_ref, mid_ref, ext_ref, probs_ref, chosen_ref, *, experts):
    mid = x_ref[...].astype(F32) + a_ref[...].astype(F32) + b_ref[...].astype(F32) + c_ref[...].astype(F32)
    mid_ref[...] = mid
    d = mid.shape[1]
    r = lax.rsqrt(jnp.mean(mid * mid, -1, keepdims=True) + EPSILON)
    low = (mid * r * g_ref[...]).astype(BF16)
    ext_ref[:, :d] = low
    logits = nt(low, w_ref[...])
    lane = lax.broadcasted_iota(jnp.int32, logits.shape, 1)
    logits = jnp.where(lane < experts, logits, -1e30)
    expo = jnp.exp(logits - jnp.max(logits, -1, keepdims=True))
    probs = expo / jnp.sum(expo, -1, keepdims=True)
    chosen = jnp.zeros_like(probs)
    for j in range(ids_ref.shape[1]):
        chosen += (ids_ref[:, j : j + 1] == lane).astype(F32)
    probs_ref[...] = probs
    chosen_ref[...] = chosen
    gates = probs * chosen
    high = gates.astype(BF16)
    rest = (gates - high.astype(F32)).astype(BF16)
    ext_ref[:, d:] = jnp.concatenate([high[:, : LANES // 2], rest[:, : LANES // 2]], 1)


def norm_two(x, sums, gain, router, ids, experts):
    t, d = x.shape
    return call(
        functools.partial(norm_two_kernel, experts=experts),
        "norm_two",
        (1,),
        [fixed((t, d))] * 4 + [fixed((1, d)), fixed(router.shape), fixed(ids.shape)],
        [fixed((t, d)), fixed((t, d + LANES)), fixed((t, LANES)), fixed((t, LANES))],
        [sds((t, d), F32), sds((t, d + LANES), BF16), sds((t, LANES), F32), sds((t, LANES), F32)],
        2 * t * d * LANES,
        14 * t * d,
    )(x, *sums, gain, router, ids)


def norm_two_back_kernel(a_ref, b_ref, c_ref, mid_ref, ext_ref, probs_ref, chosen_ref, cot_ref, g_ref, w_ref, *outs):
    mid_grad_ref, low_ref, gain_ref, router_ref = outs
    d = mid_ref.shape[1]
    du = a_ref[...].astype(F32) + b_ref[...].astype(F32) + c_ref[...].astype(F32)
    probs = probs_ref[...]
    masked = du[:, d:] * chosen_ref[...]
    d_logits = (probs * (masked - jnp.sum(probs * masked, -1, keepdims=True))).astype(BF16)
    router_ref[...] = tn(d_logits, ext_ref[:, :d])
    u = du[:, :d] + nn(d_logits, w_ref[...])
    mid = mid_ref[...]
    r = lax.rsqrt(jnp.mean(mid * mid, -1, keepdims=True) + EPSILON)
    hat = mid * r
    gain_ref[...] = jnp.sum(u * hat, 0, keepdims=True)
    w = u * g_ref[...]
    grad = cot_ref[...].astype(F32) + r * (w - hat * jnp.mean(w * hat, -1, keepdims=True))
    mid_grad_ref[...] = grad
    low_ref[...] = grad.astype(BF16)


def norm_two_back(sums, mid, ext, probs, chosen, cot, gain, router):
    t, d = mid.shape
    wide = fixed((t, d + LANES))
    return call(
        norm_two_back_kernel,
        "norm_two_back",
        (1,),
        [wide] * 3
        + [fixed((t, d)), wide, fixed((t, LANES)), fixed((t, LANES)), fixed((t, d)), fixed((1, d)), fixed(router.shape)],
        [fixed((t, d)), fixed((t, d)), fixed((1, d)), fixed((LANES, d))],
        [sds((t, d), F32), sds((t, d), BF16), sds((1, d), F32), sds((LANES, d), F32)],
        4 * t * d * LANES,
        20 * t * d,
    )(*sums, mid, ext, probs, chosen, cot, gain, router)


def norm_one_back_kernel(a_ref, b_ref, c_ref, x_ref, mid_grad_ref, g_ref, o_ref, gain_ref):
    u = a_ref[...].astype(F32) + b_ref[...].astype(F32) + c_ref[...].astype(F32)
    x = x_ref[...].astype(F32)
    r = lax.rsqrt(jnp.mean(x * x, -1, keepdims=True) + EPSILON)
    hat = x * r
    gain_ref[...] = jnp.sum(u * hat, 0, keepdims=True)
    w = u * g_ref[...]
    o_ref[...] = (mid_grad_ref[...] + r * (w - hat * jnp.mean(w * hat, -1, keepdims=True))).astype(BF16)


def norm_one_back(sums, x, mid_grad, gain):
    t, d = x.shape
    return call(
        norm_one_back_kernel,
        "norm_one_back",
        (1,),
        [fixed((t, d))] * 5 + [fixed((1, d))],
        [fixed((t, d)), fixed((1, d))],
        [sds((t, d), BF16), sds((1, d), F32)],
        20 * t * d,
        14 * t * d,
    )(*sums, x, mid_grad, gain)


def expert_kernel(first_ref, *refs, parts):
    xs, cs, w_ref = refs[:parts], refs[parts : 2 * parts], refs[2 * parts]
    hid_ref, dgu_ref, dg_ref = refs[2 * parts + 1 :]
    e = pl.program_id(0)
    t = cs[0].shape[0]
    d = cs[0].shape[1]

    @pl.when(e == 0)
    def _():
        dg_ref[...] = jnp.zeros_like(dg_ref)

    f = w_ref.shape[4]
    me = first_ref[0] + e
    lane = lax.broadcasted_iota(jnp.int32, (t, LANES), 1)
    for part, (x_ref, c_ref) in enumerate(zip(xs, cs)):

        def block(x_ref=x_ref, c_ref=c_ref, to=slice(part * t, (part + 1) * t)):
            x = x_ref[:, :d]
            a = nn(x, w_ref[:, 0, 0].reshape(d, f))
            b = nn(x, w_ref[:, 0, 1].reshape(d, f))
            dh = nn(c_ref[...], w_ref[:, 0, 2].reshape(d, f))
            mine = (lane == me) | (lane == me + LANES // 2)
            gate = jnp.sum(jnp.where(mine, x_ref[:, d:].astype(F32), 0.0), -1, keepdims=True)
            sigma = jax.nn.sigmoid(a)
            swish = a * sigma
            act = swish * b
            hid_ref[to, :] = (gate * act).astype(BF16)
            d_gate = jnp.sum(dh * act, -1, keepdims=True)
            dg_ref[to, :] += jnp.where(lane == me, d_gate, 0.0)
            inner = dh * gate
            dgu_ref[to, :f] = (inner * b * sigma * (1.0 + a * (1.0 - sigma))).astype(BF16)
            dgu_ref[to, f:] = (inner * swish).astype(BF16)

        block()


def expert_up(first, xs, cs, w):
    t, d = cs[0].shape
    parts = len(cs)
    p, e, _, ds, f = w.shape
    every = parts * t
    return call(
        functools.partial(expert_kernel, parts=parts),
        "expert_up",
        (e,),
        [fixed(x.shape) for x in xs]
        + [fixed((t, d))] * parts
        + [pl.BlockSpec((p, 1, 3, ds, f), lambda i, *_: (0, i, 0, 0, 0))],
        [
            pl.BlockSpec((every, f), lambda i, *_: (0, i)),
            pl.BlockSpec((every, 2 * f), lambda i, *_: (0, i)),
            pl.BlockSpec((every, LANES), lambda i, *_: (0, 0)),
        ],
        [sds((every, e * f), BF16), sds((every, e * 2 * f), BF16), sds((every, LANES), F32)],
        6 * every * d * f * e,
        2 * (3 * d * f * e + 2 * every * d + 3 * every * f * e),
        prefetch=1,
    )(first, *xs, *cs, w)


def expert_grad_kernel(*refs, parts):
    xs, cs, hid_ref, dgu_ref, o_ref = refs[:parts], refs[parts : 2 * parts], *refs[2 * parts :]
    pb, e, _, ds, f = o_ref.shape
    x = jnp.concatenate([r[...] for r in xs], 0)
    c = jnp.concatenate([r[...] for r in cs], 0)
    both = tn(x, dgu_ref[...]).astype(BF16)
    down = tn(c, hid_ref[...]).astype(BF16)
    for i in range(e):
        o_ref[:, i, 0] = both[:, 2 * i * f : (2 * i + 1) * f].reshape(pb, ds, f)
        o_ref[:, i, 1] = both[:, (2 * i + 1) * f : (2 * i + 2) * f].reshape(pb, ds, f)
        o_ref[:, i, 2] = down[:, i * f : (i + 1) * f].reshape(pb, ds, f)


def expert_grads(xs, cs, hid, dgu, p, e):
    t, d = cs[0].shape
    parts = len(cs)
    ds = d // p
    f = hid.shape[1] // e
    pb = max(1, TILE // ds)
    column = pl.BlockSpec((t, pb * ds), lambda g: (0, g))
    return call(
        functools.partial(expert_grad_kernel, parts=parts),
        "expert_grad",
        (p // pb,),
        [column] * (2 * parts) + [fixed(hid.shape), fixed(dgu.shape)],
        pl.BlockSpec((pb, e, 3, ds, f), lambda g: (g, 0, 0, 0, 0)),
        sds((p, e, 3, ds, f), BF16),
        6 * parts * t * d * f * e,
        2 * (3 * d * f * e + 2 * parts * t * d + 3 * parts * t * f * e),
    )(*xs, *cs, hid, dgu)


def settle_kernel(spot_ref, *refs, pieces):
    gate_up_ref, down_ref = refs[-2:]
    each = pl.num_programs(0) // pieces
    for r in range(pieces):

        @pl.when(pl.program_id(0) // each == r)
        def _():
            gate_up_ref[...] = refs[r][:, :2].astype(F32)
            down_ref[...] = refs[r][:, 2].astype(F32)


def settle(spots, pieces, kept, experts):
    e, _, ds, f = pieces[0].shape
    count = len(pieces)
    each = e // 2

    def piece(r):
        return pl.BlockSpec((2, 3, ds, f), lambda g, spot: (jnp.clip(g - r * each, 0, each - 1), 0, 0, 0))

    return call(
        functools.partial(settle_kernel, pieces=count),
        "settle",
        (count * each,),
        [piece(r) for r in range(count)] + [pl.BlockSpec(memory_space=pl.ANY)] * len(kept),
        [
            pl.BlockSpec((2, 2, ds, f), lambda g, spot: (spot[g], 0, 0, 0)),
            pl.BlockSpec((2, ds, f), lambda g, spot: (spot[g], 0, 0)),
        ],
        [sds((experts, 2, ds, f), F32), sds((experts, ds, f), F32)],
        0,
        18 * count * e * ds * f,
        prefetch=1,
        aliases={1 + count + i: i for i in range(len(kept))},
    )(spots, *pieces, *kept)


def down_kernel(*refs, planes, chunks, sides, begun):
    acts, ws = refs[:chunks], refs[chunks : 2 * chunks]
    gates = refs[2 * chunks : 2 * chunks + sides]
    before = refs[2 * chunks + sides : 2 * chunks + sides + begun]
    outs = refs[2 * chunks + sides + begun :]
    g = pl.program_id(0)
    pb, _, _, ds, f = ws[0].shape
    wide = pb * ds
    rows = outs[0].shape[0]
    joined = [
        jnp.concatenate([w[:, i, c].reshape(wide, f) for i in range(w.shape[1]) for c in range(planes)], 1)
        for w in ws
    ]
    to = pl.ds(pl.multiple_of(g * wide, wide), wide)
    for part, o in enumerate(outs):
        own = slice(part * rows, (part + 1) * rows)
        value = sum(nt(a[own, :], w) for a, w in zip(acts, joined))
        if begun:
            value += before[part][...].astype(F32)
        o[:, to] = value.astype(BF16)
    if sides:

        @pl.when(g == 0)
        def _():
            for part, o in enumerate(outs):
                own = slice(part * rows, (part + 1) * rows)
                o[:, o.shape[1] - LANES :] = sum(s[own, :] for s in gates).astype(BF16)


def expert_down(acts, ws, plane, planes, gates, before, parts, name):
    every = acts[0].shape[0]
    p, _, _, ds, f = ws[0].shape
    k = sum(a.shape[1] for a in acts)
    t = every // parts
    chunks = len(acts)
    d = p * ds + (LANES if gates else 0)
    pb = max(1, 2 * TILE // ds)
    return call(
        functools.partial(down_kernel, planes=planes, chunks=chunks, sides=len(gates), begun=len(before)),
        name,
        (p // pb,),
        [fixed(a.shape) for a in acts]
        + [pl.BlockSpec((pb, w.shape[1], planes, ds, f), lambda g: (g, 0, plane, 0, 0)) for w in ws]
        + [fixed((every, LANES))] * len(gates)
        + [pl.BlockSpec((t, pb * ds), lambda g: (0, g))] * len(before),
        [pl.BlockSpec((t, d), lambda g: (0, 0))] * parts,
        [sds((t, d), BF16)] * parts,
        2 * every * k * p * ds,
        2 * (every * k + k * p * ds) + 2 * every * d,
    )(*acts, *ws, *gates, *before)


def unturn_kernel(dq_ref, dk_ref, raw_ref, s_ref, g_ref, cos_ref, sin_ref, u_ref, in_ref, gg_ref):
    h = pl.program_id(0)
    reps = raw_ref.shape[1] // cos_ref.shape[0]
    cosine = jnp.concatenate([cos_ref[...]] * reps, 0)
    sine = jnp.concatenate([sin_ref[...]] * reps, 0)
    for i, grad in enumerate((dq_ref[...], dk_ref[...])):
        u = turn(grad, cosine, -sine)
        hat = raw_ref[i] * s_ref[i]
        product = u * hat
        u_ref[i] = u
        gg_ref[i] = jnp.sum(product, 0, keepdims=True)
        row = jnp.broadcast_to(jnp.sum(product * g_ref[i], -1, keepdims=True), in_ref.shape[1:])

        @pl.when(h == 0)
        def _():
            in_ref[i] = row

        @pl.when(h != 0)
        def _():
            in_ref[i] += row


def unturn(dq, dk, raw, scales, gains, cosine, sine):
    _, t, n = raw.shape
    h = HEAD_DIM
    length = cosine.shape[0]
    column = pl.BlockSpec((t, h), lambda i: (0, i))
    pair = pl.BlockSpec((2, t, h), lambda i: (0, 0, i))
    return call(
        unturn_kernel,
        "unturn",
        (n // h,),
        [
            column,
            column,
            pair,
            fixed((2, t, 1)),
            pl.BlockSpec((2, 1, h), lambda i: (0, 0, i)),
            fixed((length, h)),
            fixed((length, h)),
        ],
        [
            pair,
            pl.BlockSpec((2, t, 128), lambda i: (0, 0, 0)),
            pl.BlockSpec((2, 1, h), lambda i: (0, 0, i)),
        ],
        [sds((2, t, n), F32), sds((2, t, 128), F32), sds((2, 1, n), F32)],
        30 * t * n,
        24 * t * n,
    )(dq, dk, raw, scales, gains, cosine, sine)


def raw_back_kernel(place_ref, u_ref, raw_ref, s_ref, in_ref, g_ref, dv_ref, w_ref, d_ref, *outs):
    t, n = dv_ref.shape

    @pl.when(pl.program_id(0) == 0)
    def _():
        for i in range(2):
            hat = raw_ref[i] * s_ref[i]
            d_ref[:, i * n : (i + 1) * n] = (
                s_ref[i] * (u_ref[i] * g_ref[i] - hat * in_ref[i])
            ).astype(BF16)
        d_ref[:, 2 * n :] = dv_ref[...]

    pb, _, ds, _ = w_ref.shape
    w = jnp.concatenate([w_ref[:, c].reshape(pb * ds, n) for c in range(3)], 1)
    y = nt(d_ref[...], w).astype(BF16)
    rows = outs[0].shape[0]
    for r, o in enumerate(outs):
        for q in range(len(outs)):

            @pl.when(place_ref[r] == q * rows)
            def _():
                o[...] = y[q * rows : (q + 1) * rows]


def raw_back(places, u, raw, scales, inner, gains, dv, w, pieces):
    t, n = dv.shape
    p, _, ds, _ = w.shape
    d = p * ds
    pb = max(1, 2 * TILE // ds)
    return call(
        raw_back_kernel,
        "raw_back",
        (p // pb,),
        [
            fixed((2, t, n)),
            fixed((2, t, n)),
            fixed((2, t, 1)),
            fixed((2, t, 1)),
            fixed((2, 1, n)),
            fixed((t, n)),
            pl.BlockSpec((pb, 3, ds, n), lambda g, *_: (g, 0, 0, 0)),
        ],
        [pl.BlockSpec((t, 3 * n), lambda g, *_: (0, 0))]
        + [pl.BlockSpec((t // pieces, pb * ds), lambda g, *_: (0, g))] * pieces,
        [sds((t, 3 * n), BF16)] + [sds((t // pieces, d), BF16)] * pieces,
        6 * t * d * n,
        2 * (3 * d * n + t * d) + 20 * t * n,
        prefetch=1,
    )(places, u, raw, scales, inner, gains, dv, w)


def qkv_grad_kernel(n_ref, d_ref, kept_ref, o_ref):
    pb, _, ds, n = o_ref.shape
    grads = tn(n_ref[...], d_ref[...]).astype(BF16)
    for c in range(3):
        o_ref[:, c] = grads[:, c * n : (c + 1) * n].reshape(pb, ds, n)


def qkv_grads(normed, grad, kept, p):
    t, d = normed.shape
    n = grad.shape[1] // 3
    ds = d // p
    pb = max(1, TILE // ds)
    return call(
        qkv_grad_kernel,
        "qkv_grad",
        (p // pb,),
        [
            pl.BlockSpec((t, pb * ds), lambda g: (0, g)),
            fixed((t, 3 * n)),
            pl.BlockSpec(memory_space=pl.ANY),
        ],
        pl.BlockSpec((pb, 3, ds, n), lambda g: (g, 0, 0, 0)),
        sds(kept.shape, BF16),
        6 * t * d * n,
        2 * (3 * d * n + t * d + 3 * t * n),
        aliases={2: 0},
    )(normed, grad, kept)


def swap(value, axis):
    return lax.ppermute(value, axis, [(0, 1), (1, 0)])


def spread(value):
    rows = swap(value, "row")
    return (value, swap(value, "core"), rows, swap(rows, "core"))


def across(value, k):
    size = lax.axis_size("tp")
    return lax.ppermute(value, "tp", [(i, i ^ k) for i in range(size)])


def total(pieces):
    return sum(v.astype(F32) for v in pieces)


def add(*values):
    return total(values).astype(values[0].dtype)


def cut(value, pieces):
    rows = value.shape[0] // pieces
    return [value[r * rows : (r + 1) * rows] for r in range(pieces)]


def join(*pieces):
    return jnp.concatenate(pieces, 0)


class Line:
    def __init__(self):
        self.last = None

    def __call__(self, step, *operands):
        leaves, form = jax.tree.flatten(operands)
        spots = [i for i, v in enumerate(leaves) if isinstance(v, jax.Array)]
        if self.last is not None:
            kept, self.last = lax.optimization_barrier(([leaves[i] for i in spots], self.last))
            for i, v in zip(spots, kept):
                leaves[i] = v
        result = step(*jax.tree.unflatten(form, leaves))
        self.last = jax.tree.leaves(result)
        return result

    def sums(self, own, core, pieces, first=None):
        mine, theirs = cut(own, pieces), cut(swap(core, "core"), pieces)
        last = across(self(add, mine[3], theirs[3]), 1)
        near = self(add, mine[2], theirs[2], last)
        beside, first = self(lambda a, b, c, d: (add(a, b), add(c, d)), mine[1], theirs[1], mine[0], theirs[0])
        return [first, across(beside, 1), across(near, 2)]


def in_place_kernel(place_ref, *refs, count):
    for r, piece in enumerate(refs[:count]):

        @pl.when(pl.program_id(0) == r)
        def _():
            refs[-1][...] = piece[...]


def in_place(places, pieces, kept, total_rows):
    rows, d = pieces[0].shape
    count = len(pieces)
    return call(
        functools.partial(in_place_kernel, count=count),
        "inplace",
        (count,),
        [fixed((rows, d))] * count + [pl.BlockSpec(memory_space=pl.ANY)] * len(kept),
        pl.BlockSpec((rows, d), lambda r, place: (place[r] // rows, 0)),
        sds((total_rows, d), pieces[0].dtype),
        0,
        4 * rows * count * d,
        prefetch=1,
        aliases={1 + count: 0} if kept else None,
    )(places, *pieces, *kept)


def meet(value):
    value = value + across(value, 1)
    return value + across(value, 2)


def relative(value, places, pieces):
    rows = value.shape[0] // pieces
    return [lax.dynamic_slice_in_dim(value, places[r], rows, 0) for r in range(pieces)]


def body(
    inputs,
    prefix,
    expert_ids,
    norm_gains,
    qkv_weight,
    out_weight,
    router_weight,
    gate_up_weight,
    down_weight,
    cotangent,
    *,
    chunks,
):
    sequences, length, width = inputs.shape
    t = sequences * length
    tp = lax.axis_size("tp")
    quarter = t // tp
    column = lax.axis_index("tp")
    core = lax.axis_index("core")
    ctx = lax.axis_index("row") * 2 + core
    experts = router_weight.shape[1]
    group = experts // 2
    starts = [sum(chunks[:k]) for k in range(len(chunks))]
    x = inputs.reshape(t, width)
    places = jnp.stack([column ^ r for r in range(tp)]).astype(jnp.int32) * quarter
    x_q = lax.dynamic_slice_in_dim(x, column * quarter, quarter, 0)

    line = Line()
    attn_local = jnp.concatenate([qkv_weight, out_weight[None]], 0)
    attn_w = lax.all_gather(attn_local, PLANE, axis=0, tiled=False)
    triple = jnp.concatenate([gate_up_weight, down_weight[:, None]], 1)
    ds, f = triple.shape[2:]
    grouped = triple.reshape(2, group, 3, ds, f)
    ws = []
    for begin, e in zip(starts, chunks):
        mine = lax.all_to_all(grouped[:, begin : begin + e], "core", 0, 0, tiled=True)
        ws.append(lax.all_gather(mine, FR, axis=0, tiled=False).reshape(-1, e, 3, ds, f))
    gains_low = lax.all_gather(norm_gains, PLANE, axis=1, tiled=True)
    router = lax.all_gather(router_weight, PLANE, axis=0, tiled=True)
    cots = relative(cotangent.reshape(t, width), places, tp)
    c0 = join(*cots)
    c1 = swap(c0, "core")
    attn_w, gains_low, router, c0 = lax.optimization_barrier((attn_w, gains_low, router, c0))
    p = attn_w.shape[0]

    gains = gains_low.astype(F32)
    n = attn_w.shape[3]
    router_rows = jnp.concatenate([router.T, jnp.zeros((128 - experts, width), BF16)], 0)

    own_gains = lax.dynamic_slice_in_dim(gains[2:4], column * n, n, 1)[:, None, :]
    halves = jnp.arange(0, HEAD_DIM, 2).astype(F32) / HEAD_DIM
    inverse = 1.0 / THETA**halves
    positions = ctx * length + jnp.arange(length, dtype=jnp.int32)
    angles = positions.astype(F32)[:, None] * inverse[None, :]
    cosine = jnp.concatenate([jnp.cos(angles)] * 2, 1)
    sine = jnp.concatenate([-jnp.sin(angles), jnp.sin(angles)], 1)
    offsets = jnp.stack([ctx, ctx ^ 1, ctx ^ 2, ctx ^ 3, ctx]).astype(jnp.int32) * length
    scal = jnp.concatenate([offsets, prefix.astype(jnp.int32)])
    ids_q = lax.dynamic_slice_in_dim(expert_ids.reshape(t, -1), column * quarter, quarter, 0)
    normed_one, raw, values, squares = line(qkv_project, x, gains[0:1], attn_w)
    v_blocks = spread(values)
    scales = lax.rsqrt(meet(squares[:, :, 0]) / width + EPSILON)[:, :, None]
    scales, values = lax.optimization_barrier((scales, v_blocks[2]))
    v_blocks = v_blocks[:2] + (values,) + v_blocks[3:]
    queries, keys = line(prepare, raw, scales, own_gains, cosine, sine)
    k_blocks = spread(keys)
    blocks = k_blocks + v_blocks
    heads = line(attend, scal, queries, blocks, length)
    sums = line(project_out, places, heads, attn_w, tp)
    near = line(add, sums[2], across(sums[3], 1))
    sums = [sums[0], across(sums[1], 1), across(near, 2)]
    mid, ext, probs, chosen = line(norm_two, x_q, sums, gains[1:2], router_rows, ids_q, experts)
    far = across(ext, 2)
    near = across(ext, 1)
    x0 = line(join, ext, near, far, across(far, 1))
    x1 = swap(x0, "core")

    xs, cs = [x0, x1], [c0, c1]
    blocks_in = jnp.arange(width // TILE, dtype=jnp.int32)
    hid, dgu, side, grads = [], [], [], []
    dx = []

    def up(k):
        first = (core * group + starts[k]).astype(jnp.int32)[None]
        for kept, made in zip((hid, dgu, side), line(expert_up, first, xs, cs, ws[k])):
            kept.append(made)

    def back(k, before):
        gates = side if k == len(chunks) - 1 else []
        return line(expert_down, [dgu[k]], [ws[k]], 0, 2, gates, before, 2, "expert_dx")

    def weight_grad(k):
        return line(expert_grads, xs, cs, hid[k], dgu[k], p, chunks[k])

    def to_owners(made, k, after):
        made, after = lax.optimization_barrier((made, after))
        made = made.reshape(-1, 2, chunks[k], 3, ds, f)
        return lax.optimization_barrier(lax.psum_scatter(made, FR, scatter_dimension=0, tiled=False))

    for k in range(len(chunks)):
        up(k)
        dx = back(k, dx)
        if k < len(chunks) - 1:
            made = weight_grad(k)
            grads.append(to_owners(made, k, ()))
    d_normed = line.sums(*dx, tp)
    moe = line(expert_down, hid, ws, 2, 1, [], [], 2, "expert_out")
    late = weight_grad(len(chunks) - 1)

    d_mid, d_mid_low, gain_two, grad_router = line(
        norm_two_back, d_normed, mid, ext, probs, chosen, cots[0], gains[1:2], router_rows
    )
    far = across(d_mid_low, 2)
    near = across(d_mid_low, 1)
    d_mid_low = line(join, d_mid_low, near, far, across(far, 1))
    own, beside = cut(moe[0], tp), cut(swap(moe[1], "core"), tp)
    last = across(line(add, own[3], beside[3]), 1)

    d_heads = line(heads_grad, places, d_mid_low, attn_w, tp)
    grads.append(to_owners(late, len(chunks) - 1, d_heads))
    dq, b0, b1, b2, b3 = line(attend_back, scal, queries, blocks, d_heads, length)
    r1 = swap(b1, "core")
    r3 = swap(b3, "core")
    near = line(add, own[2], beside[2], last)
    next_one = line(add, own[1], beside[1])
    moe = [across(next_one, 1), across(near, 2)]
    r2 = swap(line(add, b2, r3), "row")
    grad_attn = line(out_weight_grad, places, d_mid_low, heads, p, tp)
    out = line(lambda *v: total(v).astype(BF16), mid, own[0], beside[0], *moe)
    out_far = across(out, 2)
    out_near = across(out, 1)
    def parted(k):
        own, other = line(
            lambda v: [lax.dynamic_index_in_dim(v, c, 0, keepdims=False) for c in (core, core ^ 1)], grads[k]
        )
        return own, swap(other, "core")

    def settled(k, pair, kept):
        steps = jnp.arange(chunks[k] // 2, dtype=jnp.int32)
        spots = jnp.concatenate([(c * group + starts[k]) // 2 + steps for c in (core, core ^ 1)])
        return line(settle, spots.astype(jnp.int32), pair, kept, experts)

    pairs = [parted(0)]
    d_kv = line(lambda *v: total(v), b0, r1, r2)
    out_far, d_kv = lax.optimization_barrier((out_far, d_kv))
    out_both = across(out_far, 1)
    u, inner, gain_qk = line(unturn, dq, d_kv[0], raw, scales, own_gains, cosine, sine)
    outputs = line(in_place, places, [out, out_near, out_far, out_both], [], t).reshape(inputs.shape)

    inner = (meet(inner[:, :, 0]) / width)[:, :, None]
    d_raw, *d_one = line(
        raw_back, places, u, raw, scales, inner, own_gains, d_kv[1].astype(BF16), attn_w, tp
    )
    last = across(d_one[3], 1)
    grad_attn = line(qkv_grads, normed_one, d_raw, grad_attn, p)
    grad_attn = lax.psum_scatter(grad_attn, PLANE, scatter_dimension=0, tiled=False)
    near = line(add, d_one[2], last)
    d_one = [d_one[0], across(d_one[1], 1), across(near, 2)]
    grad_in, gain_one = line(norm_one_back, d_one, x_q, d_mid, gains[0:1])
    far = across(grad_in, 2)
    near = across(grad_in, 1)
    placed = lax.dynamic_update_slice_in_dim(
        jnp.zeros((2, width), F32), gain_qk[:, 0, :], column * n, 1
    )

    small = line(lambda *v: jnp.concatenate(v, 0), grad_router[:experts], gain_one, gain_two, placed)
    rows = small.shape[0]
    small = small.reshape(rows, p, ds).transpose(1, 0, 2)
    small = jnp.sum(lax.all_to_all(small, PLANE, 0, 0, tiled=True), 0)
    other = across(small, 1)
    both = across(far, 1)
    kept = settled(0, pairs[0], [])
    placed_in = line(in_place, places[:2], [grad_in, near], [], t)
    pairs.append(parted(1))
    owned_gate_up, owned_down = settled(1, pairs[1], kept)
    small = line(lambda a, b: a + b, small, other)
    other = across(small, 2)
    grad_inputs = line(in_place, places[2:], [far, both], [placed_in], t).reshape(inputs.shape)
    grad_attn, grad_inputs = lax.optimization_barrier((grad_attn, grad_inputs))
    small = line(lambda a, b: a + b, small, other)
    owned_gains = small[experts:]
    owned_router = small[:experts].T
    return (
        outputs,
        grad_inputs,
        owned_gains,
        grad_attn[:3].astype(F32),
        grad_attn[3].astype(F32),
        owned_router,
        owned_gate_up,
        owned_down,
    )


def solution(mesh):
    fsdp, ctx, tp = (mesh.shape[a] for a in ("fsdp", "ctx", "tp"))
    fine = Mesh(mesh.devices.reshape(fsdp, ctx // 2, 2, tp), EVERY)
    tokens = P("fsdp", ("row", "core"), None)
    weights = (
        P(None, PLANE),
        P(None, PLANE, "tp"),
        P(PLANE, "tp"),
        P(PLANE, None),
        P(None, None, PLANE, "tp"),
        P(None, PLANE, "tp"),
    )
    return jax.shard_map(
        functools.partial(body, chunks=(6, 2)),
        mesh=fine,
        in_specs=(tokens, P("fsdp"), tokens) + weights + (tokens,),
        out_specs=(tokens, tokens) + weights,
        check_vma=False,
    )
```

```python
import functools

import jax
import jax.numpy as jnp
from jax import lax
from jax.experimental import pallas as pl
from jax.experimental.pallas import tpu as pltpu
from jax.sharding import Mesh, PartitionSpec as P

HEAD_DIM = 128
EPSILON = 1e-05
THETA = 10000.0
TILE = 256
F32 = jnp.float32
BF16 = jnp.bfloat16
FR = ("fsdp", "row")
LANES = 128
PLANE = ("fsdp", "row", "core")
EVERY = ("fsdp", "row", "core", "tp")


def nn(a, b):
    return lax.dot_general(a, b, (((1,), (0,)), ((), ())), preferred_element_type=F32)


def nt(a, b):
    return lax.dot_general(a, b, (((1,), (1,)), ((), ())), preferred_element_type=F32)


def tn(a, b):
    return lax.dot_general(a, b, (((0,), (0,)), ((), ())), preferred_element_type=F32)


def call(kernel, name, grid, in_specs, out_specs, out_shape, flops, moved, scratch=(), prefetch=0, limit=56, aliases=None):
    return pl.pallas_call(
        kernel,
        name=name,
        out_shape=out_shape,
        grid_spec=pltpu.PrefetchScalarGridSpec(
            num_scalar_prefetch=prefetch,
            grid=grid,
            in_specs=in_specs,
            out_specs=out_specs,
            scratch_shapes=list(scratch),
        ),
        input_output_aliases=aliases or {},
        compiler_params=pltpu.CompilerParams(
            dimension_semantics=("arbitrary",) * len(grid), vmem_limit_bytes=limit << 20
        ),
        cost_estimate=pl.CostEstimate(flops=int(flops), bytes_accessed=int(moved), transcendentals=0),
    )


def fixed(shape):
    return pl.BlockSpec(shape, lambda *a: (0,) * len(shape), pipeline_mode=pl.Buffered(1))


def sds(shape, dtype):
    return jax.ShapeDtypeStruct(shape, dtype)


def qkv_kernel(x_ref, g_ref, w_ref, n_ref, raw_ref, v_ref, sq_ref):
    c = pl.program_id(0)

    @pl.when(c == 0)
    def _():
        x = x_ref[...].astype(F32)
        r = lax.rsqrt(jnp.mean(x * x, -1, keepdims=True) + EPSILON)
        n_ref[...] = (x * r * g_ref[...]).astype(BF16)

    w = w_ref[...]
    y = nn(n_ref[...], w.reshape(w.shape[0] * w.shape[2], w.shape[3]))

    @pl.when(c < 2)
    def _():
        raw_ref[0] = y
        sq_ref[0] = jnp.broadcast_to(jnp.sum(y * y, -1, keepdims=True), sq_ref.shape[1:])

    @pl.when(c == 2)
    def _():
        v_ref[...] = y.astype(BF16)


def qkv_project(x, gain, w):
    t, d = x.shape
    p, _, ds, n = w.shape
    return call(
        qkv_kernel,
        "qkv",
        (3,),
        [
            fixed((t, d)),
            fixed((1, d)),
            pl.BlockSpec((p, 1, ds, n), lambda c: (0, c, 0, 0)),
        ],
        [
            pl.BlockSpec((t, d), lambda c: (0, 0)),
            pl.BlockSpec((1, t, n), lambda c: (jnp.minimum(c, 1), 0, 0)),
            pl.BlockSpec((t, n), lambda c: (0, 0)),
            pl.BlockSpec((1, t, 128), lambda c: (jnp.minimum(c, 1), 0, 0)),
        ],
        [sds((t, d), BF16), sds((2, t, n), F32), sds((t, n), BF16), sds((2, t, 128), F32)],
        6 * t * d * n,
        2 * (3 * d * n + 2 * t * d) + 10 * t * n,
    )(x, gain, w)


def turn(v, cosine, sine):
    half = v.shape[-1] // 2
    return v * cosine + pltpu.roll(v, half, 1) * sine


def prep_kernel(raw_ref, s_ref, g_ref, cos_ref, sin_ref, q_ref, k_ref):
    reps = raw_ref.shape[1] // cos_ref.shape[0]
    cosine = jnp.concatenate([cos_ref[...]] * reps, 0)
    sine = jnp.concatenate([sin_ref[...]] * reps, 0)
    q = raw_ref[0] * s_ref[0] * g_ref[0]
    k = raw_ref[1] * s_ref[1] * g_ref[1]
    q_ref[...] = turn(q, cosine, sine).astype(BF16)
    k_ref[...] = turn(k, cosine, sine).astype(BF16)


def prepare(raw, scales, gains, cosine, sine):
    _, t, n = raw.shape
    h = HEAD_DIM
    length = cosine.shape[0]
    return call(
        prep_kernel,
        "prep",
        (n // h,),
        [
            pl.BlockSpec((2, t, h), lambda i: (0, 0, i)),
            fixed((2, t, 1)),
            pl.BlockSpec((2, 1, h), lambda i: (0, 0, i)),
            fixed((length, h)),
            fixed((length, h)),
        ],
        [pl.BlockSpec((t, h), lambda i: (0, i))] * 2,
        [sds((t, n), BF16)] * 2,
        20 * t * n,
        12 * t * n,
    )(raw, scales, gains, cosine, sine)


def masked_probs(s, scal_ref, q, ks):
    length = q.shape[0]
    prefix = scal_ref[5 + s]
    rows = lax.broadcasted_iota(jnp.int32, (length, length), 0) + scal_ref[4]
    columns = lax.broadcasted_iota(jnp.int32, (length, length), 1)
    pieces = []
    for b, k in enumerate(ks):
        place = columns + scal_ref[b]
        visible = (place <= rows) | (place < prefix)
        pieces.append(jnp.where(visible, nt(q, k) * HEAD_DIM ** (-0.5), -1e30))
    scores = jnp.concatenate(pieces, 1)
    expo = jnp.exp(scores - jnp.max(scores, -1, keepdims=True))
    return expo / jnp.sum(expo, -1, keepdims=True)


def attend_kernel(scal_ref, q_ref, *refs):
    o_ref = refs[8]
    probs = masked_probs(pl.program_id(0), scal_ref, q_ref[...], [r[...] for r in refs[:4]])
    v = jnp.concatenate([r[...] for r in refs[4:8]], 0)
    o_ref[...] = nn(probs.astype(BF16), v).astype(BF16)


def attend(scal, q, blocks, length):
    t, n = q.shape
    h = HEAD_DIM
    one = pl.BlockSpec((length, h), lambda s, i, *_: (s, i))
    return call(
        attend_kernel,
        "attend",
        (t // length, n // h),
        [one] * 9,
        one,
        sds((t, n), BF16),
        16 * t * n * length,
        24 * t * n,
        prefetch=1,
    )(scal, q, *blocks)


def attend_back_kernel(scal_ref, q_ref, *refs):
    g_ref, dq_ref, outs = refs[8], refs[9], refs[10:]
    length = q_ref.shape[0]
    q = q_ref[...]
    grad = g_ref[...]
    probs = masked_probs(pl.program_id(0), scal_ref, q, [r[...] for r in refs[:4]])
    k = jnp.concatenate([r[...] for r in refs[:4]], 0)
    v = jnp.concatenate([r[...] for r in refs[4:8]], 0)
    d_probs = nt(grad, v)
    inner = jnp.sum(probs * d_probs, -1, keepdims=True)
    d_scores = (probs * (d_probs - inner)).astype(BF16)
    scale = HEAD_DIM ** (-0.5)
    dq_ref[...] = nn(d_scores, k) * scale
    dk = (tn(d_scores, q) * scale).astype(BF16)
    dv = tn(probs.astype(BF16), grad).astype(BF16)
    for b, o in enumerate(outs):
        o[0] = dk[b * length : (b + 1) * length]
        o[1] = dv[b * length : (b + 1) * length]


def attend_back(scal, q, blocks, grad, length):
    t, n = q.shape
    h = HEAD_DIM
    one = pl.BlockSpec((length, h), lambda s, i, *_: (s, i))
    two = pl.BlockSpec((2, length, h), lambda s, i, *_: (0, s, i))
    return call(
        attend_back_kernel,
        "attend_back",
        (t // length, n // h),
        [one] * 10,
        [one] + [two] * 4,
        [sds((t, n), F32)] + [sds((2, t, n), BF16)] * 4,
        40 * t * n * length,
        48 * t * n,
        prefetch=1,
    )(scal, q, *blocks, grad)


def out_kernel(place_ref, h_ref, w_ref, *outs):
    w = w_ref[...]
    w = w.reshape(-1, w.shape[-1])
    rows = outs[0].shape[0]
    heads = jnp.concatenate(
        [h_ref[pl.ds(pl.multiple_of(place_ref[r], rows), rows), :] for r in range(len(outs))], 0
    )
    y = nt(heads, w).astype(BF16)
    for r, o in enumerate(outs):
        o[...] = y[r * rows : (r + 1) * rows]


def project_out(places, heads, w, pieces):
    t, n = heads.shape
    p, _, ds, _ = w.shape
    pb = max(1, 2 * TILE // ds)
    return call(
        out_kernel,
        "outproj",
        (p // pb,),
        [fixed((t, n)), pl.BlockSpec((pb, 1, ds, n), lambda g, *_: (g, 3, 0, 0))],
        [pl.BlockSpec((t // pieces, pb * ds), lambda g, *_: (0, g))] * pieces,
        [sds((t // pieces, p * ds), BF16)] * pieces,
        2 * t * n * p * ds,
        2 * (t * n + n * p * ds + t * p * ds),
        prefetch=1,
    )(places, heads, w)


def d_heads_kernel(place_ref, g_ref, w_ref, o_ref, *, pieces):
    w = w_ref[...]
    y = nn(g_ref[...], w.reshape(w.shape[0] * w.shape[2], w.shape[3])).astype(BF16)
    rows = y.shape[0] // pieces
    for r in range(pieces):
        o_ref[pl.ds(pl.multiple_of(place_ref[r], rows), rows), :] = y[r * rows : (r + 1) * rows]


def heads_grad(places, grad, w, pieces):
    t, d = grad.shape
    p, _, ds, n = w.shape
    return call(
        functools.partial(d_heads_kernel, pieces=pieces),
        "dheads",
        (1,),
        [fixed((t, d)), pl.BlockSpec((p, 1, ds, n), lambda g, *_: (0, 3, 0, 0), pipeline_mode=pl.Buffered(1))],
        fixed((t, n)),
        sds((t, n), BF16),
        2 * t * n * d,
        2 * (t * n + n * d + t * d),
        prefetch=1,
    )(places, grad, w)


def grad_out_kernel(place_ref, g_ref, h_ref, o_ref, *, pieces):
    rows = g_ref.shape[0] // pieces
    heads = jnp.concatenate(
        [h_ref[pl.ds(pl.multiple_of(place_ref[r], rows), rows), :] for r in range(pieces)], 0
    )
    o_ref[...] = tn(g_ref[...], heads).astype(BF16).reshape(o_ref.shape)


def out_weight_grad(places, grad, heads, p, pieces):
    t, d = grad.shape
    n = heads.shape[1]
    ds = d // p
    pb = max(1, TILE // ds)
    return call(
        functools.partial(grad_out_kernel, pieces=pieces),
        "gradout",
        (p // pb,),
        [pl.BlockSpec((t, pb * ds), lambda g, *_: (0, g)), fixed((t, n))],
        pl.BlockSpec((pb, 1, ds, n), lambda g, *_: (g, 3, 0, 0)),
        sds((p, 4, ds, n), BF16),
        2 * t * n * d,
        2 * (t * n + n * d + t * d),
        prefetch=1,
    )(places, grad, heads)


def norm_two_kernel(x_ref, a_ref, b_ref, c_ref, g_ref, w_ref, ids_ref, mid_ref, ext_ref, probs_ref, chosen_ref, *, experts):
    mid = x_ref[...].astype(F32) + a_ref[...].astype(F32) + b_ref[...].astype(F32) + c_ref[...].astype(F32)
    mid_ref[...] = mid
    d = mid.shape[1]
    r = lax.rsqrt(jnp.mean(mid * mid, -1, keepdims=True) + EPSILON)
    low = (mid * r * g_ref[...]).astype(BF16)
    ext_ref[:, :d] = low
    logits = nt(low, w_ref[...])
    lane = lax.broadcasted_iota(jnp.int32, logits.shape, 1)
    logits = jnp.where(lane < experts, logits, -1e30)
    expo = jnp.exp(logits - jnp.max(logits, -1, keepdims=True))
    probs = expo / jnp.sum(expo, -1, keepdims=True)
    chosen = jnp.zeros_like(probs)
    for j in range(ids_ref.shape[1]):
        chosen += (ids_ref[:, j : j + 1] == lane).astype(F32)
    probs_ref[...] = probs
    chosen_ref[...] = chosen
    gates = probs * chosen
    high = gates.astype(BF16)
    rest = (gates - high.astype(F32)).astype(BF16)
    ext_ref[:, d:] = jnp.concatenate([high[:, : LANES // 2], rest[:, : LANES // 2]], 1)


def norm_two(x, sums, gain, router, ids, experts):
    t, d = x.shape
    return call(
        functools.partial(norm_two_kernel, experts=experts),
        "norm_two",
        (1,),
        [fixed((t, d))] * 4 + [fixed((1, d)), fixed(router.shape), fixed(ids.shape)],
        [fixed((t, d)), fixed((t, d + LANES)), fixed((t, LANES)), fixed((t, LANES))],
        [sds((t, d), F32), sds((t, d + LANES), BF16), sds((t, LANES), F32), sds((t, LANES), F32)],
        2 * t * d * LANES,
        14 * t * d,
    )(x, *sums, gain, router, ids)


def norm_two_back_kernel(a_ref, b_ref, c_ref, mid_ref, ext_ref, probs_ref, chosen_ref, cot_ref, g_ref, w_ref, *outs):
    mid_grad_ref, low_ref, gain_ref, router_ref = outs
    d = mid_ref.shape[1]
    du = a_ref[...].astype(F32) + b_ref[...].astype(F32) + c_ref[...].astype(F32)
    probs = probs_ref[...]
    masked = du[:, d:] * chosen_ref[...]
    d_logits = (probs * (masked - jnp.sum(probs * masked, -1, keepdims=True))).astype(BF16)
    router_ref[...] = tn(d_logits, ext_ref[:, :d])
    u = du[:, :d] + nn(d_logits, w_ref[...])
    mid = mid_ref[...]
    r = lax.rsqrt(jnp.mean(mid * mid, -1, keepdims=True) + EPSILON)
    hat = mid * r
    gain_ref[...] = jnp.sum(u * hat, 0, keepdims=True)
    w = u * g_ref[...]
    grad = cot_ref[...].astype(F32) + r * (w - hat * jnp.mean(w * hat, -1, keepdims=True))
    mid_grad_ref[...] = grad
    low_ref[...] = grad.astype(BF16)


def norm_two_back(sums, mid, ext, probs, chosen, cot, gain, router):
    t, d = mid.shape
    wide = fixed((t, d + LANES))
    return call(
        norm_two_back_kernel,
        "norm_two_back",
        (1,),
        [wide] * 3
        + [fixed((t, d)), wide, fixed((t, LANES)), fixed((t, LANES)), fixed((t, d)), fixed((1, d)), fixed(router.shape)],
        [fixed((t, d)), fixed((t, d)), fixed((1, d)), fixed((LANES, d))],
        [sds((t, d), F32), sds((t, d), BF16), sds((1, d), F32), sds((LANES, d), F32)],
        4 * t * d * LANES,
        20 * t * d,
    )(*sums, mid, ext, probs, chosen, cot, gain, router)


def norm_one_back_kernel(a_ref, b_ref, c_ref, x_ref, mid_grad_ref, g_ref, o_ref, gain_ref):
    u = a_ref[...].astype(F32) + b_ref[...].astype(F32) + c_ref[...].astype(F32)
    x = x_ref[...].astype(F32)
    r = lax.rsqrt(jnp.mean(x * x, -1, keepdims=True) + EPSILON)
    hat = x * r
    gain_ref[...] = jnp.sum(u * hat, 0, keepdims=True)
    w = u * g_ref[...]
    o_ref[...] = (mid_grad_ref[...] + r * (w - hat * jnp.mean(w * hat, -1, keepdims=True))).astype(BF16)


def norm_one_back(sums, x, mid_grad, gain):
    t, d = x.shape
    return call(
        norm_one_back_kernel,
        "norm_one_back",
        (1,),
        [fixed((t, d))] * 5 + [fixed((1, d))],
        [fixed((t, d)), fixed((1, d))],
        [sds((t, d), BF16), sds((1, d), F32)],
        20 * t * d,
        14 * t * d,
    )(*sums, x, mid_grad, gain)


def expert_kernel(first_ref, *refs, parts):
    xs, cs, w_ref = refs[:parts], refs[parts : 2 * parts], refs[2 * parts]
    hid_ref, dgu_ref, dg_ref = refs[2 * parts + 1 :]
    e = pl.program_id(0)
    t = cs[0].shape[0]
    d = cs[0].shape[1]

    @pl.when(e == 0)
    def _():
        dg_ref[...] = jnp.zeros_like(dg_ref)

    f = w_ref.shape[4]
    me = first_ref[0] + e
    lane = lax.broadcasted_iota(jnp.int32, (t, LANES), 1)
    for part, (x_ref, c_ref) in enumerate(zip(xs, cs)):

        def block(x_ref=x_ref, c_ref=c_ref, to=slice(part * t, (part + 1) * t)):
            x = x_ref[:, :d]
            a = nn(x, w_ref[:, 0, 0].reshape(d, f))
            b = nn(x, w_ref[:, 0, 1].reshape(d, f))
            dh = nn(c_ref[...], w_ref[:, 0, 2].reshape(d, f))
            mine = (lane == me) | (lane == me + LANES // 2)
            gate = jnp.sum(jnp.where(mine, x_ref[:, d:].astype(F32), 0.0), -1, keepdims=True)
            sigma = jax.nn.sigmoid(a)
            swish = a * sigma
            act = swish * b
            hid_ref[to, :] = (gate * act).astype(BF16)
            d_gate = jnp.sum(dh * act, -1, keepdims=True)
            dg_ref[to, :] += jnp.where(lane == me, d_gate, 0.0)
            inner = dh * gate
            dgu_ref[to, :f] = (inner * b * sigma * (1.0 + a * (1.0 - sigma))).astype(BF16)
            dgu_ref[to, f:] = (inner * swish).astype(BF16)

        block()


def expert_up(first, xs, cs, w):
    t, d = cs[0].shape
    parts = len(cs)
    p, e, _, ds, f = w.shape
    every = parts * t
    return call(
        functools.partial(expert_kernel, parts=parts),
        "expert_up",
        (e,),
        [fixed(x.shape) for x in xs]
        + [fixed((t, d))] * parts
        + [pl.BlockSpec((p, 1, 3, ds, f), lambda i, *_: (0, i, 0, 0, 0))],
        [
            pl.BlockSpec((every, f), lambda i, *_: (0, i)),
            pl.BlockSpec((every, 2 * f), lambda i, *_: (0, i)),
            pl.BlockSpec((every, LANES), lambda i, *_: (0, 0)),
        ],
        [sds((every, e * f), BF16), sds((every, e * 2 * f), BF16), sds((every, LANES), F32)],
        6 * every * d * f * e,
        2 * (3 * d * f * e + 2 * every * d + 3 * every * f * e),
        prefetch=1,
    )(first, *xs, *cs, w)


def expert_grad_kernel(*refs, parts):
    xs, cs, hid_ref, dgu_ref, o_ref = refs[:parts], refs[parts : 2 * parts], *refs[2 * parts :]
    pb, e, _, ds, f = o_ref.shape
    x = jnp.concatenate([r[...] for r in xs], 0)
    c = jnp.concatenate([r[...] for r in cs], 0)
    both = tn(x, dgu_ref[...]).astype(BF16)
    down = tn(c, hid_ref[...]).astype(BF16)
    for i in range(e):
        o_ref[:, i, 0] = both[:, 2 * i * f : (2 * i + 1) * f].reshape(pb, ds, f)
        o_ref[:, i, 1] = both[:, (2 * i + 1) * f : (2 * i + 2) * f].reshape(pb, ds, f)
        o_ref[:, i, 2] = down[:, i * f : (i + 1) * f].reshape(pb, ds, f)


def expert_grads(xs, cs, hid, dgu, p, e):
    t, d = cs[0].shape
    parts = len(cs)
    ds = d // p
    f = hid.shape[1] // e
    pb = max(1, TILE // ds)
    column = pl.BlockSpec((t, pb * ds), lambda g: (0, g))
    return call(
        functools.partial(expert_grad_kernel, parts=parts),
        "expert_grad",
        (p // pb,),
        [column] * (2 * parts) + [fixed(hid.shape), fixed(dgu.shape)],
        pl.BlockSpec((pb, e, 3, ds, f), lambda g: (g, 0, 0, 0, 0)),
        sds((p, e, 3, ds, f), BF16),
        6 * parts * t * d * f * e,
        2 * (3 * d * f * e + 2 * parts * t * d + 3 * parts * t * f * e),
    )(*xs, *cs, hid, dgu)


def settle_kernel(spot_ref, *refs, pieces):
    gate_up_ref, down_ref = refs[-2:]
    each = pl.num_programs(0) // pieces
    for r in range(pieces):

        @pl.when(pl.program_id(0) // each == r)
        def _():
            gate_up_ref[...] = refs[r][:, :2].astype(F32)
            down_ref[...] = refs[r][:, 2].astype(F32)


def settle(spots, pieces, kept, experts):
    e, _, ds, f = pieces[0].shape
    count = len(pieces)
    each = e // 2

    def piece(r):
        return pl.BlockSpec((2, 3, ds, f), lambda g, spot: (jnp.clip(g - r * each, 0, each - 1), 0, 0, 0))

    return call(
        functools.partial(settle_kernel, pieces=count),
        "settle",
        (count * each,),
        [piece(r) for r in range(count)] + [pl.BlockSpec(memory_space=pl.ANY)] * len(kept),
        [
            pl.BlockSpec((2, 2, ds, f), lambda g, spot: (spot[g], 0, 0, 0)),
            pl.BlockSpec((2, ds, f), lambda g, spot: (spot[g], 0, 0)),
        ],
        [sds((experts, 2, ds, f), F32), sds((experts, ds, f), F32)],
        0,
        18 * count * e * ds * f,
        prefetch=1,
        aliases={1 + count + i: i for i in range(len(kept))},
    )(spots, *pieces, *kept)


def down_kernel(*refs, planes, chunks, sides, begun):
    acts, ws = refs[:chunks], refs[chunks : 2 * chunks]
    gates = refs[2 * chunks : 2 * chunks + sides]
    before = refs[2 * chunks + sides : 2 * chunks + sides + begun]
    outs = refs[2 * chunks + sides + begun :]
    g = pl.program_id(0)
    pb, _, _, ds, f = ws[0].shape
    wide = pb * ds
    rows = outs[0].shape[0]
    joined = [
        jnp.concatenate([w[:, i, c].reshape(wide, f) for i in range(w.shape[1]) for c in range(planes)], 1)
        for w in ws
    ]
    to = pl.ds(pl.multiple_of(g * wide, wide), wide)
    for part, o in enumerate(outs):
        own = slice(part * rows, (part + 1) * rows)
        value = sum(nt(a[own, :], w) for a, w in zip(acts, joined))
        if begun:
            value += before[part][...].astype(F32)
        o[:, to] = value.astype(BF16)
    if sides:

        @pl.when(g == 0)
        def _():
            for part, o in enumerate(outs):
                own = slice(part * rows, (part + 1) * rows)
                o[:, o.shape[1] - LANES :] = sum(s[own, :] for s in gates).astype(BF16)


def expert_down(acts, ws, plane, planes, gates, before, parts, name):
    every = acts[0].shape[0]
    p, _, _, ds, f = ws[0].shape
    k = sum(a.shape[1] for a in acts)
    t = every // parts
    chunks = len(acts)
    d = p * ds + (LANES if gates else 0)
    pb = max(1, 2 * TILE // ds)
    return call(
        functools.partial(down_kernel, planes=planes, chunks=chunks, sides=len(gates), begun=len(before)),
        name,
        (p // pb,),
        [fixed(a.shape) for a in acts]
        + [pl.BlockSpec((pb, w.shape[1], planes, ds, f), lambda g: (g, 0, plane, 0, 0)) for w in ws]
        + [fixed((every, LANES))] * len(gates)
        + [pl.BlockSpec((t, pb * ds), lambda g: (0, g))] * len(before),
        [pl.BlockSpec((t, d), lambda g: (0, 0))] * parts,
        [sds((t, d), BF16)] * parts,
        2 * every * k * p * ds,
        2 * (every * k + k * p * ds) + 2 * every * d,
    )(*acts, *ws, *gates, *before)


def unturn_kernel(dq_ref, dk_ref, raw_ref, s_ref, g_ref, cos_ref, sin_ref, u_ref, in_ref, gg_ref):
    h = pl.program_id(0)
    reps = raw_ref.shape[1] // cos_ref.shape[0]
    cosine = jnp.concatenate([cos_ref[...]] * reps, 0)
    sine = jnp.concatenate([sin_ref[...]] * reps, 0)
    for i, grad in enumerate((dq_ref[...], dk_ref[...])):
        u = turn(grad, cosine, -sine)
        hat = raw_ref[i] * s_ref[i]
        product = u * hat
        u_ref[i] = u
        gg_ref[i] = jnp.sum(product, 0, keepdims=True)
        row = jnp.broadcast_to(jnp.sum(product * g_ref[i], -1, keepdims=True), in_ref.shape[1:])

        @pl.when(h == 0)
        def _():
            in_ref[i] = row

        @pl.when(h != 0)
        def _():
            in_ref[i] += row


def unturn(dq, dk, raw, scales, gains, cosine, sine):
    _, t, n = raw.shape
    h = HEAD_DIM
    length = cosine.shape[0]
    column = pl.BlockSpec((t, h), lambda i: (0, i))
    pair = pl.BlockSpec((2, t, h), lambda i: (0, 0, i))
    return call(
        unturn_kernel,
        "unturn",
        (n // h,),
        [
            column,
            column,
            pair,
            fixed((2, t, 1)),
            pl.BlockSpec((2, 1, h), lambda i: (0, 0, i)),
            fixed((length, h)),
            fixed((length, h)),
        ],
        [
            pair,
            pl.BlockSpec((2, t, 128), lambda i: (0, 0, 0)),
            pl.BlockSpec((2, 1, h), lambda i: (0, 0, i)),
        ],
        [sds((2, t, n), F32), sds((2, t, 128), F32), sds((2, 1, n), F32)],
        30 * t * n,
        24 * t * n,
    )(dq, dk, raw, scales, gains, cosine, sine)


def raw_back_kernel(place_ref, u_ref, raw_ref, s_ref, in_ref, g_ref, dv_ref, w_ref, d_ref, *outs):
    t, n = dv_ref.shape

    @pl.when(pl.program_id(0) == 0)
    def _():
        for i in range(2):
            hat = raw_ref[i] * s_ref[i]
            d_ref[:, i * n : (i + 1) * n] = (
                s_ref[i] * (u_ref[i] * g_ref[i] - hat * in_ref[i])
            ).astype(BF16)
        d_ref[:, 2 * n :] = dv_ref[...]

    pb, _, ds, _ = w_ref.shape
    w = jnp.concatenate([w_ref[:, c].reshape(pb * ds, n) for c in range(3)], 1)
    y = nt(d_ref[...], w).astype(BF16)
    rows = outs[0].shape[0]
    for r, o in enumerate(outs):
        for q in range(len(outs)):

            @pl.when(place_ref[r] == q * rows)
            def _():
                o[...] = y[q * rows : (q + 1) * rows]


def raw_back(places, u, raw, scales, inner, gains, dv, w, pieces):
    t, n = dv.shape
    p, _, ds, _ = w.shape
    d = p * ds
    pb = max(1, 2 * TILE // ds)
    return call(
        raw_back_kernel,
        "raw_back",
        (p // pb,),
        [
            fixed((2, t, n)),
            fixed((2, t, n)),
            fixed((2, t, 1)),
            fixed((2, t, 1)),
            fixed((2, 1, n)),
            fixed((t, n)),
            pl.BlockSpec((pb, 3, ds, n), lambda g, *_: (g, 0, 0, 0)),
        ],
        [pl.BlockSpec((t, 3 * n), lambda g, *_: (0, 0))]
        + [pl.BlockSpec((t // pieces, pb * ds), lambda g, *_: (0, g))] * pieces,
        [sds((t, 3 * n), BF16)] + [sds((t // pieces, d), BF16)] * pieces,
        6 * t * d * n,
        2 * (3 * d * n + t * d) + 20 * t * n,
        prefetch=1,
    )(places, u, raw, scales, inner, gains, dv, w)


def qkv_grad_kernel(n_ref, d_ref, kept_ref, o_ref):
    pb, _, ds, n = o_ref.shape
    grads = tn(n_ref[...], d_ref[...]).astype(BF16)
    for c in range(3):
        o_ref[:, c] = grads[:, c * n : (c + 1) * n].reshape(pb, ds, n)


def qkv_grads(normed, grad, kept, p):
    t, d = normed.shape
    n = grad.shape[1] // 3
    ds = d // p
    pb = max(1, TILE // ds)
    return call(
        qkv_grad_kernel,
        "qkv_grad",
        (p // pb,),
        [
            pl.BlockSpec((t, pb * ds), lambda g: (0, g)),
            fixed((t, 3 * n)),
            pl.BlockSpec(memory_space=pl.ANY),
        ],
        pl.BlockSpec((pb, 3, ds, n), lambda g: (g, 0, 0, 0)),
        sds(kept.shape, BF16),
        6 * t * d * n,
        2 * (3 * d * n + t * d + 3 * t * n),
        aliases={2: 0},
    )(normed, grad, kept)


def swap(value, axis):
    return lax.ppermute(value, axis, [(0, 1), (1, 0)])


def spread(value):
    rows = swap(value, "row")
    return (value, swap(value, "core"), rows, swap(rows, "core"))


def across(value, k):
    size = lax.axis_size("tp")
    return lax.ppermute(value, "tp", [(i, i ^ k) for i in range(size)])


def total(pieces):
    return sum(v.astype(F32) for v in pieces)


def add(*values):
    return total(values).astype(values[0].dtype)


def cut(value, pieces):
    rows = value.shape[0] // pieces
    return [value[r * rows : (r + 1) * rows] for r in range(pieces)]


def join(*pieces):
    return jnp.concatenate(pieces, 0)


class Line:
    def __init__(self):
        self.last = None

    def __call__(self, step, *operands):
        leaves, form = jax.tree.flatten(operands)
        spots = [i for i, v in enumerate(leaves) if isinstance(v, jax.Array)]
        if self.last is not None:
            kept, self.last = lax.optimization_barrier(([leaves[i] for i in spots], self.last))
            for i, v in zip(spots, kept):
                leaves[i] = v
        result = step(*jax.tree.unflatten(form, leaves))
        self.last = jax.tree.leaves(result)
        return result

    def sums(self, own, core, pieces, first=None):
        mine, theirs = cut(own, pieces), cut(swap(core, "core"), pieces)
        last = across(self(add, mine[3], theirs[3]), 1)
        near = self(add, mine[2], theirs[2], last)
        beside, first = self(lambda a, b, c, d: (add(a, b), add(c, d)), mine[1], theirs[1], mine[0], theirs[0])
        return [first, across(beside, 1), across(near, 2)]


def in_place_kernel(place_ref, *refs, count):
    for r, piece in enumerate(refs[:count]):

        @pl.when(pl.program_id(0) == r)
        def _():
            refs[-1][...] = piece[...]


def in_place(places, pieces, kept, total_rows):
    rows, d = pieces[0].shape
    count = len(pieces)
    return call(
        functools.partial(in_place_kernel, count=count),
        "inplace",
        (count,),
        [fixed((rows, d))] * count + [pl.BlockSpec(memory_space=pl.ANY)] * len(kept),
        pl.BlockSpec((rows, d), lambda r, place: (place[r] // rows, 0)),
        sds((total_rows, d), pieces[0].dtype),
        0,
        4 * rows * count * d,
        prefetch=1,
        aliases={1 + count: 0} if kept else None,
    )(places, *pieces, *kept)


def meet(value):
    value = value + across(value, 1)
    return value + across(value, 2)


def relative(value, places, pieces):
    rows = value.shape[0] // pieces
    return [lax.dynamic_slice_in_dim(value, places[r], rows, 0) for r in range(pieces)]


def body(
    inputs,
    prefix,
    expert_ids,
    norm_gains,
    qkv_weight,
    out_weight,
    router_weight,
    gate_up_weight,
    down_weight,
    cotangent,
    *,
    chunks,
):
    sequences, length, width = inputs.shape
    t = sequences * length
    tp = lax.axis_size("tp")
    quarter = t // tp
    column = lax.axis_index("tp")
    core = lax.axis_index("core")
    ctx = lax.axis_index("row") * 2 + core
    experts = router_weight.shape[1]
    group = experts // 2
    starts = [sum(chunks[:k]) for k in range(len(chunks))]
    x = inputs.reshape(t, width)
    places = jnp.stack([column ^ r for r in range(tp)]).astype(jnp.int32) * quarter
    x_q = lax.dynamic_slice_in_dim(x, column * quarter, quarter, 0)

    line = Line()
    attn_local = jnp.concatenate([qkv_weight, out_weight[None]], 0)
    attn_w = lax.all_gather(attn_local, PLANE, axis=0, tiled=False)
    triple = jnp.concatenate([gate_up_weight, down_weight[:, None]], 1)
    ds, f = triple.shape[2:]
    grouped = triple.reshape(2, group, 3, ds, f)
    ws = []
    for begin, e in zip(starts, chunks):
        mine = lax.all_to_all(grouped[:, begin : begin + e], "core", 0, 0, tiled=True)
        ws.append(lax.all_gather(mine, FR, axis=0, tiled=False).reshape(-1, e, 3, ds, f))
    gains_low = lax.all_gather(norm_gains, PLANE, axis=1, tiled=True)
    router = lax.all_gather(router_weight, PLANE, axis=0, tiled=True)
    cots = relative(cotangent.reshape(t, width), places, tp)
    c0 = join(*cots)
    c1 = swap(c0, "core")
    attn_w, gains_low, router, c0 = lax.optimization_barrier((attn_w, gains_low, router, c0))
    p = attn_w.shape[0]

    gains = gains_low.astype(F32)
    n = attn_w.shape[3]
    router_rows = jnp.concatenate([router.T, jnp.zeros((128 - experts, width), BF16)], 0)

    own_gains = lax.dynamic_slice_in_dim(gains[2:4], column * n, n, 1)[:, None, :]
    halves = jnp.arange(0, HEAD_DIM, 2).astype(F32) / HEAD_DIM
    inverse = 1.0 / THETA**halves
    positions = ctx * length + jnp.arange(length, dtype=jnp.int32)
    angles = positions.astype(F32)[:, None] * inverse[None, :]
    cosine = jnp.concatenate([jnp.cos(angles)] * 2, 1)
    sine = jnp.concatenate([-jnp.sin(angles), jnp.sin(angles)], 1)
    offsets = jnp.stack([ctx, ctx ^ 1, ctx ^ 2, ctx ^ 3, ctx]).astype(jnp.int32) * length
    scal = jnp.concatenate([offsets, prefix.astype(jnp.int32)])
    ids_q = lax.dynamic_slice_in_dim(expert_ids.reshape(t, -1), column * quarter, quarter, 0)
    normed_one, raw, values, squares = line(qkv_project, x, gains[0:1], attn_w)
    v_blocks = spread(values)
    scales = lax.rsqrt(meet(squares[:, :, 0]) / width + EPSILON)[:, :, None]
    scales, values = lax.optimization_barrier((scales, v_blocks[2]))
    v_blocks = v_blocks[:2] + (values,) + v_blocks[3:]
    queries, keys = line(prepare, raw, scales, own_gains, cosine, sine)
    k_blocks = spread(keys)
    blocks = k_blocks + v_blocks
    heads = line(attend, scal, queries, blocks, length)
    sums = line(project_out, places, heads, attn_w, tp)
    near = line(add, sums[2], across(sums[3], 1))
    sums = [sums[0], across(sums[1], 1), across(near, 2)]
    mid, ext, probs, chosen = line(norm_two, x_q, sums, gains[1:2], router_rows, ids_q, experts)
    far = across(ext, 2)
    near = across(ext, 1)
    x0 = line(join, ext, near, far, across(far, 1))
    x1 = swap(x0, "core")

    xs, cs = [x0, x1], [c0, c1]
    blocks_in = jnp.arange(width // TILE, dtype=jnp.int32)
    hid, dgu, side, grads = [], [], [], []
    dx = []

    def up(k):
        first = (core * group + starts[k]).astype(jnp.int32)[None]
        for kept, made in zip((hid, dgu, side), line(expert_up, first, xs, cs, ws[k])):
            kept.append(made)

    def back(k, before):
        gates = side if k == len(chunks) - 1 else []
        return line(expert_down, [dgu[k]], [ws[k]], 0, 2, gates, before, 2, "expert_dx")

    def weight_grad(k):
        return line(expert_grads, xs, cs, hid[k], dgu[k], p, chunks[k])

    def to_owners(made, k, after):
        made, after = lax.optimization_barrier((made, after))
        made = made.reshape(-1, 2, chunks[k], 3, ds, f)
        return lax.optimization_barrier(lax.psum_scatter(made, FR, scatter_dimension=0, tiled=False))

    for k in range(len(chunks)):
        up(k)
        dx = back(k, dx)
        if k < len(chunks) - 1:
            made = weight_grad(k)
            grads.append(to_owners(made, k, ()))
    d_normed = line.sums(*dx, tp)
    moe = line(expert_down, hid, ws, 2, 1, [], [], 2, "expert_out")

    d_mid, d_mid_low, gain_two, grad_router = line(
        norm_two_back, d_normed, mid, ext, probs, chosen, cots[0], gains[1:2], router_rows
    )
    far = across(d_mid_low, 2)
    near = across(d_mid_low, 1)
    late = weight_grad(len(chunks) - 1)
    d_mid_low = line(join, d_mid_low, near, far, across(far, 1))
    own, beside = cut(moe[0], tp), cut(swap(moe[1], "core"), tp)
    last = across(line(add, own[3], beside[3]), 1)

    d_heads = line(heads_grad, places, d_mid_low, attn_w, tp)
    grads.append(to_owners(late, len(chunks) - 1, d_heads))
    dq, b0, b1, b2, b3 = line(attend_back, scal, queries, blocks, d_heads, length)
    r1 = swap(b1, "core")
    r3 = swap(b3, "core")
    near = line(add, own[2], beside[2], last)
    next_one = line(add, own[1], beside[1])
    moe = [across(next_one, 1), across(near, 2)]
    r2 = swap(line(add, b2, r3), "row")
    grad_attn = line(out_weight_grad, places, d_mid_low, heads, p, tp)
    out = line(lambda *v: total(v).astype(BF16), mid, own[0], beside[0], *moe)
    out_far = across(out, 2)
    out_near = across(out, 1)
    def parted(k):
        own, other = line(
            lambda v: [lax.dynamic_index_in_dim(v, c, 0, keepdims=False) for c in (core, core ^ 1)], grads[k]
        )
        return own, swap(other, "core")

    def settled(k, pair, kept):
        steps = jnp.arange(chunks[k] // 2, dtype=jnp.int32)
        spots = jnp.concatenate([(c * group + starts[k]) // 2 + steps for c in (core, core ^ 1)])
        return line(settle, spots.astype(jnp.int32), pair, kept, experts)

    pairs = [parted(0)]
    d_kv = line(lambda *v: total(v), b0, r1, r2)
    out_far, d_kv = lax.optimization_barrier((out_far, d_kv))
    out_both = across(out_far, 1)
    u, inner, gain_qk = line(unturn, dq, d_kv[0], raw, scales, own_gains, cosine, sine)
    outputs = line(in_place, places, [out, out_near, out_far, out_both], [], t).reshape(inputs.shape)

    inner = (meet(inner[:, :, 0]) / width)[:, :, None]
    d_raw, *d_one = line(
        raw_back, places, u, raw, scales, inner, own_gains, d_kv[1].astype(BF16), attn_w, tp
    )
    last = across(d_one[3], 1)
    grad_attn = line(qkv_grads, normed_one, d_raw, grad_attn, p)
    grad_attn = lax.psum_scatter(grad_attn, PLANE, scatter_dimension=0, tiled=False)
    near = line(add, d_one[2], last)
    d_one = [d_one[0], across(d_one[1], 1), across(near, 2)]
    grad_in, gain_one = line(norm_one_back, d_one, x_q, d_mid, gains[0:1])
    far = across(grad_in, 2)
    near = across(grad_in, 1)
    placed = lax.dynamic_update_slice_in_dim(
        jnp.zeros((2, width), F32), gain_qk[:, 0, :], column * n, 1
    )

    small = line(lambda *v: jnp.concatenate(v, 0), grad_router[:experts], gain_one, gain_two, placed)
    rows = small.shape[0]
    small = small.reshape(rows, p, ds).transpose(1, 0, 2)
    small = jnp.sum(lax.all_to_all(small, PLANE, 0, 0, tiled=True), 0)
    other = across(small, 1)
    both = across(far, 1)
    kept = settled(0, pairs[0], [])
    placed_in = line(in_place, places[:2], [grad_in, near], [], t)
    pairs.append(parted(1))
    owned_gate_up, owned_down = settled(1, pairs[1], kept)
    small = line(lambda a, b: a + b, small, other)
    other = across(small, 2)
    grad_inputs = line(in_place, places[2:], [far, both], [placed_in], t).reshape(inputs.shape)
    grad_attn, grad_inputs = lax.optimization_barrier((grad_attn, grad_inputs))
    small = line(lambda a, b: a + b, small, other)
    owned_gains = small[experts:]
    owned_router = small[:experts].T
    return (
        outputs,
        grad_inputs,
        owned_gains,
        grad_attn[:3].astype(F32),
        grad_attn[3].astype(F32),
        owned_router,
        owned_gate_up,
        owned_down,
    )


def solution(mesh):
    fsdp, ctx, tp = (mesh.shape[a] for a in ("fsdp", "ctx", "tp"))
    fine = Mesh(mesh.devices.reshape(fsdp, ctx // 2, 2, tp), EVERY)
    tokens = P("fsdp", ("row", "core"), None)
    weights = (
        P(None, PLANE),
        P(None, PLANE, "tp"),
        P(PLANE, "tp"),
        P(PLANE, None),
        P(None, None, PLANE, "tp"),
        P(None, PLANE, "tp"),
    )
    return jax.shard_map(
        functools.partial(body, chunks=(6, 2)),
        mesh=fine,
        in_specs=(tokens, P("fsdp"), tokens) + weights + (tokens,),
        out_specs=(tokens, tokens) + weights,
        check_vma=False,
    )
```

```python
import functools

import jax
import jax.numpy as jnp
from jax import lax
from jax.experimental import pallas as pl
from jax.experimental.pallas import tpu as pltpu
from jax.sharding import Mesh, PartitionSpec as P

HEAD_DIM = 128
EPSILON = 1e-05
THETA = 10000.0
TILE = 256
F32 = jnp.float32
BF16 = jnp.bfloat16
FR = ("fsdp", "row")
LANES = 128
PLANE = ("fsdp", "row", "core")
EVERY = ("fsdp", "row", "core", "tp")


def nn(a, b):
    return lax.dot_general(a, b, (((1,), (0,)), ((), ())), preferred_element_type=F32)


def nt(a, b):
    return lax.dot_general(a, b, (((1,), (1,)), ((), ())), preferred_element_type=F32)


def tn(a, b):
    return lax.dot_general(a, b, (((0,), (0,)), ((), ())), preferred_element_type=F32)


def call(kernel, name, grid, in_specs, out_specs, out_shape, flops, moved, scratch=(), prefetch=0, limit=56, aliases=None):
    return pl.pallas_call(
        kernel,
        name=name,
        out_shape=out_shape,
        grid_spec=pltpu.PrefetchScalarGridSpec(
            num_scalar_prefetch=prefetch,
            grid=grid,
            in_specs=in_specs,
            out_specs=out_specs,
            scratch_shapes=list(scratch),
        ),
        input_output_aliases=aliases or {},
        compiler_params=pltpu.CompilerParams(
            dimension_semantics=("arbitrary",) * len(grid), vmem_limit_bytes=limit << 20
        ),
        cost_estimate=pl.CostEstimate(flops=int(flops), bytes_accessed=int(moved), transcendentals=0),
    )


def fixed(shape):
    return pl.BlockSpec(shape, lambda *a: (0,) * len(shape), pipeline_mode=pl.Buffered(1))


def sds(shape, dtype):
    return jax.ShapeDtypeStruct(shape, dtype)


def qkv_kernel(x_ref, g_ref, w_ref, n_ref, raw_ref, v_ref, sq_ref):
    c = pl.program_id(0)

    @pl.when(c == 0)
    def _():
        x = x_ref[...].astype(F32)
        r = lax.rsqrt(jnp.mean(x * x, -1, keepdims=True) + EPSILON)
        n_ref[...] = (x * r * g_ref[...]).astype(BF16)

    w = w_ref[...]
    y = nn(n_ref[...], w.reshape(w.shape[0] * w.shape[2], w.shape[3]))

    @pl.when(c < 2)
    def _():
        raw_ref[0] = y
        sq_ref[0] = jnp.broadcast_to(jnp.sum(y * y, -1, keepdims=True), sq_ref.shape[1:])

    @pl.when(c == 2)
    def _():
        v_ref[...] = y.astype(BF16)


def qkv_project(x, gain, w):
    t, d = x.shape
    p, _, ds, n = w.shape
    return call(
        qkv_kernel,
        "qkv",
        (3,),
        [
            fixed((t, d)),
            fixed((1, d)),
            pl.BlockSpec((p, 1, ds, n), lambda c: (0, c, 0, 0)),
        ],
        [
            pl.BlockSpec((t, d), lambda c: (0, 0)),
            pl.BlockSpec((1, t, n), lambda c: (jnp.minimum(c, 1), 0, 0)),
            pl.BlockSpec((t, n), lambda c: (0, 0)),
            pl.BlockSpec((1, t, 128), lambda c: (jnp.minimum(c, 1), 0, 0)),
        ],
        [sds((t, d), BF16), sds((2, t, n), F32), sds((t, n), BF16), sds((2, t, 128), F32)],
        6 * t * d * n,
        2 * (3 * d * n + 2 * t * d) + 10 * t * n,
    )(x, gain, w)


def turn(v, cosine, sine):
    half = v.shape[-1] // 2
    return v * cosine + pltpu.roll(v, half, 1) * sine


def prep_kernel(raw_ref, s_ref, g_ref, cos_ref, sin_ref, q_ref, k_ref):
    reps = raw_ref.shape[1] // cos_ref.shape[0]
    cosine = jnp.concatenate([cos_ref[...]] * reps, 0)
    sine = jnp.concatenate([sin_ref[...]] * reps, 0)
    q = raw_ref[0] * s_ref[0] * g_ref[0]
    k = raw_ref[1] * s_ref[1] * g_ref[1]
    q_ref[...] = turn(q, cosine, sine).astype(BF16)
    k_ref[...] = turn(k, cosine, sine).astype(BF16)


def prepare(raw, scales, gains, cosine, sine):
    _, t, n = raw.shape
    h = HEAD_DIM
    length = cosine.shape[0]
    return call(
        prep_kernel,
        "prep",
        (n // h,),
        [
            pl.BlockSpec((2, t, h), lambda i: (0, 0, i)),
            fixed((2, t, 1)),
            pl.BlockSpec((2, 1, h), lambda i: (0, 0, i)),
            fixed((length, h)),
            fixed((length, h)),
        ],
        [pl.BlockSpec((t, h), lambda i: (0, i))] * 2,
        [sds((t, n), BF16)] * 2,
        20 * t * n,
        12 * t * n,
    )(raw, scales, gains, cosine, sine)


def masked_probs(s, scal_ref, q, ks):
    length = q.shape[0]
    prefix = scal_ref[5 + s]
    rows = lax.broadcasted_iota(jnp.int32, (length, length), 0) + scal_ref[4]
    columns = lax.broadcasted_iota(jnp.int32, (length, length), 1)
    pieces = []
    for b, k in enumerate(ks):
        place = columns + scal_ref[b]
        visible = (place <= rows) | (place < prefix)
        pieces.append(jnp.where(visible, nt(q, k) * HEAD_DIM ** (-0.5), -1e30))
    scores = jnp.concatenate(pieces, 1)
    expo = jnp.exp(scores - jnp.max(scores, -1, keepdims=True))
    return expo / jnp.sum(expo, -1, keepdims=True)


def attend_kernel(scal_ref, q_ref, *refs):
    o_ref = refs[8]
    probs = masked_probs(pl.program_id(0), scal_ref, q_ref[...], [r[...] for r in refs[:4]])
    v = jnp.concatenate([r[...] for r in refs[4:8]], 0)
    o_ref[...] = nn(probs.astype(BF16), v).astype(BF16)


def attend(scal, q, blocks, length):
    t, n = q.shape
    h = HEAD_DIM
    one = pl.BlockSpec((length, h), lambda s, i, *_: (s, i))
    return call(
        attend_kernel,
        "attend",
        (t // length, n // h),
        [one] * 9,
        one,
        sds((t, n), BF16),
        16 * t * n * length,
        24 * t * n,
        prefetch=1,
    )(scal, q, *blocks)


def attend_back_kernel(scal_ref, q_ref, *refs):
    g_ref, dq_ref, outs = refs[8], refs[9], refs[10:]
    length = q_ref.shape[0]
    q = q_ref[...]
    grad = g_ref[...]
    probs = masked_probs(pl.program_id(0), scal_ref, q, [r[...] for r in refs[:4]])
    k = jnp.concatenate([r[...] for r in refs[:4]], 0)
    v = jnp.concatenate([r[...] for r in refs[4:8]], 0)
    d_probs = nt(grad, v)
    inner = jnp.sum(probs * d_probs, -1, keepdims=True)
    d_scores = (probs * (d_probs - inner)).astype(BF16)
    scale = HEAD_DIM ** (-0.5)
    dq_ref[...] = nn(d_scores, k) * scale
    dk = (tn(d_scores, q) * scale).astype(BF16)
    dv = tn(probs.astype(BF16), grad).astype(BF16)
    for b, o in enumerate(outs):
        o[0] = dk[b * length : (b + 1) * length]
        o[1] = dv[b * length : (b + 1) * length]


def attend_back(scal, q, blocks, grad, length):
    t, n = q.shape
    h = HEAD_DIM
    one = pl.BlockSpec((length, h), lambda s, i, *_: (s, i))
    two = pl.BlockSpec((2, length, h), lambda s, i, *_: (0, s, i))
    return call(
        attend_back_kernel,
        "attend_back",
        (t // length, n // h),
        [one] * 10,
        [one] + [two] * 4,
        [sds((t, n), F32)] + [sds((2, t, n), BF16)] * 4,
        40 * t * n * length,
        48 * t * n,
        prefetch=1,
    )(scal, q, *blocks, grad)


def out_kernel(place_ref, h_ref, w_ref, *outs):
    w = w_ref[...]
    w = w.reshape(-1, w.shape[-1])
    rows = outs[0].shape[0]
    heads = jnp.concatenate(
        [h_ref[pl.ds(pl.multiple_of(place_ref[r], rows), rows), :] for r in range(len(outs))], 0
    )
    y = nt(heads, w).astype(BF16)
    for r, o in enumerate(outs):
        o[...] = y[r * rows : (r + 1) * rows]


def project_out(places, heads, w, pieces):
    t, n = heads.shape
    p, _, ds, _ = w.shape
    pb = max(1, 2 * TILE // ds)
    return call(
        out_kernel,
        "outproj",
        (p // pb,),
        [fixed((t, n)), pl.BlockSpec((pb, 1, ds, n), lambda g, *_: (g, 3, 0, 0))],
        [pl.BlockSpec((t // pieces, pb * ds), lambda g, *_: (0, g))] * pieces,
        [sds((t // pieces, p * ds), BF16)] * pieces,
        2 * t * n * p * ds,
        2 * (t * n + n * p * ds + t * p * ds),
        prefetch=1,
    )(places, heads, w)


def d_heads_kernel(place_ref, g_ref, w_ref, o_ref, *, pieces):
    w = w_ref[...]
    y = nn(g_ref[...], w.reshape(w.shape[0] * w.shape[2], w.shape[3])).astype(BF16)
    rows = y.shape[0] // pieces
    for r in range(pieces):
        o_ref[pl.ds(pl.multiple_of(place_ref[r], rows), rows), :] = y[r * rows : (r + 1) * rows]


def heads_grad(places, grad, w, pieces):
    t, d = grad.shape
    p, _, ds, n = w.shape
    return call(
        functools.partial(d_heads_kernel, pieces=pieces),
        "dheads",
        (1,),
        [fixed((t, d)), pl.BlockSpec((p, 1, ds, n), lambda g, *_: (0, 3, 0, 0), pipeline_mode=pl.Buffered(1))],
        fixed((t, n)),
        sds((t, n), BF16),
        2 * t * n * d,
        2 * (t * n + n * d + t * d),
        prefetch=1,
    )(places, grad, w)


def grad_out_kernel(place_ref, g_ref, h_ref, o_ref, *, pieces):
    rows = g_ref.shape[0] // pieces
    heads = jnp.concatenate(
        [h_ref[pl.ds(pl.multiple_of(place_ref[r], rows), rows), :] for r in range(pieces)], 0
    )
    o_ref[...] = tn(g_ref[...], heads).astype(BF16).reshape(o_ref.shape)


def out_weight_grad(places, grad, heads, p, pieces):
    t, d = grad.shape
    n = heads.shape[1]
    ds = d // p
    pb = max(1, TILE // ds)
    return call(
        functools.partial(grad_out_kernel, pieces=pieces),
        "gradout",
        (p // pb,),
        [pl.BlockSpec((t, pb * ds), lambda g, *_: (0, g)), fixed((t, n))],
        pl.BlockSpec((pb, 1, ds, n), lambda g, *_: (g, 3, 0, 0)),
        sds((p, 4, ds, n), BF16),
        2 * t * n * d,
        2 * (t * n + n * d + t * d),
        prefetch=1,
    )(places, grad, heads)


def norm_two_kernel(x_ref, a_ref, b_ref, c_ref, g_ref, w_ref, ids_ref, mid_ref, ext_ref, probs_ref, chosen_ref, *, experts):
    mid = x_ref[...].astype(F32) + a_ref[...].astype(F32) + b_ref[...].astype(F32) + c_ref[...].astype(F32)
    mid_ref[...] = mid
    d = mid.shape[1]
    r = lax.rsqrt(jnp.mean(mid * mid, -1, keepdims=True) + EPSILON)
    low = (mid * r * g_ref[...]).astype(BF16)
    ext_ref[:, :d] = low
    logits = nt(low, w_ref[...])
    lane = lax.broadcasted_iota(jnp.int32, logits.shape, 1)
    logits = jnp.where(lane < experts, logits, -1e30)
    expo = jnp.exp(logits - jnp.max(logits, -1, keepdims=True))
    probs = expo / jnp.sum(expo, -1, keepdims=True)
    chosen = jnp.zeros_like(probs)
    for j in range(ids_ref.shape[1]):
        chosen += (ids_ref[:, j : j + 1] == lane).astype(F32)
    probs_ref[...] = probs
    chosen_ref[...] = chosen
    gates = probs * chosen
    high = gates.astype(BF16)
    rest = (gates - high.astype(F32)).astype(BF16)
    ext_ref[:, d:] = jnp.concatenate([high[:, : LANES // 2], rest[:, : LANES // 2]], 1)


def norm_two(x, sums, gain, router, ids, experts):
    t, d = x.shape
    return call(
        functools.partial(norm_two_kernel, experts=experts),
        "norm_two",
        (1,),
        [fixed((t, d))] * 4 + [fixed((1, d)), fixed(router.shape), fixed(ids.shape)],
        [fixed((t, d)), fixed((t, d + LANES)), fixed((t, LANES)), fixed((t, LANES))],
        [sds((t, d), F32), sds((t, d + LANES), BF16), sds((t, LANES), F32), sds((t, LANES), F32)],
        2 * t * d * LANES,
        14 * t * d,
    )(x, *sums, gain, router, ids)


def norm_two_back_kernel(a_ref, b_ref, c_ref, mid_ref, ext_ref, probs_ref, chosen_ref, cot_ref, g_ref, w_ref, *outs):
    mid_grad_ref, low_ref, gain_ref, router_ref = outs
    d = mid_ref.shape[1]
    du = a_ref[...].astype(F32) + b_ref[...].astype(F32) + c_ref[...].astype(F32)
    probs = probs_ref[...]
    masked = du[:, d:] * chosen_ref[...]
    d_logits = (probs * (masked - jnp.sum(probs * masked, -1, keepdims=True))).astype(BF16)
    router_ref[...] = tn(d_logits, ext_ref[:, :d])
    u = du[:, :d] + nn(d_logits, w_ref[...])
    mid = mid_ref[...]
    r = lax.rsqrt(jnp.mean(mid * mid, -1, keepdims=True) + EPSILON)
    hat = mid * r
    gain_ref[...] = jnp.sum(u * hat, 0, keepdims=True)
    w = u * g_ref[...]
    grad = cot_ref[...].astype(F32) + r * (w - hat * jnp.mean(w * hat, -1, keepdims=True))
    mid_grad_ref[...] = grad
    low_ref[...] = grad.astype(BF16)


def norm_two_back(sums, mid, ext, probs, chosen, cot, gain, router):
    t, d = mid.shape
    wide = fixed((t, d + LANES))
    return call(
        norm_two_back_kernel,
        "norm_two_back",
        (1,),
        [wide] * 3
        + [fixed((t, d)), wide, fixed((t, LANES)), fixed((t, LANES)), fixed((t, d)), fixed((1, d)), fixed(router.shape)],
        [fixed((t, d)), fixed((t, d)), fixed((1, d)), fixed((LANES, d))],
        [sds((t, d), F32), sds((t, d), BF16), sds((1, d), F32), sds((LANES, d), F32)],
        4 * t * d * LANES,
        20 * t * d,
    )(*sums, mid, ext, probs, chosen, cot, gain, router)


def norm_one_back_kernel(a_ref, b_ref, c_ref, x_ref, mid_grad_ref, g_ref, o_ref, gain_ref):
    u = a_ref[...].astype(F32) + b_ref[...].astype(F32) + c_ref[...].astype(F32)
    x = x_ref[...].astype(F32)
    r = lax.rsqrt(jnp.mean(x * x, -1, keepdims=True) + EPSILON)
    hat = x * r
    gain_ref[...] = jnp.sum(u * hat, 0, keepdims=True)
    w = u * g_ref[...]
    o_ref[...] = (mid_grad_ref[...] + r * (w - hat * jnp.mean(w * hat, -1, keepdims=True))).astype(BF16)


def norm_one_back(sums, x, mid_grad, gain):
    t, d = x.shape
    return call(
        norm_one_back_kernel,
        "norm_one_back",
        (1,),
        [fixed((t, d))] * 5 + [fixed((1, d))],
        [fixed((t, d)), fixed((1, d))],
        [sds((t, d), BF16), sds((1, d), F32)],
        20 * t * d,
        14 * t * d,
    )(*sums, x, mid_grad, gain)


def expert_kernel(first_ref, *refs, parts):
    xs, cs, w_ref = refs[:parts], refs[parts : 2 * parts], refs[2 * parts]
    hid_ref, dgu_ref, dg_ref = refs[2 * parts + 1 :]
    e = pl.program_id(0)
    t = cs[0].shape[0]
    d = cs[0].shape[1]

    @pl.when(e == 0)
    def _():
        dg_ref[...] = jnp.zeros_like(dg_ref)

    f = w_ref.shape[4]
    me = first_ref[0] + e
    lane = lax.broadcasted_iota(jnp.int32, (t, LANES), 1)
    for part, (x_ref, c_ref) in enumerate(zip(xs, cs)):

        def block(x_ref=x_ref, c_ref=c_ref, to=slice(part * t, (part + 1) * t)):
            x = x_ref[:, :d]
            a = nn(x, w_ref[:, 0, 0].reshape(d, f))
            b = nn(x, w_ref[:, 0, 1].reshape(d, f))
            dh = nn(c_ref[...], w_ref[:, 0, 2].reshape(d, f))
            mine = (lane == me) | (lane == me + LANES // 2)
            gate = jnp.sum(jnp.where(mine, x_ref[:, d:].astype(F32), 0.0), -1, keepdims=True)
            sigma = jax.nn.sigmoid(a)
            swish = a * sigma
            act = swish * b
            hid_ref[to, :] = (gate * act).astype(BF16)
            d_gate = jnp.sum(dh * act, -1, keepdims=True)
            dg_ref[to, :] += jnp.where(lane == me, d_gate, 0.0)
            inner = dh * gate
            dgu_ref[to, :f] = (inner * b * sigma * (1.0 + a * (1.0 - sigma))).astype(BF16)
            dgu_ref[to, f:] = (inner * swish).astype(BF16)

        block()


def expert_up(first, xs, cs, w):
    t, d = cs[0].shape
    parts = len(cs)
    p, e, _, ds, f = w.shape
    every = parts * t
    return call(
        functools.partial(expert_kernel, parts=parts),
        "expert_up",
        (e,),
        [fixed(x.shape) for x in xs]
        + [fixed((t, d))] * parts
        + [pl.BlockSpec((p, 1, 3, ds, f), lambda i, *_: (0, i, 0, 0, 0))],
        [
            pl.BlockSpec((every, f), lambda i, *_: (0, i)),
            pl.BlockSpec((every, 2 * f), lambda i, *_: (0, i)),
            pl.BlockSpec((every, LANES), lambda i, *_: (0, 0)),
        ],
        [sds((every, e * f), BF16), sds((every, e * 2 * f), BF16), sds((every, LANES), F32)],
        6 * every * d * f * e,
        2 * (3 * d * f * e + 2 * every * d + 3 * every * f * e),
        prefetch=1,
    )(first, *xs, *cs, w)


def expert_grad_kernel(*refs, parts):
    xs, cs, hid_ref, dgu_ref, o_ref = refs[:parts], refs[parts : 2 * parts], *refs[2 * parts :]
    pb, e, _, ds, f = o_ref.shape
    x = jnp.concatenate([r[...] for r in xs], 0)
    c = jnp.concatenate([r[...] for r in cs], 0)
    both = tn(x, dgu_ref[...]).astype(BF16)
    down = tn(c, hid_ref[...]).astype(BF16)
    for i in range(e):
        o_ref[:, i, 0] = both[:, 2 * i * f : (2 * i + 1) * f].reshape(pb, ds, f)
        o_ref[:, i, 1] = both[:, (2 * i + 1) * f : (2 * i + 2) * f].reshape(pb, ds, f)
        o_ref[:, i, 2] = down[:, i * f : (i + 1) * f].reshape(pb, ds, f)


def expert_grads(xs, cs, hid, dgu, p, e):
    t, d = cs[0].shape
    parts = len(cs)
    ds = d // p
    f = hid.shape[1] // e
    pb = max(1, TILE // ds)
    column = pl.BlockSpec((t, pb * ds), lambda g: (0, g))
    return call(
        functools.partial(expert_grad_kernel, parts=parts),
        "expert_grad",
        (p // pb,),
        [column] * (2 * parts) + [fixed(hid.shape), fixed(dgu.shape)],
        pl.BlockSpec((pb, e, 3, ds, f), lambda g: (g, 0, 0, 0, 0)),
        sds((p, e, 3, ds, f), BF16),
        6 * parts * t * d * f * e,
        2 * (3 * d * f * e + 2 * parts * t * d + 3 * parts * t * f * e),
    )(*xs, *cs, hid, dgu)


def settle_kernel(spot_ref, *refs, pieces):
    gate_up_ref, down_ref = refs[-2:]
    each = pl.num_programs(0) // pieces
    for r in range(pieces):

        @pl.when(pl.program_id(0) // each == r)
        def _():
            gate_up_ref[...] = refs[r][:, :2].astype(F32)
            down_ref[...] = refs[r][:, 2].astype(F32)


def settle(spots, pieces, kept, experts):
    e, _, ds, f = pieces[0].shape
    count = len(pieces)
    each = e // 2

    def piece(r):
        return pl.BlockSpec((2, 3, ds, f), lambda g, spot: (jnp.clip(g - r * each, 0, each - 1), 0, 0, 0))

    return call(
        functools.partial(settle_kernel, pieces=count),
        "settle",
        (count * each,),
        [piece(r) for r in range(count)] + [pl.BlockSpec(memory_space=pl.ANY)] * len(kept),
        [
            pl.BlockSpec((2, 2, ds, f), lambda g, spot: (spot[g], 0, 0, 0)),
            pl.BlockSpec((2, ds, f), lambda g, spot: (spot[g], 0, 0)),
        ],
        [sds((experts, 2, ds, f), F32), sds((experts, ds, f), F32)],
        0,
        18 * count * e * ds * f,
        prefetch=1,
        aliases={1 + count + i: i for i in range(len(kept))},
    )(spots, *pieces, *kept)


def down_kernel(*refs, planes, chunks, sides, begun):
    acts, ws = refs[:chunks], refs[chunks : 2 * chunks]
    gates = refs[2 * chunks : 2 * chunks + sides]
    before = refs[2 * chunks + sides : 2 * chunks + sides + begun]
    outs = refs[2 * chunks + sides + begun :]
    g = pl.program_id(0)
    pb, _, _, ds, f = ws[0].shape
    wide = pb * ds
    rows = outs[0].shape[0]
    joined = [
        jnp.concatenate([w[:, i, c].reshape(wide, f) for i in range(w.shape[1]) for c in range(planes)], 1)
        for w in ws
    ]
    to = pl.ds(pl.multiple_of(g * wide, wide), wide)
    for part, o in enumerate(outs):
        own = slice(part * rows, (part + 1) * rows)
        value = sum(nt(a[own, :], w) for a, w in zip(acts, joined))
        if begun:
            value += before[part][...].astype(F32)
        o[:, to] = value.astype(BF16)
    if sides:

        @pl.when(g == 0)
        def _():
            for part, o in enumerate(outs):
                own = slice(part * rows, (part + 1) * rows)
                o[:, o.shape[1] - LANES :] = sum(s[own, :] for s in gates).astype(BF16)


def expert_down(acts, ws, plane, planes, gates, before, parts, name):
    every = acts[0].shape[0]
    p, _, _, ds, f = ws[0].shape
    k = sum(a.shape[1] for a in acts)
    t = every // parts
    chunks = len(acts)
    d = p * ds + (LANES if gates else 0)
    pb = max(1, 2 * TILE // ds)
    return call(
        functools.partial(down_kernel, planes=planes, chunks=chunks, sides=len(gates), begun=len(before)),
        name,
        (p // pb,),
        [fixed(a.shape) for a in acts]
        + [pl.BlockSpec((pb, w.shape[1], planes, ds, f), lambda g: (g, 0, plane, 0, 0)) for w in ws]
        + [fixed((every, LANES))] * len(gates)
        + [pl.BlockSpec((t, pb * ds), lambda g: (0, g))] * len(before),
        [pl.BlockSpec((t, d), lambda g: (0, 0))] * parts,
        [sds((t, d), BF16)] * parts,
        2 * every * k * p * ds,
        2 * (every * k + k * p * ds) + 2 * every * d,
    )(*acts, *ws, *gates, *before)


def unturn_kernel(dq_ref, dk_ref, raw_ref, s_ref, g_ref, cos_ref, sin_ref, u_ref, in_ref, gg_ref):
    h = pl.program_id(0)
    reps = raw_ref.shape[1] // cos_ref.shape[0]
    cosine = jnp.concatenate([cos_ref[...]] * reps, 0)
    sine = jnp.concatenate([sin_ref[...]] * reps, 0)
    for i, grad in enumerate((dq_ref[...], dk_ref[...])):
        u = turn(grad, cosine, -sine)
        hat = raw_ref[i] * s_ref[i]
        product = u * hat
        u_ref[i] = u
        gg_ref[i] = jnp.sum(product, 0, keepdims=True)
        row = jnp.broadcast_to(jnp.sum(product * g_ref[i], -1, keepdims=True), in_ref.shape[1:])

        @pl.when(h == 0)
        def _():
            in_ref[i] = row

        @pl.when(h != 0)
        def _():
            in_ref[i] += row


def unturn(dq, dk, raw, scales, gains, cosine, sine):
    _, t, n = raw.shape
    h = HEAD_DIM
    length = cosine.shape[0]
    column = pl.BlockSpec((t, h), lambda i: (0, i))
    pair = pl.BlockSpec((2, t, h), lambda i: (0, 0, i))
    return call(
        unturn_kernel,
        "unturn",
        (n // h,),
        [
            column,
            column,
            pair,
            fixed((2, t, 1)),
            pl.BlockSpec((2, 1, h), lambda i: (0, 0, i)),
            fixed((length, h)),
            fixed((length, h)),
        ],
        [
            pair,
            pl.BlockSpec((2, t, 128), lambda i: (0, 0, 0)),
            pl.BlockSpec((2, 1, h), lambda i: (0, 0, i)),
        ],
        [sds((2, t, n), F32), sds((2, t, 128), F32), sds((2, 1, n), F32)],
        30 * t * n,
        24 * t * n,
    )(dq, dk, raw, scales, gains, cosine, sine)


def raw_back_kernel(place_ref, u_ref, raw_ref, s_ref, in_ref, g_ref, dv_ref, w_ref, d_ref, *outs):
    t, n = dv_ref.shape

    @pl.when(pl.program_id(0) == 0)
    def _():
        for i in range(2):
            hat = raw_ref[i] * s_ref[i]
            d_ref[:, i * n : (i + 1) * n] = (
                s_ref[i] * (u_ref[i] * g_ref[i] - hat * in_ref[i])
            ).astype(BF16)
        d_ref[:, 2 * n :] = dv_ref[...]

    pb, _, ds, _ = w_ref.shape
    w = jnp.concatenate([w_ref[:, c].reshape(pb * ds, n) for c in range(3)], 1)
    y = nt(d_ref[...], w).astype(BF16)
    rows = outs[0].shape[0]
    for r, o in enumerate(outs):
        for q in range(len(outs)):

            @pl.when(place_ref[r] == q * rows)
            def _():
                o[...] = y[q * rows : (q + 1) * rows]


def raw_back(places, u, raw, scales, inner, gains, dv, w, pieces):
    t, n = dv.shape
    p, _, ds, _ = w.shape
    d = p * ds
    pb = max(1, 2 * TILE // ds)
    return call(
        raw_back_kernel,
        "raw_back",
        (p // pb,),
        [
            fixed((2, t, n)),
            fixed((2, t, n)),
            fixed((2, t, 1)),
            fixed((2, t, 1)),
            fixed((2, 1, n)),
            fixed((t, n)),
            pl.BlockSpec((pb, 3, ds, n), lambda g, *_: (g, 0, 0, 0)),
        ],
        [pl.BlockSpec((t, 3 * n), lambda g, *_: (0, 0))]
        + [pl.BlockSpec((t // pieces, pb * ds), lambda g, *_: (0, g))] * pieces,
        [sds((t, 3 * n), BF16)] + [sds((t // pieces, d), BF16)] * pieces,
        6 * t * d * n,
        2 * (3 * d * n + t * d) + 20 * t * n,
        prefetch=1,
    )(places, u, raw, scales, inner, gains, dv, w)


def qkv_grad_kernel(n_ref, d_ref, kept_ref, o_ref):
    pb, _, ds, n = o_ref.shape
    grads = tn(n_ref[...], d_ref[...]).astype(BF16)
    for c in range(3):
        o_ref[:, c] = grads[:, c * n : (c + 1) * n].reshape(pb, ds, n)


def qkv_grads(normed, grad, kept, p):
    t, d = normed.shape
    n = grad.shape[1] // 3
    ds = d // p
    pb = max(1, TILE // ds)
    return call(
        qkv_grad_kernel,
        "qkv_grad",
        (p // pb,),
        [
            pl.BlockSpec((t, pb * ds), lambda g: (0, g)),
            fixed((t, 3 * n)),
            pl.BlockSpec(memory_space=pl.ANY),
        ],
        pl.BlockSpec((pb, 3, ds, n), lambda g: (g, 0, 0, 0)),
        sds(kept.shape, BF16),
        6 * t * d * n,
        2 * (3 * d * n + t * d + 3 * t * n),
        aliases={2: 0},
    )(normed, grad, kept)


def swap(value, axis):
    return lax.ppermute(value, axis, [(0, 1), (1, 0)])


def spread(value):
    rows = swap(value, "row")
    return (value, swap(value, "core"), rows, swap(rows, "core"))


def across(value, k):
    size = lax.axis_size("tp")
    return lax.ppermute(value, "tp", [(i, i ^ k) for i in range(size)])


def total(pieces):
    return sum(v.astype(F32) for v in pieces)


def add(*values):
    return total(values).astype(values[0].dtype)


def cut(value, pieces):
    rows = value.shape[0] // pieces
    return [value[r * rows : (r + 1) * rows] for r in range(pieces)]


def join(*pieces):
    return jnp.concatenate(pieces, 0)


class Line:
    def __init__(self):
        self.last = None

    def __call__(self, step, *operands):
        leaves, form = jax.tree.flatten(operands)
        spots = [i for i, v in enumerate(leaves) if isinstance(v, jax.Array)]
        if self.last is not None:
            kept, self.last = lax.optimization_barrier(([leaves[i] for i in spots], self.last))
            for i, v in zip(spots, kept):
                leaves[i] = v
        result = step(*jax.tree.unflatten(form, leaves))
        self.last = jax.tree.leaves(result)
        return result

    def sums(self, own, core, pieces, first=None):
        mine, theirs = cut(own, pieces), cut(swap(core, "core"), pieces)
        last = across(self(add, mine[3], theirs[3]), 1)
        near = self(add, mine[2], theirs[2], last)
        beside, first = self(lambda a, b, c, d: (add(a, b), add(c, d)), mine[1], theirs[1], mine[0], theirs[0])
        return [first, across(beside, 1), across(near, 2)]


def in_place_kernel(place_ref, *refs, count):
    for r, piece in enumerate(refs[:count]):

        @pl.when(pl.program_id(0) == r)
        def _():
            refs[-1][...] = piece[...]


def in_place(places, pieces, kept, total_rows):
    rows, d = pieces[0].shape
    count = len(pieces)
    return call(
        functools.partial(in_place_kernel, count=count),
        "inplace",
        (count,),
        [fixed((rows, d))] * count + [pl.BlockSpec(memory_space=pl.ANY)] * len(kept),
        pl.BlockSpec((rows, d), lambda r, place: (place[r] // rows, 0)),
        sds((total_rows, d), pieces[0].dtype),
        0,
        4 * rows * count * d,
        prefetch=1,
        aliases={1 + count: 0} if kept else None,
    )(places, *pieces, *kept)


def meet(value):
    value = value + across(value, 1)
    return value + across(value, 2)


def relative(value, places, pieces):
    rows = value.shape[0] // pieces
    return [lax.dynamic_slice_in_dim(value, places[r], rows, 0) for r in range(pieces)]


def body(
    inputs,
    prefix,
    expert_ids,
    norm_gains,
    qkv_weight,
    out_weight,
    router_weight,
    gate_up_weight,
    down_weight,
    cotangent,
    *,
    chunks,
):
    sequences, length, width = inputs.shape
    t = sequences * length
    tp = lax.axis_size("tp")
    quarter = t // tp
    column = lax.axis_index("tp")
    core = lax.axis_index("core")
    ctx = lax.axis_index("row") * 2 + core
    experts = router_weight.shape[1]
    group = experts // 2
    starts = [sum(chunks[:k]) for k in range(len(chunks))]
    x = inputs.reshape(t, width)
    places = jnp.stack([column ^ r for r in range(tp)]).astype(jnp.int32) * quarter
    x_q = lax.dynamic_slice_in_dim(x, column * quarter, quarter, 0)

    line = Line()
    attn_local = jnp.concatenate([qkv_weight, out_weight[None]], 0)
    attn_w = lax.all_gather(attn_local, PLANE, axis=0, tiled=False)
    triple = jnp.concatenate([gate_up_weight, down_weight[:, None]], 1)
    ds, f = triple.shape[2:]
    grouped = triple.reshape(2, group, 3, ds, f)
    ws = []
    for begin, e in zip(starts, chunks):
        mine = lax.all_to_all(grouped[:, begin : begin + e], "core", 0, 0, tiled=True)
        ws.append(lax.all_gather(mine, FR, axis=0, tiled=False).reshape(-1, e, 3, ds, f))
    gains_low = lax.all_gather(norm_gains, PLANE, axis=1, tiled=True)
    router = lax.all_gather(router_weight, PLANE, axis=0, tiled=True)
    cots = relative(cotangent.reshape(t, width), places, tp)
    c0 = join(*cots)
    c1 = swap(c0, "core")
    attn_w, gains_low, router, c0 = lax.optimization_barrier((attn_w, gains_low, router, c0))
    p = attn_w.shape[0]

    gains = gains_low.astype(F32)
    n = attn_w.shape[3]
    router_rows = jnp.concatenate([router.T, jnp.zeros((128 - experts, width), BF16)], 0)

    own_gains = lax.dynamic_slice_in_dim(gains[2:4], column * n, n, 1)[:, None, :]
    halves = jnp.arange(0, HEAD_DIM, 2).astype(F32) / HEAD_DIM
    inverse = 1.0 / THETA**halves
    positions = ctx * length + jnp.arange(length, dtype=jnp.int32)
    angles = positions.astype(F32)[:, None] * inverse[None, :]
    cosine = jnp.concatenate([jnp.cos(angles)] * 2, 1)
    sine = jnp.concatenate([-jnp.sin(angles), jnp.sin(angles)], 1)
    offsets = jnp.stack([ctx, ctx ^ 1, ctx ^ 2, ctx ^ 3, ctx]).astype(jnp.int32) * length
    scal = jnp.concatenate([offsets, prefix.astype(jnp.int32)])
    ids_q = lax.dynamic_slice_in_dim(expert_ids.reshape(t, -1), column * quarter, quarter, 0)
    normed_one, raw, values, squares = line(qkv_project, x, gains[0:1], attn_w)
    v_blocks = spread(values)
    scales = lax.rsqrt(meet(squares[:, :, 0]) / width + EPSILON)[:, :, None]
    scales, values = lax.optimization_barrier((scales, v_blocks[2]))
    v_blocks = v_blocks[:2] + (values,) + v_blocks[3:]
    queries, keys = line(prepare, raw, scales, own_gains, cosine, sine)
    k_blocks = spread(keys)
    blocks = k_blocks + v_blocks
    heads = line(attend, scal, queries, blocks, length)
    sums = line(project_out, places, heads, attn_w, tp)
    near = line(add, sums[2], across(sums[3], 1))
    sums = [sums[0], across(sums[1], 1), across(near, 2)]
    mid, ext, probs, chosen = line(norm_two, x_q, sums, gains[1:2], router_rows, ids_q, experts)
    far = across(ext, 2)
    near = across(ext, 1)
    x0 = line(join, ext, near, far, across(far, 1))
    x1 = swap(x0, "core")

    xs, cs = [x0, x1], [c0, c1]
    blocks_in = jnp.arange(width // TILE, dtype=jnp.int32)
    hid, dgu, side, grads = [], [], [], []
    dx = []

    def up(k):
        first = (core * group + starts[k]).astype(jnp.int32)[None]
        for kept, made in zip((hid, dgu, side), line(expert_up, first, xs, cs, ws[k])):
            kept.append(made)

    def back(k, before):
        gates = side if k == len(chunks) - 1 else []
        return line(expert_down, [dgu[k]], [ws[k]], 0, 2, gates, before, 2, "expert_dx")

    def weight_grad(k):
        return line(expert_grads, xs, cs, hid[k], dgu[k], p, chunks[k])

    def to_owners(made, k, after):
        made, after = lax.optimization_barrier((made, after))
        made = made.reshape(-1, 2, chunks[k], 3, ds, f)
        return lax.optimization_barrier(lax.psum_scatter(made, FR, scatter_dimension=0, tiled=False))

    for k in range(len(chunks)):
        up(k)
        dx = back(k, dx)
        if k < len(chunks) - 1:
            made = weight_grad(k)
            grads.append(to_owners(made, k, ()))
    d_normed = line.sums(*dx, tp)
    moe = line(expert_down, hid, ws, 2, 1, [], [], 2, "expert_out")

    d_mid, d_mid_low, gain_two, grad_router = line(
        norm_two_back, d_normed, mid, ext, probs, chosen, cots[0], gains[1:2], router_rows
    )
    far = across(d_mid_low, 2)
    near = across(d_mid_low, 1)
    late = weight_grad(len(chunks) - 1)
    d_mid_low = line(join, d_mid_low, near, far, across(far, 1))
    own, beside = cut(moe[0], tp), cut(swap(moe[1], "core"), tp)
    last = across(line(add, own[3], beside[3]), 1)

    d_heads = line(heads_grad, places, d_mid_low, attn_w, tp)
    grads.append(to_owners(late, len(chunks) - 1, d_heads))
    dq, b0, b1, b2, b3 = line(attend_back, scal, queries, blocks, d_heads, length)
    r1 = swap(b1, "core")
    r3 = swap(b3, "core")
    near = line(add, own[2], beside[2], last)
    next_one = line(add, own[1], beside[1])
    moe = [across(next_one, 1), across(near, 2)]
    r2 = swap(line(add, b2, r3), "row")
    grad_attn = line(out_weight_grad, places, d_mid_low, heads, p, tp)
    out = line(lambda *v: total(v).astype(BF16), mid, own[0], beside[0], *moe)
    out_far = across(out, 2)
    out_near = across(out, 1)
    d_kv = line(lambda *v: total(v), b0, r1, r2)
    out_far, d_kv = lax.optimization_barrier((out_far, d_kv))
    out_both = across(out_far, 1)
    u, inner, gain_qk = line(unturn, dq, d_kv[0], raw, scales, own_gains, cosine, sine)
    outputs = line(in_place, places, [out, out_near, out_far, out_both], [], t).reshape(inputs.shape)

    def parted(k):
        own, other = line(
            lambda v: [lax.dynamic_index_in_dim(v, c, 0, keepdims=False) for c in (core, core ^ 1)], grads[k]
        )
        return own, swap(other, "core")

    def settled(k, pair, kept):
        steps = jnp.arange(chunks[k] // 2, dtype=jnp.int32)
        spots = jnp.concatenate([(c * group + starts[k]) // 2 + steps for c in (core, core ^ 1)])
        return line(settle, spots.astype(jnp.int32), pair, kept, experts)

    inner = (meet(inner[:, :, 0]) / width)[:, :, None]
    d_raw, *d_one = line(
        raw_back, places, u, raw, scales, inner, own_gains, d_kv[1].astype(BF16), attn_w, tp
    )
    last = across(d_one[3], 1)
    grad_attn = line(qkv_grads, normed_one, d_raw, grad_attn, p)
    grad_attn = lax.psum_scatter(grad_attn, PLANE, scatter_dimension=0, tiled=False)
    pairs = [parted(0)]
    near = line(add, d_one[2], last)
    d_one = [d_one[0], across(d_one[1], 1), across(near, 2)]
    grad_in, gain_one = line(norm_one_back, d_one, x_q, d_mid, gains[0:1])
    far = across(grad_in, 2)
    near = across(grad_in, 1)
    placed = lax.dynamic_update_slice_in_dim(
        jnp.zeros((2, width), F32), gain_qk[:, 0, :], column * n, 1
    )

    small = line(lambda *v: jnp.concatenate(v, 0), grad_router[:experts], gain_one, gain_two, placed)
    rows = small.shape[0]
    small = small.reshape(rows, p, ds).transpose(1, 0, 2)
    small = jnp.sum(lax.all_to_all(small, PLANE, 0, 0, tiled=True), 0)
    other = across(small, 1)
    both = across(far, 1)
    kept = settled(0, pairs[0], [])
    placed_in = line(in_place, places[:2], [grad_in, near], [], t)
    pairs.append(parted(1))
    owned_gate_up, owned_down = settled(1, pairs[1], kept)
    small = line(lambda a, b: a + b, small, other)
    other = across(small, 2)
    grad_inputs = line(in_place, places[2:], [far, both], [placed_in], t).reshape(inputs.shape)
    grad_attn, grad_inputs = lax.optimization_barrier((grad_attn, grad_inputs))
    small = line(lambda a, b: a + b, small, other)
    owned_gains = small[experts:]
    owned_router = small[:experts].T
    return (
        outputs,
        grad_inputs,
        owned_gains,
        grad_attn[:3].astype(F32),
        grad_attn[3].astype(F32),
        owned_router,
        owned_gate_up,
        owned_down,
    )


def solution(mesh):
    fsdp, ctx, tp = (mesh.shape[a] for a in ("fsdp", "ctx", "tp"))
    fine = Mesh(mesh.devices.reshape(fsdp, ctx // 2, 2, tp), EVERY)
    tokens = P("fsdp", ("row", "core"), None)
    weights = (
        P(None, PLANE),
        P(None, PLANE, "tp"),
        P(PLANE, "tp"),
        P(PLANE, None),
        P(None, None, PLANE, "tp"),
        P(None, PLANE, "tp"),
    )
    return jax.shard_map(
        functools.partial(body, chunks=(6, 2)),
        mesh=fine,
        in_specs=(tokens, P("fsdp"), tokens) + weights + (tokens,),
        out_specs=(tokens, tokens) + weights,
        check_vma=False,
    )
```
